32 devices in a mesh: dp: 8 (over z, x), tensor: 4 (over y, core).
Axes of the slice: x: 2, y: 2, z: 4, core: 2. Of those that a mesh axis runs over, the one named last changes fastest.
Arguments:
- tokens: bfloat16 [16384, 768], P(('dp', 'tensor')), may hold values from -6 to 6
- input_gain: float32 [768], replicated, may hold values from 0.5 to 1.5
- input_bias: float32 [768], replicated, may hold values from -1.5 to 1.5
- post_gain: float32 [768], replicated, may hold values from 0.5 to 1.5
- post_bias: float32 [768], replicated, may hold values from -1.5 to 1.5
- query_key_value: bfloat16 [3, 768, 768], P(None, None, 'tensor'), may hold values from -0.21875 to 0.21875
- query_key_value_bias: float32 [3, 768], P(None, 'tensor'), may hold values from -1.5 to 1.5
- dense_weight: bfloat16 [768, 768], P('tensor'), may hold values from -3 to 3
- dense_bias: float32 [768], replicated, may hold values from -1.5 to 1.5
- expand_weight: bfloat16 [768, 3072], P(None, 'tensor'), may hold values from -0.21875 to 0.21875
- expand_bias: float32 [3072], P('tensor'), may hold values from -2.5 to 2.5
- contract_weight: bfloat16 [3072, 768], P('tensor'), may hold values from -0.109375 to 0.109375
- contract_bias: float32 [768], replicated, may hold values from -1.5 to 1.5
- lengths: int32 [8], P('dp'), may hold values from 102 to 2048, as said below
- cotangent: bfloat16 [16384, 768], P(('dp', 'tensor')), may hold values from -6 to 6
Outputs:
- mixed: bfloat16 [16384, 768], P(('dp', 'tensor'))
- grad_tokens: float32 [16384, 768], P(('dp', 'tensor'))
- grad_input_gain: float32 [768], replicated
- grad_input_bias: float32 [768], replicated
- grad_post_gain: float32 [768], replicated
- grad_post_bias: float32 [768], replicated
- grad_query_key_value: float32 [3, 768, 768], P(None, None, 'tensor')
- grad_query_key_value_bias: float32 [3, 768], P(None, 'tensor')
- grad_dense_weight: float32 [768, 768], P('tensor')
- grad_dense_bias: float32 [768], replicated
- grad_expand_weight: float32 [768, 3072], P(None, 'tensor')
- grad_expand_bias: float32 [3072], P('tensor')
- grad_contract_weight: float32 [3072, 768], P('tensor')
- grad_contract_bias: float32 [768], replicated
The draws below stay inside these ranges and needn't reach their ends.
Inputs may be any that keep to these rules, and one draw needn't show every extreme that they name: lengths[s] is the number of real tokens of sentence s, the rest of its 2048 slots being padding; in every draw some sentence fills all 2048 slots.
All inputs are finite; a program needn't handle non-finite values.
Results may differ from the reference program's by a relative error of at most 0.012.
Values may be sent and summed in bfloat16 or wider, within the bound.
A program may use at most 128 MiB of HBM per device.

```python
import jax
import jax.numpy as jnp
from jax import lax

D = 768
H = 12
HD = 64
ROT = 16
FF = 3072
LEN = 2048
SHORT = 102
SEQS = 8
TOKENS = 16384


def draw_lengths(key, part):
    first_key, second_key, third_key, pick_key = jax.random.split(key, 4)
    span = LEN - SHORT + 1
    first = jax.random.randint(first_key, (SEQS,), 0, span)
    second = jax.random.randint(second_key, (SEQS,), 0, span)
    third = jax.random.randint(third_key, (SEQS,), 0, span)
    shorter = jnp.minimum(jnp.minimum(first, second), third)
    chosen = jax.random.randint(pick_key, (), 0, SEQS)
    filled = jnp.arange(SEQS) == chosen
    return jnp.where(filled, LEN, LEN - shorter).astype(jnp.int32)


def level_of(key, dims, cuts, least, top_value):
    def one(dim, shards_of):
        steps = jax.random.uniform(jax.random.fold_in(jax.random.fold_in(key, 6), dim), (shards_of,), jnp.float32, least / len(cuts), top_value / len(cuts))
        return jnp.repeat(jnp.exp(steps), dims[dim] // shards_of).reshape((-1,) + (1,) * (len(dims) - dim - 1))

    level = one(*cuts[0])
    for cut in cuts[1:]:
        level = level * one(*cut)
    return level


def bell_draw(own_key, shape, width, reach, cuts=(), kind=jnp.bfloat16):
    values = width * jax.random.normal(own_key, shape, jnp.float32)
    if cuts:
        values = values * level_of(own_key, shape, cuts, -0.22, 0.18)
    return jnp.clip(values, -reach, reach).astype(kind)


def setup_inputs(seed: int = 0) -> dict:
    splits = jax.random.split(jax.random.key(seed), 16)
    tokens = bell_draw(splits[0], (TOKENS, D), 1.0, 6.0, ((0, 32),))
    input_gain = jnp.clip(1.0 + 0.1 * jax.random.normal(splits[1], (D,), jnp.float32), 0.5, 1.5)
    input_bias = bell_draw(splits[2], (D,), 0.3, 1.5, (), jnp.float32)
    post_gain = jnp.clip(1.0 + 0.1 * jax.random.normal(splits[3], (D,), jnp.float32), 0.5, 1.5)
    post_bias = bell_draw(splits[4], (D,), 0.3, 1.5, (), jnp.float32)
    query_key_value = bell_draw(splits[5], (3, D, D), D ** -0.5, 0.21875, ((2, 4),))
    query_key_value_bias = bell_draw(splits[6], (3, D), 0.3, 1.5, ((1, 4),), jnp.float32)
    dense_weight = bell_draw(splits[7], (D, D), (max(D // 192, 1)) ** -0.5, 3.0, ((0, 4),))
    dense_bias = bell_draw(splits[8], (D,), 0.3, 1.5, (), jnp.float32)
    expand_weight = bell_draw(splits[9], (D, FF), D ** -0.5, 0.21875, ((1, 4),))
    expand_bias = bell_draw(splits[10], (FF,), 0.5, 2.5, ((0, 4),), jnp.float32)
    contract_weight = bell_draw(splits[11], (FF, D), FF ** -0.5, 0.109375, ((0, 4),))
    contract_bias = bell_draw(splits[12], (D,), 0.3, 1.5, (), jnp.float32)
    lengths = draw_lengths(jax.random.fold_in(splits[15], 71), 0)
    cotangent = bell_draw(splits[14], (TOKENS, D), 1.0, 6.0, ((0, 32),))
    return dict(tokens=tokens, input_gain=input_gain, input_bias=input_bias, post_gain=post_gain, post_bias=post_bias, query_key_value=query_key_value, query_key_value_bias=query_key_value_bias, dense_weight=dense_weight, dense_bias=dense_bias, expand_weight=expand_weight, expand_bias=expand_bias, contract_weight=contract_weight, contract_bias=contract_bias, lengths=lengths, cotangent=cotangent)


@jax.custom_vjp
def low(v):
    return lax.optimization_barrier(v.astype(jnp.bfloat16)).astype(jnp.float32)

@jax.custom_vjp
def low_back(v):
    return v

def low_keep(v):
    return (low(v), None)

def low_pass(kept, grad):
    return (grad,)

def back_keep(v):
    return (v, None)

def back_low(kept, grad):
    return (low(grad),)
low.defvjp(low_keep, low_pass)
low_back.defvjp(back_keep, back_low)
EPS = 1e-05
HIGH = lax.Precision.HIGHEST
MASKED = -1e+30

def layer_norm(values, gain, bias):
    centred = values - lax.optimization_barrier(jnp.mean(values, -1, keepdims=True))
    inverse = lax.rsqrt(lax.optimization_barrier(jnp.mean(centred * centred, -1, keepdims=True)) + EPS)
    return centred * inverse * gain + bias

def angles(count):
    half = ROT // 2
    freqs = 10000.0 ** (-2.0 * jnp.arange(half, dtype=jnp.float32) / ROT)
    place = (jnp.arange(count) % LEN).astype(jnp.float32)
    angle = place[:, None] * freqs[None, :]
    return (jnp.cos(angle), jnp.sin(angle))

def rotate(values, cosine, sine):
    half = ROT // 2
    first = values[..., :half]
    second = values[..., half:ROT]
    cosine = cosine[:, None, :]
    sine = sine[:, None, :]
    return jnp.concatenate([first * cosine - second * sine, second * cosine + first * sine, values[..., ROT:]], -1)

def sentence(rows, length, params):
    in_gain, in_bias, out_gain, out_bias, proj_weight, proj_bias, dense_w, dense_b, expand_w, expand_b, contract_w, contract_b = params
    normed_one = low(layer_norm(rows, in_gain, in_bias))
    normed_two = low(layer_norm(rows, out_gain, out_bias))
    projected = low_back(jnp.einsum('td,cdh->cth', normed_one, proj_weight, precision=HIGH) + proj_bias[:, None, :])
    cosine, sine = angles(LEN)
    queries = low(rotate(projected[0].reshape(LEN, H, HD), cosine, sine))
    key_rows = low(rotate(projected[1].reshape(LEN, H, HD), cosine, sine))
    value_rows = low(projected[2].reshape(LEN, H, HD))
    block = min(512, LEN)
    key_place = jnp.arange(LEN)

    def attend(start):
        query_block = lax.dynamic_slice_in_dim(queries, start, block, 0)
        scores = low_back(jnp.einsum('qhe,khe->hqk', query_block, key_rows, precision=HIGH) * HD ** (-0.5))
        query_place = start + jnp.arange(block)
        allowed = (key_place[None, :] <= query_place[:, None]) & (key_place[None, :] < length)
        scores = jnp.where(allowed[None], scores, MASKED)
        highest = lax.optimization_barrier(jnp.max(scores, -1, keepdims=True))
        weights = jnp.exp(scores - highest)
        probs = low(weights / lax.optimization_barrier(jnp.sum(weights, -1, keepdims=True)))
        return jnp.einsum('hqk,khe->qhe', probs, value_rows, precision=HIGH)
    starts = (jnp.arange(LEN // block) * block).astype(jnp.int32)
    outputs = lax.map(jax.checkpoint(attend), starts)
    context = low(low_back(outputs.reshape(LEN, D)))
    pre_act = low_back(jnp.dot(normed_two, expand_w, precision=HIGH) + expand_b)
    activation = low(jax.nn.gelu(pre_act, approximate=False))
    return rows + jnp.dot(context, dense_w, precision=HIGH) + jnp.dot(activation, contract_w, precision=HIGH) + dense_b + contract_b

def reference(tokens, input_gain, input_bias, post_gain, post_bias, query_key_value, query_key_value_bias, dense_weight, dense_bias, expand_weight, expand_bias, contract_weight, contract_bias, lengths, cotangent):
    params = (input_gain, input_bias, post_gain, post_bias, query_key_value.astype(jnp.float32), query_key_value_bias, dense_weight.astype(jnp.float32), dense_bias, expand_weight.astype(jnp.float32), expand_bias, contract_weight.astype(jnp.float32), contract_bias)
    rows = tokens.astype(jnp.float32).reshape(SEQS, LEN, D)
    grads = cotangent.astype(jnp.float32).reshape(SEQS, LEN, D)

    def step(totals, item):
        sentence_rows, sentence_grads, length = item

        def forward(values, weights):
            return sentence(values, length, weights)
        output, pullback = jax.vjp(forward, sentence_rows, params)
        grad_rows, grad_params = pullback(sentence_grads)
        return (jax.tree.map(jnp.add, totals, grad_params), (output.astype(jnp.bfloat16), grad_rows))
    zeros = jax.tree.map(jnp.zeros_like, params)
    totals, (outputs, grad_rows) = lax.scan(step, zeros, (rows, grads, lengths))
    return (outputs.reshape(TOKENS, D), grad_rows.reshape(TOKENS, D), totals[0], totals[1], totals[2], totals[3], totals[4], totals[5], totals[6], totals[7], totals[8], totals[9], totals[10], totals[11])
```

```python
import functools

import jax
import jax.numpy as jnp
import numpy as np
from jax import lax
from jax.experimental import pallas as pl
from jax.experimental.pallas import tpu as pltpu
from jax.sharding import PartitionSpec as P

HD = 64
ROT = 16
LEN = 2048
EPS = 1e-05
MASKED = -1e30
F32 = jnp.float32
BF16 = jnp.bfloat16


def dot(a, b, ca, cb):
    return lax.dot_general(a, b, (((ca,), (cb,)), ((), ())), preferred_element_type=F32)


def angle_rows(count):
    half = ROT // 2
    freqs = np.float32(10000.0) ** (
        np.float32(-2.0) * np.arange(half, dtype=np.float32) / np.float32(ROT)
    )
    place = (np.arange(count) % LEN).astype(np.float32)
    angle = (freqs[:, None] * place[None, :]).astype(np.float32)
    return np.cos(angle), np.sin(angle)


def unit_rows(rows):
    values = rows.astype(F32)
    centred = values - jnp.mean(values, -1, keepdims=True)
    inverse = lax.rsqrt(jnp.mean(centred * centred, -1, keepdims=True) + EPS)
    return centred * inverse, inverse


def core(
    blk,
    x_ref,
    g_ref,
    len_ref,
    gain1,
    bias1,
    gain2,
    bias2,
    wt,
    qkv_b,
    wd,
    we,
    exp_b,
    wc,
    cos_t,
    sin_t,
    mix_o,
    s_o,
    dwt,
    dwd,
    dwe,
    dwc,
    vec_o,
    dbe,
    dbq,
    n1_s,
    qa,
    kt,
    kr,
    va,
    vr,
    dot_s,
    sc,
    pt,
    dkt,
    dvt,
    ctx_s,
    gp,
    dq_s,
):
    total, width = x_ref.shape
    local = wd.shape[0]
    heads = local // HD
    count = total // blk
    per = LEN // blk
    root = HD**-0.5

    for ref in (dwt, dwd, dwe, dwc, vec_o, dbe, dbq, dkt, dvt):
        ref[...] = jnp.zeros_like(ref)
    one_row = (lax.broadcasted_iota(jnp.int32, (heads, HD, total), 1) == 0).astype(F32)
    qa[:, HD:, :] = one_row.astype(BF16)
    va[:, HD:, :] = one_row[:, : va.shape[1] - HD, :].astype(BF16)

    def dense(b, _):
        rows = pl.ds(pl.multiple_of(b * blk, blk), blk)
        unit, _inv = unit_rows(x_ref[rows, :])
        n1 = (unit * gain1[...] + bias1[...]).astype(BF16)
        n2 = (unit * gain2[...] + bias2[...]).astype(BF16)
        n1_s[rows, :] = n1
        g = g_ref[rows, :]
        proj = dot(wt[...], n1, 1, 1) + qkv_b[...]
        cosine = cos_t[:, rows]
        sine = sin_t[:, rows]

        def turn(block):
            a = block[: ROT // 2]
            c = block[ROT // 2 : ROT]
            return jnp.concatenate(
                [a * cosine - c * sine, c * cosine + a * sine, block[ROT:]], 0
            )

        place = lax.broadcasted_iota(jnp.int32, (HD, blk), 1) + lax.rem(b, per) * blk
        first = lax.broadcasted_iota(jnp.int32, (HD, blk), 0) == 0
        extra = jnp.where(first & (place >= len_ref[b // per]), MASKED, 0.0)
        for h in range(heads):
            lo = h * HD
            q = turn(proj[lo : lo + HD])
            k = turn(proj[local + lo : local + lo + HD])
            v = proj[2 * local + lo : 2 * local + lo + HD]
            qa[h, :HD, rows] = (q * root).astype(BF16)
            kt[h, :, rows] = k.astype(BF16)
            kr[h, rows, :] = jnp.transpose(jnp.concatenate([k, extra], 0)).astype(BF16)
            va[h, :HD, rows] = v.astype(BF16)
            vr[h, rows, :] = jnp.transpose(v).astype(BF16)
        grad_ctx = dot(wd[...], g, 1, 1).astype(BF16)
        for h in range(heads):
            dot_s[h, :, rows] = grad_ctx[h * HD : (h + 1) * HD]
        pre = dot(n2, we[...], 1, 0) + exp_b[...]
        big = 0.5 * (1.0 + lax.erf(pre * np.float32(0.5**0.5)))
        act = (pre * big).astype(BF16)
        slope = big + pre * (jnp.exp(-0.5 * pre * pre) * np.float32((2 * np.pi) ** -0.5))
        mix_o[rows, :] = dot(act, wc[...], 1, 0).astype(BF16)
        dwc[...] += dot(act, g, 0, 0)
        grad_pre_f = dot(g, wc[...], 1, 1) * slope
        grad_pre = grad_pre_f.astype(BF16)
        dbe[...] += jnp.sum(grad_pre.astype(F32), 0, keepdims=True)
        dwe[...] += dot(n2, grad_pre, 0, 0)
        part = dot(grad_pre, we[...], 1, 1)
        s_o[rows, :] = (part * gain2[...]).astype(BF16)
        vec_o[2:3, :] += jnp.sum(part * unit, 0, keepdims=True)
        vec_o[3:4, :] += jnp.sum(part, 0, keepdims=True)
        return 0

    lax.fori_loop(0, count, dense, 0)

    key_i = lax.broadcasted_iota(jnp.int32, (blk, blk), 0)
    query_i = lax.broadcasted_iota(jnp.int32, (blk, blk), 1)

    def attend(step, _):
        i = count - 1 - step
        base = (i // per) * per
        mine = pl.ds(pl.multiple_of(i * blk, blk), blk)

        def head(h, _):
            q_aug = qa[h, :, mine]

            def score(j, high):
                cols = pl.ds(pl.multiple_of(j * blk, blk), blk)
                s = dot(kr[h, cols, :], q_aug, 1, 0)
                sc[pl.ds(pl.multiple_of((j - base) * blk, blk), blk), :] = s
                return jnp.maximum(high, jnp.max(s.reshape(blk // 8, 8, blk), 0))

            high = lax.fori_loop(base, i, score, jnp.full((8, blk), MASKED, F32))
            s = dot(kr[h, mine, :], q_aug, 1, 0)
            s = jnp.where(key_i <= query_i, s, MASKED)
            sc[pl.ds(pl.multiple_of((i - base) * blk, blk), blk), :] = s
            high = jnp.maximum(high, jnp.max(s.reshape(blk // 8, 8, blk), 0))
            high = jnp.max(high, 0, keepdims=True)

            def weigh(j, out):
                cols = pl.ds(pl.multiple_of(j * blk, blk), blk)
                here = pl.ds(pl.multiple_of((j - base) * blk, blk), blk)
                p = jnp.exp(sc[here, :] - high).astype(BF16)
                pt[here, :] = p
                return out + dot(va[h, :, cols], p, 1, 0)

            out = lax.fori_loop(base, i + 1, weigh, jnp.zeros((va.shape[1], blk), F32))
            scale = 1.0 / out[HD : HD + 1]
            ctx = out[:HD] * scale
            ctx_s[h] = ctx.astype(BF16)
            go = (dot_s[h, :, mine].astype(F32) * scale).astype(BF16)
            inner = jnp.sum(ctx * go.astype(F32), 0, keepdims=True)
            q = q_aug[:HD]

            def back(j, dq):
                cols = pl.ds(pl.multiple_of(j * blk, blk), blk)
                here = pl.ds(pl.multiple_of((j - base) * blk, blk), blk)
                p = pt[here, :]
                dvt[h, :, cols] += dot(go, p, 1, 1)
                dp = dot(vr[h, cols, :], go, 1, 0)
                ds = (p.astype(F32) * (dp - inner)).astype(BF16)
                dkt[h, :, cols] += dot(q, ds, 1, 1)
                return dq + dot(kt[h, :, cols], ds, 1, 0)

            dq_s[h] = lax.fori_loop(base, i + 1, back, jnp.zeros((HD, blk), F32))
            return 0

        lax.fori_loop(0, heads, head, 0)
        cosine = cos_t[:, mine]
        sine = sin_t[:, mine]

        def unturn(block):
            a = block[: ROT // 2]
            c = block[ROT // 2 : ROT]
            return jnp.concatenate(
                [a * cosine + c * sine, c * cosine - a * sine, block[ROT:]], 0
            )

        for h in range(heads):
            lo = h * HD
            gp[lo : lo + HD, :] = unturn(dq_s[h] * root).astype(BF16)
            gp[local + lo : local + lo + HD, :] = unturn(dkt[h, :, mine]).astype(BF16)
            gp[2 * local + lo : 2 * local + lo + HD, :] = dvt[h, :, mine].astype(BF16)
        grad_proj = gp[...]
        ctx_all = ctx_s[...].reshape(local, blk)
        mix = dot(ctx_all, wd[...], 0, 0) + mix_o[mine, :].astype(F32)
        mix_o[mine, :] = mix.astype(BF16)
        dwd[...] += dot(ctx_all, g_ref[mine, :], 1, 0)
        dwt[...] += dot(grad_proj, n1_s[mine, :], 1, 0)
        part = dot(grad_proj, wt[...], 0, 0) * gain1[...] + s_o[mine, :].astype(F32)
        s_o[mine, :] = part.astype(BF16)
        dbq[...] += jnp.sum(grad_proj.astype(F32), 1, keepdims=True)
        return 0

    lax.fori_loop(0, count, attend, 0)
    w32 = wt[...].astype(F32)
    grad_bias = jnp.sum(w32 * dbq[...], 0, keepdims=True)
    vec_o[1:2, :] = grad_bias
    vec_o[0:1, :] = (jnp.sum(w32 * dwt[...], 0, keepdims=True) - bias1[...] * grad_bias) / gain1[
        ...
    ]


def shards(
    tokens,
    input_gain,
    input_bias,
    post_gain,
    post_bias,
    query_key_value,
    query_key_value_bias,
    dense_weight,
    dense_bias,
    expand_weight,
    expand_bias,
    contract_weight,
    contract_bias,
    lengths,
    cotangent,
):
    width = tokens.shape[1]
    local = query_key_value.shape[2]
    heads = local // HD
    hidden = expand_weight.shape[1]
    blk = tokens.shape[0]
    x = lax.all_gather(tokens, "tensor", axis=0, tiled=True)
    g = lax.all_gather(cotangent, "tensor", axis=0, tiled=True)
    total = x.shape[0]
    wt = jnp.transpose(query_key_value, (0, 2, 1)).reshape(3 * local, width)
    cosine, sine = angle_rows(total)
    vmem = pl.BlockSpec(memory_space=pltpu.VMEM)
    smem = pl.BlockSpec(memory_space=pltpu.SMEM)
    outs = pl.pallas_call(
        functools.partial(core, blk),
        name="core",
        out_shape=(
            jax.ShapeDtypeStruct((total, width), BF16),
            jax.ShapeDtypeStruct((total, width), BF16),
            jax.ShapeDtypeStruct((3 * local, width), F32),
            jax.ShapeDtypeStruct((local, width), F32),
            jax.ShapeDtypeStruct((width, hidden), F32),
            jax.ShapeDtypeStruct((hidden, width), F32),
            jax.ShapeDtypeStruct((8, width), F32),
            jax.ShapeDtypeStruct((1, hidden), F32),
            jax.ShapeDtypeStruct((3 * local, 1), F32),
        ),
        in_specs=[vmem, vmem, smem] + [vmem] * 12,
        out_specs=[vmem] * 9,
        scratch_shapes=[
            pltpu.VMEM((total, width), BF16),
            pltpu.VMEM((heads, 2 * HD, total), BF16),
            pltpu.VMEM((heads, HD, total), BF16),
            pltpu.VMEM((heads, total, 2 * HD), BF16),
            pltpu.VMEM((heads, HD + 16, total), BF16),
            pltpu.VMEM((heads, total, HD), BF16),
            pltpu.VMEM((heads, HD, total), BF16),
            pltpu.VMEM((LEN, blk), F32),
            pltpu.VMEM((LEN, blk), BF16),
            pltpu.VMEM((heads, HD, total), F32),
            pltpu.VMEM((heads, HD, total), F32),
            pltpu.VMEM((heads, HD, blk), BF16),
            pltpu.VMEM((3 * local, blk), BF16),
            pltpu.VMEM((heads, HD, blk), F32),
        ],
        compiler_params=pltpu.CompilerParams(vmem_limit_bytes=62 * 2**20),
    )(
        x,
        g,
        lengths,
        input_gain[None],
        input_bias[None],
        post_gain[None],
        post_bias[None],
        wt,
        query_key_value_bias.reshape(3 * local, 1),
        dense_weight,
        expand_weight,
        expand_bias[None],
        contract_weight,
        cosine,
        sine,
    )
    mix_p, s_p, dwt, dwd, dwe, dwc, vec, dbe, dbq = outs
    mix = lax.psum_scatter(mix_p, "tensor", scatter_dimension=0, tiled=True)
    grad_s = lax.psum_scatter(s_p, "tensor", scatter_dimension=0, tiled=True).astype(F32)
    mixed = (
        tokens.astype(F32) + mix.astype(F32) + dense_bias + contract_bias
    ).astype(BF16)
    unit, inverse = unit_rows(tokens)
    grad_tokens = cotangent.astype(F32) + inverse * (
        grad_s
        - jnp.mean(grad_s, -1, keepdims=True)
        - unit * jnp.mean(grad_s * unit, -1, keepdims=True)
    )
    vec = vec.at[4].set(jnp.sum(cotangent.astype(F32), 0))
    vec = lax.psum(vec, ("dp", "tensor"))
    small = lax.psum((dbe, dbq), "dp")
    grads = lax.psum(
        (dwt.astype(BF16), dwd.astype(BF16), dwe.astype(BF16), dwc.astype(BF16)), "dp"
    )
    grad_qkv = jnp.transpose(grads[0].astype(F32).reshape(3, local, width), (0, 2, 1))
    return (
        mixed,
        grad_tokens,
        vec[0],
        vec[1],
        vec[2],
        vec[3],
        grad_qkv,
        small[1].reshape(3, local),
        grads[1].astype(F32),
        vec[4],
        grads[2].astype(F32),
        small[0][0],
        grads[3].astype(F32),
        vec[4],
    )


def solution(mesh):
    rows = P(("dp", "tensor"), None)
    weights = (
        P(None, None, "tensor"),
        P(None, "tensor"),
        P("tensor", None),
        P(),
        P(None, "tensor"),
        P("tensor"),
        P("tensor", None),
        P(),
    )
    return jax.shard_map(
        shards,
        mesh=mesh,
        in_specs=(rows, P(), P(), P(), P()) + weights + (P("dp"), rows),
        out_specs=(rows, rows, P(), P(), P(), P()) + weights,
        check_vma=False,
    )
```

```python
import functools

import jax
import jax.numpy as jnp
import numpy as np
from jax import lax
from jax.experimental import pallas as pl
from jax.experimental.pallas import tpu as pltpu
from jax.sharding import PartitionSpec as P

HD = 64
ROT = 16
LEN = 2048
EPS = 1e-05
MASKED = -1e30
F32 = jnp.float32
BF16 = jnp.bfloat16


def dot(a, b, ca, cb):
    return lax.dot_general(a, b, (((ca,), (cb,)), ((), ())), preferred_element_type=F32)


def angle_rows(count):
    half = ROT // 2
    freqs = np.float32(10000.0) ** (
        np.float32(-2.0) * np.arange(half, dtype=np.float32) / np.float32(ROT)
    )
    place = (np.arange(count) % LEN).astype(np.float32)
    angle = (freqs[:, None] * place[None, :]).astype(np.float32)
    return np.cos(angle), np.sin(angle)


def unit_rows(rows):
    values = rows.astype(F32)
    centred = values - jnp.mean(values, -1, keepdims=True)
    inverse = lax.rsqrt(jnp.mean(centred * centred, -1, keepdims=True) + EPS)
    return centred * inverse, inverse

MESH = pl.DeviceIdType.MESH
PARTS = 3


def flip(value, bits):
    bit = 1
    while bit <= bits:
        if (bits // bit) % 2:
            value = value + bit * (1 - 2 * ((value // bit) % 2))
        bit *= 2
    return value


def core(
    n,
    tok,
    cot,
    len_ref,
    par,
    qkv,
    qkv_b,
    wd,
    we,
    wc,
    cos_t,
    sin_t,
    mixed_o,
    gtok_o,
    res_o,
    vec_o,
    x_s,
    g_s,
    n1_s,
    s_s,
    wt,
    qb_s,
    acc,
    res,
    hold,
    qa,
    kt,
    kr,
    va,
    vr,
    dot_s,
    sc,
    pt,
    dkt,
    dvt,
    ctx_s,
    gp,
    dq_s,
    vec,
    vec_in,
    sx,
    rx,
    sz,
    rz,
    ag_send,
    ag_recv,
    rs_send,
    rs_recv,
    x_send,
    x_recv,
    z_send,
    z_recv,
    v_send,
    v_recv,
    out_sem,
    free_sem,
):
    blk, width = tok.shape
    total = x_s.shape[0]
    local = wd.shape[0]
    heads = local // HD
    count = total // blk
    per = LEN // blk
    root = HD**-0.5
    members = n // 2
    piece = acc.shape[1] // members
    dp = lax.axis_index("dp")
    t = lax.axis_index("tensor")
    core_bit = t % 2
    chip_bit = t // 2
    sib = (dp, flip(t, 1))
    across = (dp, flip(t, 2))
    near = (flip(dp, 1), t)
    far = [(flip(dp, 2 * j), t) for j in range(1, members)]
    gain1, bias1, gain2, bias2, exp_b, out_b = (par[r : r + 1, :] for r in range(6))

    def send(src, dst, ssem, rsem, where):
        return pltpu.make_async_remote_copy(
            src_ref=src,
            dst_ref=dst,
            send_sem=ssem,
            recv_sem=rsem,
            device_id=where,
            device_id_type=MESH,
        )

    barrier = pltpu.get_barrier_semaphore()
    greeted = [sib, across, near] + far
    for other in greeted:
        pl.semaphore_signal(barrier, inc=1, device_id=other, device_id_type=MESH)
    pl.semaphore_wait(barrier, len(greeted))

    def block(b):
        return pl.ds(pl.multiple_of(b * blk, blk), blk)

    own = block(t)
    other = block(flip(t, 2))
    gather = [
        send(tok, x_s.at[own], ag_send.at[0], ag_recv.at[0], across),
        send(cot, g_s.at[own], ag_send.at[1], ag_recv.at[1], across),
        send(tok, x_s.at[own], ag_send.at[2], ag_recv.at[2], sib),
        send(cot, g_s.at[own], ag_send.at[3], ag_recv.at[3], sib),
        send(x_s.at[other], x_s.at[other], ag_send.at[4], ag_recv.at[4], sib),
        send(g_s.at[other], g_s.at[other], ag_send.at[5], ag_recv.at[5], sib),
    ]
    gather[0].start()
    gather[2].start()
    gather[3].start()

    x_s[own, :] = tok[...]
    g_s[own, :] = cot[...]
    for c in range(3):
        wt[c * local : (c + 1) * local, :] = jnp.transpose(qkv[c])
        column = jnp.transpose(jnp.broadcast_to(qkv_b[c : c + 1, :], (8, local)))
        qb_s[c * local : (c + 1) * local, :] = column[:, :1]
    for ref in (acc, vec, dkt, dvt):
        ref[...] = jnp.zeros_like(ref)
    one_row = (lax.broadcasted_iota(jnp.int32, (heads, HD, total), 1) == 0).astype(F32)
    qa[:, HD:, :] = one_row.astype(BF16)
    va[:, HD:, :] = one_row[:, : va.shape[1] - HD, :].astype(BF16)

    def forward(b, slot, before_mix):
        rows = block(b)
        unit, _ = unit_rows(x_s[rows, :])
        n1 = (unit * gain1 + bias1).astype(BF16)
        n2 = (unit * gain2 + bias2).astype(BF16)
        n1_s[rows, :] = n1
        hold[2 + slot] = n2
        proj = dot(wt[...], n1, 1, 1) + qb_s[...]
        cosine = cos_t[:, rows]
        sine = sin_t[:, rows]

        def turn(rows_in):
            a = rows_in[: ROT // 2]
            c = rows_in[ROT // 2 : ROT]
            return jnp.concatenate(
                [a * cosine - c * sine, c * cosine + a * sine, rows_in[ROT:]], 0
            )

        place = lax.broadcasted_iota(jnp.int32, (HD, blk), 1) + (b % per) * blk
        first = lax.broadcasted_iota(jnp.int32, (HD, blk), 0) == 0
        extra = jnp.where(first & (place >= len_ref[0]), MASKED, 0.0)
        for h in range(heads):
            lo = h * HD
            q = turn(proj[lo : lo + HD])
            k = turn(proj[local + lo : local + lo + HD])
            v = proj[2 * local + lo : 2 * local + lo + HD]
            qa[h, :HD, rows] = (q * root).astype(BF16)
            kt[h, :, rows] = k.astype(BF16)
            kr[h, rows, :] = jnp.transpose(jnp.concatenate([k, extra], 0)).astype(BF16)
            va[h, :HD, rows] = v.astype(BF16)
            vr[h, rows, :] = jnp.transpose(v).astype(BF16)
        pre = dot(n2, we[...], 1, 0) + exp_b
        big = 0.5 * (1.0 + lax.erf(pre * np.float32(0.5**0.5)))
        act = (pre * big).astype(BF16)
        slope = big + pre * (jnp.exp(-0.5 * pre * pre) * np.float32((2 * np.pi) ** -0.5))
        hold[slot] = act
        hold[4 + slot] = slope.astype(BF16)
        mix = dot(act, wc[...], 1, 0).astype(BF16)
        before_mix()
        x_s[rows, :] = mix

    def backward(b, slot):
        rows = block(b)
        g = g_s[rows, :]
        act = hold[slot]
        n2 = hold[2 + slot]
        grad_ctx = dot(wd[...], g, 1, 1).astype(BF16)
        for h in range(heads):
            dot_s[h, :, rows] = grad_ctx[h * HD : (h + 1) * HD]
        acc[0] += dot(act, g, 0, 0)
        grad_pre = (dot(g, wc[...], 1, 1) * hold[4 + slot].astype(F32)).astype(BF16)
        vec[5:6, :] += jnp.sum(grad_pre.astype(F32), 0, keepdims=True)
        acc[1] += dot(n2, grad_pre, 0, 0)
        part = dot(grad_pre, we[...], 1, 1)
        s_s[rows, :] = (part * gain2).astype(BF16)
        vec[2:3, :] += jnp.sum(part * n2.astype(F32), 0, keepdims=True)
        vec[3:4, :] += jnp.sum(part, 0, keepdims=True)

    def mate(k):
        low = (t + k) % 2
        high = (t // 2 + k // 2) % 2
        return low + 2 * high

    def phase(it, _):
        @pl.when(it == 1)
        def _():
            gather[2].wait_recv()
            gather[3].wait_recv()

        @pl.when(it == 2)
        def _():
            gather[0].wait_send()
            gather[1].start()
            gather[0].wait_recv()
            gather[4].start()

        @pl.when(it == 3)
        def _():
            gather[4].wait_recv()

        @pl.when(it < 4)
        def _():
            def settle():
                @pl.when(it == 2)
                def _():
                    gather[4].wait_send()

            forward(mate(it), it // 3, settle)

        @pl.when(it == 3)
        def _():
            gather[1].wait_recv()
            gather[5].start()

        @pl.when(it == 4)
        def _():
            gather[5].wait_recv()

        @pl.when(it != 2)
        def _():
            backward(mate(it - it // 3), it // 4)

        return 0

    lax.fori_loop(0, 5, phase, 0)
    for k in (1, 2, 3, 5):
        gather[k].wait_send()
    pl.semaphore_signal(free_sem.at[0], inc=1, device_id=sib, device_id_type=MESH)
    pl.semaphore_signal(free_sem.at[1], inc=1, device_id=across, device_id_type=MESH)
    vec[4:5, :] = jnp.sum(cot[...].astype(F32), 0, keepdims=True)

    near_bit = dp % 2
    seat = dp // 2
    ROWS = acc.shape[1]
    LAST = 3 * PARTS

    def lanes(k, bit):
        return pl.ds(pl.multiple_of((k % PARTS) * 256 + bit * 128, 128), 128)

    def band(member):
        return pl.ds(pl.multiple_of(member * piece, piece), piece)

    def seat_of(j):
        return flip(seat, j)

    def halves(k):
        return send(sx, rx.at[k % 2], x_send.at[0], x_recv.at[0, k % 2], near)

    def spread(k):
        return [
            send(
                sz.at[band(seat_of(j))],
                rz.at[k % 2, j - 1],
                z_send.at[0, j - 1],
                z_recv.at[0, k % 2, j - 1],
                far[j - 1],
            )
            for j in range(1, members)
        ]

    def collect(k):
        mine = res.at[k // PARTS, band(seat), lanes(k, near_bit)]
        return [
            send(mine, mine, z_send.at[1, j - 1], z_recv.at[1, k % 2, j - 1], far[j - 1])
            for j in range(1, members)
        ]

    def whole(k):
        half = res.at[k // PARTS, :, lanes(k, near_bit)]
        return send(half, half, x_send.at[1], x_recv.at[1, k % 2], near)

    def beat(b):
        def stage(lag, body):
            k = b - lag
            pl.when((k >= 0) & (k < LAST))(functools.partial(body, k))

        def last(k):
            whole(k).wait()

        def third(k):
            for copy in collect(k):
                copy.wait()
            whole(k).start()

        def second(k):
            for copy in spread(k):
                copy.wait()
            mine = acc[k // PARTS, band(seat), lanes(k, near_bit)]
            for j in range(1, members):
                mine += rz[k % 2, j - 1].astype(F32)
            res[k // PARTS, band(seat), lanes(k, near_bit)] = mine.astype(BF16)
            for copy in collect(k):
                copy.start()

        def first(k):
            halves(k).wait()
            mine = acc[k // PARTS, :, lanes(k, near_bit)] + rx[k % 2].astype(F32)
            acc[k // PARTS, :, lanes(k, near_bit)] = mine
            sz[...] = mine.astype(BF16)
            for copy in spread(k):
                copy.start()

        def zeroth(k):
            sx[...] = acc[k // PARTS, :, lanes(k, 1 - near_bit)].astype(BF16)
            halves(k).start()

        stage(4, last)
        stage(3, third)
        stage(2, second)
        stage(1, first)
        stage(0, zeroth)

    def to_sib(i):
        rows = block(i)
        slot = i // 2
        return [
            send(x_s.at[rows], hold.at[2 * slot], rs_send.at[slot, 0], rs_recv.at[slot, 0], sib),
            send(s_s.at[rows], hold.at[2 * slot + 1], rs_send.at[slot, 1], rs_recv.at[slot, 1], sib),
        ]

    def to_owner(i):
        rows = block(i)
        return [
            send(x_s.at[rows], hold.at[4], rs_send.at[2, 0], rs_recv.at[2, 0], across),
            send(s_s.at[rows], hold.at[5], rs_send.at[2, 1], rs_recv.at[2, 1], across),
        ]

    def hand_over(i):
        @pl.when(core_bit != i % 2)
        def _():
            for copy in to_sib(i):
                copy.start()

    def pass_on(i):
        @pl.when(core_bit == i % 2)
        def _():
            for copy in to_sib(i):
                copy.wait_recv()

        @pl.when((core_bit == i % 2) & (chip_bit != i // 2))
        def _():
            rows = block(i)
            slot = i // 2
            for w, ref in enumerate((x_s, s_s)):
                both = ref[rows, :].astype(F32) + hold[2 * slot + w].astype(F32)
                ref[rows, :] = both.astype(BF16)
            for copy in to_owner(i):
                copy.start()

    beat(0)
    key_i = lax.broadcasted_iota(jnp.int32, (blk, blk), 0)
    query_i = lax.broadcasted_iota(jnp.int32, (blk, blk), 1)

    def attend(step, _):
        i = count - 1 - step
        base = (i // per) * per
        mine = block(i)

        def head(h, _):
            q_aug = qa[h, :, mine]

            def score(j, high):
                s = dot(kr[h, block(j), :], q_aug, 1, 0)
                sc[block(j - base), :] = s
                return jnp.maximum(high, jnp.max(s.reshape(blk // 8, 8, blk), 0))

            high = lax.fori_loop(base, i, score, jnp.full((8, blk), MASKED, F32))
            s = dot(kr[h, mine, :], q_aug, 1, 0)
            s = jnp.where(key_i <= query_i, s, MASKED)
            sc[block(i - base), :] = s
            high = jnp.maximum(high, jnp.max(s.reshape(blk // 8, 8, blk), 0))
            high = jnp.max(high, 0, keepdims=True)

            def weigh(j, out):
                p = jnp.exp(sc[block(j - base), :] - high).astype(BF16)
                pt[block(j - base), :] = p
                return out + dot(va[h, :, block(j)], p, 1, 0)

            out = lax.fori_loop(base, i + 1, weigh, jnp.zeros((va.shape[1], blk), F32))
            scale = 1.0 / out[HD : HD + 1]
            ctx = out[:HD] * scale
            ctx_s[h] = ctx.astype(BF16)
            go = (dot_s[h, :, mine].astype(F32) * scale).astype(BF16)
            inner = jnp.sum(ctx * go.astype(F32), 0, keepdims=True)
            q = q_aug[:HD]

            def back(j, dq):
                cols = block(j)
                p = pt[block(j - base), :]
                dvt[h, :, cols] += dot(go, p, 1, 1)
                dp_t = dot(vr[h, cols, :], go, 1, 0)
                ds = (p.astype(F32) * (dp_t - inner)).astype(BF16)
                dkt[h, :, cols] += dot(q, ds, 1, 1)
                return dq + dot(kt[h, :, cols], ds, 1, 0)

            dq_s[h] = lax.fori_loop(base, i + 1, back, jnp.zeros((HD, blk), F32))

            @pl.when((h == 0) & (step > 0))
            def _():
                pass_on(i + 1)

            tick = step * heads + h
            number = (
                1 * (tick == 0).astype(jnp.int32)
                + 2 * (tick == 1).astype(jnp.int32)
                + 3 * (tick == 2).astype(jnp.int32)
                + 4 * (tick == 4).astype(jnp.int32)
                + 5 * (tick == 6).astype(jnp.int32)
            )

            @pl.when(number > 0)
            def _():
                beat(number)

            return 0

        lax.fori_loop(0, heads, head, 0)
        cosine = cos_t[:, mine]
        sine = sin_t[:, mine]

        def unturn(rows_in):
            a = rows_in[: ROT // 2]
            c = rows_in[ROT // 2 : ROT]
            return jnp.concatenate(
                [a * cosine + c * sine, c * cosine - a * sine, rows_in[ROT:]], 0
            )

        for h in range(heads):
            lo = h * HD
            gp[lo : lo + HD, :] = unturn(dq_s[h] * root).astype(BF16)
            gp[local + lo : local + lo + HD, :] = unturn(dkt[h, :, mine]).astype(BF16)
            gp[2 * local + lo : 2 * local + lo + HD, :] = dvt[h, :, mine].astype(BF16)
        grad_proj = gp[...]
        ctx_all = ctx_s[...].reshape(local, blk)
        mix = dot(ctx_all, wd[...], 0, 0) + x_s[mine, :].astype(F32)
        x_s[mine, :] = mix.astype(BF16)
        part = dot(grad_proj, wt[...], 0, 0) * gain1 + s_s[mine, :].astype(F32)
        s_s[mine, :] = part.astype(BF16)

        @pl.when(step == 0)
        def _():
            pl.semaphore_wait(free_sem.at[0], 1)
            pl.semaphore_wait(free_sem.at[1], 1)

        hand_over(i)
        acc[2, 3 * local :, :] += dot(ctx_all, g_s[mine, :], 1, 0)
        acc[2, : 3 * local, :] += dot(grad_proj, n1_s[mine, :], 1, 0)
        ones = jnp.ones((8, blk), BF16)
        vec[6:7, : 3 * local] += dot(ones, grad_proj, 1, 1)[:1]
        return 0

    lax.fori_loop(0, count, attend, 0)
    w32 = wt[...].astype(F32)
    column = jnp.transpose(jnp.broadcast_to(vec[6:7, : 3 * local], (8, 3 * local)))[:, :1]
    grad_bias = jnp.sum(w32 * column, 0, keepdims=True)
    grad_gain = jnp.sum(w32 * acc[2, : 3 * local, :], 0, keepdims=True)
    vec[1:2, :] = grad_bias
    vec[0:1, :] = (grad_gain - bias1 * grad_bias) / gain1
    vec[2:3, :] = (vec[2:3, :] - bias2 * vec[3:4, :]) / gain2

    swaps = []
    bit = 1
    while bit < n:
        swaps.append((flip(dp, bit), t))
        bit *= 2
    inside = len(swaps)
    swaps += [sib, across]

    def swap(q):
        return send(vec, vec_in.at[q], v_send.at[q], v_recv.at[q], swaps[q])

    shared = lax.broadcasted_iota(jnp.int32, vec.shape, 0) < 5

    def finish_swap(q):
        swap(q).wait()
        extra = vec_in[q]
        if q >= inside:
            extra = jnp.where(shared, extra, 0.0)
        vec[...] += extra

    beat(2 * PARTS)
    swap(0).start()
    pass_on(0)
    steps = max(LAST + 4, 2 * PARTS + len(swaps) + 1)

    def tail(b, _):
        beat(b)
        for q in range(1, len(swaps) + 1):

            @pl.when(b == 2 * PARTS + q)
            def _(q=q):
                finish_swap(q - 1)
                if q < len(swaps):
                    swap(q).start()

        return 0

    lax.fori_loop(2 * PARTS + 1, steps, tail, 0)
    out_copy = pltpu.make_async_copy(res, res_o, out_sem.at[0])
    out_copy.start()
    vec_o[...] = vec[...]

    for copy in to_owner(flip(t, 2)):
        copy.wait()
    slot = chip_bit
    mix = tok[...].astype(F32) + out_b
    s = s_s[own, :].astype(F32)
    mix += x_s[own, :].astype(F32)
    for w in (2 * slot, 4):
        mix += hold[w].astype(F32)
        s += hold[w + 1].astype(F32)
    mixed_o[...] = mix.astype(BF16)
    unit, inverse = unit_rows(tok[...])
    gtok_o[...] = cot[...].astype(F32) + inverse * (
        s - jnp.mean(s, -1, keepdims=True) - unit * jnp.mean(s * unit, -1, keepdims=True)
    )
    for i in range(count):

        @pl.when(core_bit != i % 2)
        def _(i=i):
            for copy in to_sib(i):
                copy.wait_send()

    out_copy.wait()


def shards(
    n,
    tokens,
    input_gain,
    input_bias,
    post_gain,
    post_bias,
    query_key_value,
    query_key_value_bias,
    dense_weight,
    dense_bias,
    expand_weight,
    expand_bias,
    contract_weight,
    contract_bias,
    lengths,
    cotangent,
):
    blk, width = tokens.shape
    local = query_key_value.shape[2]
    heads = local // HD
    total = 4 * blk
    members = n // 2
    swaps = n.bit_length() + 1
    cosine, sine = angle_rows(total)
    par = jnp.stack(
        [
            input_gain,
            input_bias,
            post_gain,
            post_bias,
            expand_bias,
            dense_bias + contract_bias,
        ]
    )
    vmem = pl.BlockSpec(memory_space=pltpu.VMEM)
    smem = pl.BlockSpec(memory_space=pltpu.SMEM)
    dma = pltpu.SemaphoreType.DMA
    mixed, grad_tokens, res, vec = pl.pallas_call(
        functools.partial(core, n),
        name="core",
        out_shape=(
            jax.ShapeDtypeStruct((blk, width), BF16),
            jax.ShapeDtypeStruct((blk, width), F32),
            jax.ShapeDtypeStruct((3, width, width), BF16),
            jax.ShapeDtypeStruct((8, width), F32),
        ),
        in_specs=[vmem, vmem, smem] + [vmem] * 8,
        out_specs=[vmem, vmem, pl.BlockSpec(memory_space=pl.ANY), vmem],
        scratch_shapes=[
            pltpu.VMEM((total, width), BF16),
            pltpu.VMEM((total, width), BF16),
            pltpu.VMEM((total, width), BF16),
            pltpu.VMEM((total, width), BF16),
            pltpu.VMEM((3 * local, width), BF16),
            pltpu.VMEM((3 * local, 1), F32),
            pltpu.VMEM((3, width, width), F32),
            pltpu.VMEM((3, width, width), BF16),
            pltpu.VMEM((6, blk, width), BF16),
            pltpu.VMEM((heads, 2 * HD, total), BF16),
            pltpu.VMEM((heads, HD, total), BF16),
            pltpu.VMEM((heads, total, 2 * HD), BF16),
            pltpu.VMEM((heads, HD + 16, total), BF16),
            pltpu.VMEM((heads, total, HD), BF16),
            pltpu.VMEM((heads, HD, total), BF16),
            pltpu.VMEM((LEN, blk), F32),
            pltpu.VMEM((LEN, blk), BF16),
            pltpu.VMEM((heads, HD, total), F32),
            pltpu.VMEM((heads, HD, total), F32),
            pltpu.VMEM((heads, HD, blk), BF16),
            pltpu.VMEM((3 * local, blk), BF16),
            pltpu.VMEM((heads, HD, blk), F32),
            pltpu.VMEM((8, width), F32),
            pltpu.VMEM((swaps, 8, width), F32),
            pltpu.VMEM((width, 128), BF16),
            pltpu.VMEM((2, width, 128), BF16),
            pltpu.VMEM((width, 128), BF16),
            pltpu.VMEM((2, members - 1, width // members, 128), BF16),
            dma((6,)),
            dma((6,)),
            dma((3, 2)),
            dma((3, 2)),
            dma((2,)),
            dma((2, 2)),
            dma((2, members - 1)),
            dma((2, 2, members - 1)),
            dma((swaps,)),
            dma((swaps,)),
            dma((1,)),
            pltpu.SemaphoreType.REGULAR((2,)),
        ],
        compiler_params=pltpu.CompilerParams(
            vmem_limit_bytes=63 * 2**20, collective_id=0, has_side_effects=True
        ),
    )(
        tokens,
        cotangent,
        lengths,
        par,
        query_key_value,
        query_key_value_bias,
        dense_weight,
        expand_weight,
        contract_weight,
        cosine,
        sine,
    )
    rest = 3 * local
    grad_qkv = jnp.transpose(res[2, :rest].reshape(3, local, width), (0, 2, 1)).astype(F32)
    return (
        mixed,
        grad_tokens,
        vec[0],
        vec[1],
        vec[2],
        vec[3],
        grad_qkv,
        vec[6, :rest].reshape(3, local),
        res[2, rest:].astype(F32),
        vec[4],
        res[1].astype(F32),
        vec[5],
        res[0].astype(F32),
        vec[4],
    )


def solution(mesh):
    rows = P(("dp", "tensor"), None)
    weights = (
        P(None, None, "tensor"),
        P(None, "tensor"),
        P("tensor", None),
        P(),
        P(None, "tensor"),
        P("tensor"),
        P("tensor", None),
        P(),
    )
    return jax.shard_map(
        functools.partial(shards, mesh.shape["dp"]),
        mesh=mesh,
        in_specs=(rows, P(), P(), P(), P()) + weights + (P("dp"), rows),
        out_specs=(rows, rows, P(), P(), P(), P()) + weights,
        check_vma=False,
    )
```

```python
import functools

import jax
import jax.numpy as jnp
import numpy as np
from jax import lax
from jax.experimental import pallas as pl
from jax.experimental.pallas import tpu as pltpu
from jax.sharding import PartitionSpec as P

HD = 64
ROT = 16
LEN = 2048
EPS = 1e-05
MASKED = -1e30
F32 = jnp.float32
BF16 = jnp.bfloat16


def dot(a, b, ca, cb):
    return lax.dot_general(a, b, (((ca,), (cb,)), ((), ())), preferred_element_type=F32)


def angle_rows(count):
    half = ROT // 2
    freqs = np.float32(10000.0) ** (
        np.float32(-2.0) * np.arange(half, dtype=np.float32) / np.float32(ROT)
    )
    place = (np.arange(count) % LEN).astype(np.float32)
    angle = (freqs[:, None] * place[None, :]).astype(np.float32)
    return np.cos(angle), np.sin(angle)


def unit_rows(rows):
    values = rows.astype(F32)
    centred = values - jnp.mean(values, -1, keepdims=True)
    inverse = lax.rsqrt(jnp.mean(centred * centred, -1, keepdims=True) + EPS)
    return centred * inverse, inverse

MESH = pl.DeviceIdType.MESH
SUB = 256
UNIT = 1.25


def flip(value, bits):
    bit = 1
    while bit <= bits:
        if (bits // bit) % 2:
            value = value + bit * (1 - 2 * ((value // bit) % 2))
        bit *= 2
    return value


def pieces(n):
    made = [(SUB * k, SUB, k, 0) for k in range(7)]
    parts = 2 if n <= 16 else 1
    size = SUB // parts
    for k in range(2 * parts):
        made.append((7 * SUB + size * k, size, k // parts, size * (k % parts)))
    return made


def plan(rounds, chunks, points, width, margin=0.4, rate=0.05, delay=2.6, work=0.35):
    free = [points[0], points[0]]
    clock = points[0]
    reached = 0
    todo = [(when, k, 0) for k, (when, _) in enumerate(chunks)]
    made = []
    while todo:
        todo.sort()
        when, k, step = todo.pop(0)
        later = [(at, u) for u, at in enumerate(points) if at >= when and u >= reached]
        if later:
            at, reached = later[0]
            u = reached
            clock = max(at, clock)
        else:
            u = reached = len(points)
            clock = max(when, clock, points[-1] + 1.5)
        clock += work
        made.append((clock, u, k, step))
        if step < 2 * rounds + 2:
            size = chunks[k][1] * width * 1e-6
            turn = min(step, 2 * rounds + 1 - step)
            kind = 1 if turn else 0
            free[kind] = max(free[kind], clock) + size / 2**turn / rate
            todo.append((free[kind] + delay + (margin if later else 0.0), k, step + 1))
    return made


def core(
    n,
    tok,
    cot,
    len_ref,
    gain1_r,
    bias1_r,
    gain2_r,
    bias2_r,
    exp_r,
    outb1_r,
    outb2_r,
    qkv,
    qkv_b,
    wd_h,
    we_h,
    wc_h,
    cos_t,
    sin_t,
    mixed_o,
    gtok_o,
    res_o,
    vec_o,
    x_s,
    g_s,
    n1_s,
    s_s,
    wt,
    wd,
    we,
    wc,
    qb_s,
    acc,
    res,
    hold,
    qa,
    kt,
    kr,
    va,
    vr,
    dot_s,
    pt,
    mrun,
    dkt,
    dvt,
    ctx_s,
    dq_s,
    vec,
    vec_in,
    sx,
    rx,
    rz,
    in_sem,
    ag_send,
    ag_recv,
    rs_send,
    rs_recv,
    ar_send,
    ar_recv,
    v_send,
    v_recv,
    out_sem,
    free_sem,
):
    blk, width = tok.shape
    total = x_s.shape[0]
    local = wd.shape[0]
    heads = local // HD
    count = total // blk
    per = LEN // blk
    root = HD**-0.5
    band = 4 * HD
    attn = 2 * width
    rounds = n.bit_length() - 2
    dp = lax.axis_index("dp")
    t = lax.axis_index("tensor")
    core_bit = t % 2
    chip_bit = t // 2
    sib = (dp, flip(t, 1))
    across = (dp, flip(t, 2))
    peers = [(flip(dp, 2**q), t) for q in range(rounds + 1)]

    def send(src, dst, ssem, rsem, where):
        return pltpu.make_async_remote_copy(
            src_ref=src,
            dst_ref=dst,
            send_sem=ssem,
            recv_sem=rsem,
            device_id=where,
            device_id_type=MESH,
        )

    def block(b):
        return pl.ds(pl.multiple_of(b * blk, blk), blk)

    own = block(t)
    other = block(flip(t, 2))
    fetch = [
        pltpu.make_async_copy(tok, x_s.at[own], in_sem.at[0]),
        pltpu.make_async_copy(cot, g_s.at[own], in_sem.at[1]),
        pltpu.make_async_copy(we_h, we, in_sem.at[2]),
        pltpu.make_async_copy(wc_h, wc, in_sem.at[3]),
        pltpu.make_async_copy(wd_h, wd, in_sem.at[4]),
    ]
    for h in range(heads):
        for c in range(3):
            fetch.append(
                pltpu.make_async_copy(
                    qkv.at[c, h * HD : (h + 1) * HD, :],
                    wt.at[(3 * h + c) * HD : (3 * h + c + 1) * HD, :],
                    in_sem.at[5 + 3 * h + c],
                )
            )
    for copy in fetch:
        copy.start()

    barrier = pltpu.get_barrier_semaphore()
    greeted = [sib, across] + peers
    for who in greeted:
        pl.semaphore_signal(barrier, inc=1, device_id=who, device_id_type=MESH)
    pl.semaphore_wait(barrier, len(greeted))

    gather = [
        send(tok, x_s.at[own], ag_send.at[0], ag_recv.at[0], across),
        send(cot, g_s.at[own], ag_send.at[1], ag_recv.at[1], across),
        send(tok, x_s.at[own], ag_send.at[2], ag_recv.at[2], sib),
        send(cot, g_s.at[own], ag_send.at[3], ag_recv.at[3], sib),
        send(x_s.at[other], x_s.at[other], ag_send.at[4], ag_recv.at[4], sib),
        send(g_s.at[other], g_s.at[other], ag_send.at[5], ag_recv.at[5], sib),
    ]
    gather[0].start()
    gather[2].start()
    gather[3].start()

    gain1, bias1, gain2, bias2, exp_b = (
        r[...].reshape(1, width) for r in (gain1_r, bias1_r, gain2_r, bias2_r, exp_r)
    )
    for c in range(3):
        column = jnp.transpose(jnp.broadcast_to(qkv_b[c : c + 1, :], (8, local)))
        for h in range(heads):
            qb_s[(3 * h + c) * HD : (3 * h + c + 1) * HD, :] = column[h * HD : (h + 1) * HD, :1]
    for ref in (acc, vec, dkt, dvt):
        ref[...] = jnp.zeros_like(ref)
    one_row = (lax.broadcasted_iota(jnp.int32, (heads, HD, total), 1) == 0).astype(F32)
    qa[:, HD:, :] = one_row.astype(BF16)
    va[:, HD:, :] = one_row[:, : va.shape[1] - HD, :].astype(BF16)
    for copy in fetch:
        copy.wait()

    half = width // 2
    near_bit = dp % 2
    seat = dp // 2

    def lanes(bit):
        return pl.ds(pl.multiple_of(bit * half, 128), half)

    my_lanes = lanes(near_bit)
    chunks = pieces(n)

    def first_of(k, q):
        first = 0
        for p in range(q):
            first = first + ((seat // 2**p) % 2) * (chunks[k][1] // 2 ** (p + 1))
        return first

    def span(k, q, first):
        size = chunks[k][1] // 2**q
        return pl.ds(pl.multiple_of(chunks[k][0] + first, chunks[k][1] // 2**rounds), size)

    def kept(k, q):
        return span(k, q, first_of(k, q))

    def given(k, q):
        bit = (seat // 2 ** (q - 1)) % 2
        return span(k, q, first_of(k, q - 1) + (1 - bit) * (chunks[k][1] // 2**q))

    def whole_slot(k):
        _, rows, slot, low = chunks[k]
        return slot, pl.ds(low, rows)

    def slot_part(k, q):
        _, rows, slot, low = chunks[k]
        return slot, pl.ds(low + rows - rows // 2 ** (q - 1), rows // 2**q)

    def ar_copy(k, step):
        sems = (ar_send.at[step, k], ar_recv.at[step, k])
        if step == 0:
            return send(sx.at[whole_slot(k)], rx.at[whole_slot(k)], *sems, peers[0])
        if step <= rounds:
            return send(sx.at[slot_part(k, step)], rz.at[slot_part(k, step)], *sems, peers[step])
        if step <= 2 * rounds:
            q = 2 * rounds - step + 1
            piece = res.at[kept(k, q), my_lanes]
            return send(piece, piece, *sems, peers[q])
        piece = res.at[kept(k, 0), my_lanes]
        return send(piece, piece, *sems, peers[0])

    def advance(k, step):
        if step == 0:
            sx[whole_slot(k)] = acc[kept(k, 0), lanes(1 - near_bit)].astype(BF16)
        else:
            ar_copy(k, step - 1).wait()
        if step == 1:
            mine = kept(k, 0)
            acc[mine, my_lanes] = acc[mine, my_lanes] + rx[whole_slot(k)].astype(F32)
        if 2 <= step <= rounds + 1:
            mine = kept(k, step - 1)
            done = acc[mine, my_lanes] + rz[slot_part(k, step - 1)].astype(F32)
            if step <= rounds:
                acc[mine, my_lanes] = done
            else:
                res[mine, my_lanes] = done.astype(BF16)
        if 1 <= step <= rounds:
            sx[slot_part(k, step)] = acc[given(k, step), my_lanes].astype(BF16)
        if step < 2 * rounds + 2:
            ar_copy(k, step).start()

    clock = -7.0
    points = [-7.0, -5.0, -3.2, -1.6]
    clock = 0.0
    for group in (1, heads - 1):
        for i in range(count - 1, -1, -1):
            for _ in range(group * (i + 1)):
                clock += UNIT
                points.append(clock)
            clock += 0.9 if group == 1 else 2.2
            if group == 1 and i == 0:
                first_head = clock
    last_time = clock
    ready = [points[0]] * 3 + [points[2]] * 3 + [first_head]
    begin = last_time
    while True:
        times = ready + [begin] * (len(chunks) - len(ready))
        made = plan(rounds, [(r, c[1]) for r, c in zip(times, chunks)], points, width)
        through = max(at for at, (_, _, k, step) in enumerate(made) if k < 2)
        if through < min(at for at, (_, _, k, _) in enumerate(made) if k > 6):
            break
        begin = max(begin, made[through][0]) + 0.1
    ticks = {}
    after = []
    for when, u, k, step in made:
        if u < len(points):
            ticks.setdefault(u, []).append((k, step))
        else:
            after.append((when, k, step))

    def forward(b, slot, before_mix):
        rows = block(b)
        unit, _ = unit_rows(x_s[rows, :])
        n1 = (unit * gain1 + bias1).astype(BF16)
        n2 = (unit * gain2 + bias2).astype(BF16)
        n1_s[rows, :] = n1
        hold[2 + slot] = n2
        pre = dot(n2, we[...], 1, 0) + exp_b
        big = 0.5 * (1.0 + lax.erf(pre * np.float32(0.5**0.5)))
        act = (pre * big).astype(BF16)
        slope = big + pre * (jnp.exp(-0.5 * pre * pre) * np.float32((2 * np.pi) ** -0.5))
        hold[slot] = act
        hold[4 + slot] = slope.astype(BF16)
        mix = dot(act, wc[...], 1, 0).astype(BF16)
        before_mix()
        x_s[rows, :] = mix
        proj = dot(wt[...], n1, 1, 1) + qb_s[...]
        cosine = cos_t[:, rows]
        sine = sin_t[:, rows]

        def turn(rows_in):
            a = rows_in[: ROT // 2]
            c = rows_in[ROT // 2 : ROT]
            return jnp.concatenate(
                [a * cosine - c * sine, c * cosine + a * sine, rows_in[ROT:]], 0
            )

        place = lax.broadcasted_iota(jnp.int32, (HD, blk), 1) + (b % per) * blk
        first = lax.broadcasted_iota(jnp.int32, (HD, blk), 0) == 0
        extra = jnp.where(first & (place >= len_ref[0]), MASKED, 0.0)
        for h in range(heads):
            lo = 3 * h * HD
            q = turn(proj[lo : lo + HD])
            k = turn(proj[lo + HD : lo + 2 * HD])
            v = proj[lo + 2 * HD : lo + 3 * HD]
            qa[h, :HD, rows] = (q * root).astype(BF16)
            kt[h, :, rows] = k.astype(BF16)
            kr[h, rows, :] = jnp.transpose(jnp.concatenate([k, extra], 0)).astype(BF16)
            va[h, :HD, rows] = v.astype(BF16)
            vr[h, rows, :] = jnp.transpose(v).astype(BF16)

    def mate(k):
        low = (t + k) % 2
        high = (t // 2 + k // 2) % 2
        return low + 2 * high

    def phase(it, _):
        late = it // 4 > 0
        b = mate(jnp.where(late, 2 + it % 2, it))
        slot = jnp.where(late, it % 2, it // 3)
        rows = block(b)

        @pl.when(it == 1)
        def _():
            gather[2].wait_recv()
            gather[3].wait_recv()

        @pl.when(it == 2)
        def _():
            gather[0].wait_send()
            gather[1].start()
            gather[0].wait_recv()
            gather[4].start()

        @pl.when(it == 3)
        def _():
            gather[4].wait_recv()

        @pl.when(it < 4)
        def _():
            def settle():
                @pl.when(it == 2)
                def _():
                    gather[4].wait_send()

            forward(b, slot, settle)

        @pl.when(it == 4)
        def _():
            gather[1].wait_recv()
            gather[5].start()

        @pl.when(it == 5)
        def _():
            gather[5].wait_recv()

        for u in range(4):

            @pl.when(it == 6 + u)
            def _(u=u):
                for k, at in ticks.get(u, ()):
                    advance(k, at)

        @pl.when((it < 2) | (it == 4) | (it == 5))
        def _():
            acc[:width] += dot(hold[slot], g_s[rows, :], 0, 0)

        @pl.when((it < 2) | (it == 6) | (it == 7))
        def _():
            slope = hold[4 + slot].astype(F32)
            grad_pre = (dot(g_s[rows, :], wc[...], 1, 1) * slope).astype(BF16)
            hold[slot] = grad_pre
            vec[5:6, :] += jnp.sum(grad_pre.astype(F32), 0, keepdims=True)
            acc[width : 2 * width] += dot(hold[2 + slot], grad_pre, 0, 0)

        @pl.when((it < 2) | (it > 7))
        def _():
            part = dot(hold[slot], we[...], 1, 1)
            s_s[rows, :] = (part * gain2).astype(BF16)
            vec[2:3, :] += jnp.sum(part * hold[2 + slot].astype(F32), 0, keepdims=True)
            vec[3:4, :] += jnp.sum(part, 0, keepdims=True)
            grad_ctx = dot(wd[...], g_s[rows, :], 1, 1).astype(BF16)
            for h in range(heads):
                dot_s[h, :, rows] = grad_ctx[h * HD : (h + 1) * HD]

        return 0

    lax.fori_loop(0, 10, phase, 0)
    for k in (1, 2, 3, 5):
        gather[k].wait_send()
    pl.semaphore_signal(free_sem.at[0], inc=1, device_id=sib, device_id_type=MESH)
    pl.semaphore_signal(free_sem.at[1], inc=1, device_id=across, device_id_type=MESH)

    def to_sib(i):
        rows = block(i)
        slot = i // 2
        return [
            send(x_s.at[rows], hold.at[2 * slot], rs_send.at[slot, 0], rs_recv.at[slot, 0], sib),
            send(s_s.at[rows], hold.at[2 * slot + 1], rs_send.at[slot, 1], rs_recv.at[slot, 1], sib),
        ]

    def to_owner(i):
        rows = block(i)
        return [
            send(x_s.at[rows], hold.at[4], rs_send.at[2, 0], rs_recv.at[2, 0], across),
            send(s_s.at[rows], hold.at[5], rs_send.at[2, 1], rs_recv.at[2, 1], across),
        ]

    def hand_over(i):
        @pl.when(core_bit != i % 2)
        def _():
            for copy in to_sib(i):
                copy.start()

    def pass_on(i):
        @pl.when(core_bit == i % 2)
        def _():
            for copy in to_sib(i):
                copy.wait_recv()

        @pl.when((core_bit == i % 2) & (chip_bit != i // 2))
        def _():
            rows = block(i)
            slot = i // 2
            for w, ref in enumerate((x_s, s_s)):
                both = ref[rows, :].astype(F32) + hold[2 * slot + w].astype(F32)
                ref[rows, :] = both.astype(BF16)
            for copy in to_owner(i):
                copy.start()

    key_i = lax.broadcasted_iota(jnp.int32, (blk, blk), 0)
    query_i = lax.broadcasted_iota(jnp.int32, (blk, blk), 1)

    def gain_sum(some):
        for h in some:
            w32 = wt[3 * h * HD : 3 * (h + 1) * HD, :].astype(F32)
            mine = acc[attn + h * band : attn + h * band + 3 * HD, :]
            vec[0:1, :] += jnp.sum(w32 * mine, 0, keepdims=True)

    def attend(visit, _):
        group = visit // count
        step = visit % count
        i = count - 1 - step
        base = (i // per) * per
        mine = block(i)
        size = 1 + group * (heads - 2)
        passed = size * (count * step - (step * (step - 1)) // 2)
        passed += 4 + group * (count * (count + 1) // 2)

        def head(h, _):
            q_aug = qa[h, :, mine]

            def weigh(j, s, high, out):
                top = jnp.max(jnp.max(s.reshape(blk // 8, 8, blk), 0), 0, keepdims=True)
                top = jnp.maximum(high, top)
                p = jnp.exp(s - top).astype(BF16)
                pt[block(j - base), :] = p
                mrun[pl.ds(j - base, 1), :] = top
                return top, out * jnp.exp(high - top) + dot(va[h, :, block(j)], p, 1, 0)

            def onward(j, carry):
                return weigh(j, dot(kr[h, block(j), :], q_aug, 1, 0), *carry)

            begin = (jnp.full((1, blk), MASKED, F32), jnp.zeros((va.shape[1], blk), F32))
            carry = lax.fori_loop(base, i, onward, begin)
            s = dot(kr[h, mine, :], q_aug, 1, 0)
            high, out = weigh(i, jnp.where(key_i <= query_i, s, MASKED), *carry)
            scale = 1.0 / out[HD : HD + 1]
            ctx = out[:HD] * scale
            ctx_s[h, :, mine] = ctx.astype(BF16)
            grad = dot_s[h, :, mine].astype(F32) * scale
            q = q_aug[:HD]

            def back(j, dq):
                cols = block(j)
                p = pt[block(j - base), :]
                go = (grad * jnp.exp(mrun[pl.ds(j - base, 1), :] - high)).astype(BF16)
                inner = jnp.sum(ctx * go.astype(F32), 0, keepdims=True)
                dvt[h, :, cols] += dot(go, p, 1, 1)
                dp_t = dot(vr[h, cols, :], go, 1, 0)
                ds = (p.astype(F32) * (dp_t - inner)).astype(BF16)
                dkt[h, :, cols] += dot(q, ds, 1, 1)
                unit = passed + (h - group) * (i + 1) + (j - base)
                for u, steps in ticks.items():
                    if u < 4:
                        continue

                    @pl.when(unit == u)
                    def _(steps=steps):
                        for k, at in steps:
                            advance(k, at)

                return dq + dot(kt[h, :, cols], ds, 1, 0)

            dq_s[h] = lax.fori_loop(base, i + 1, back, jnp.zeros((HD, blk), F32))

            @pl.when((h == 1) & (step > 0))
            def _():
                pass_on(i + 1)

            return 0

        lax.fori_loop(group, group + size, head, 0)
        cosine = cos_t[:, mine]
        sine = sin_t[:, mine]

        def unturn(rows_in):
            a = rows_in[: ROT // 2]
            c = rows_in[ROT // 2 : ROT]
            return jnp.concatenate(
                [a * cosine + c * sine, c * cosine - a * sine, rows_in[ROT:]], 0
            )

        def projected(some):
            parts = [(qa[h, :HD, mine], kt[h, :, mine], va[h, :HD, mine]) for h in some]
            return jnp.concatenate([x for three in parts for x in three], 0)

        def weights(some):
            for h in some:
                qa[h, :HD, mine] = unturn(dq_s[h] * root).astype(BF16)
                kt[h, :, mine] = unturn(dkt[h, :, mine]).astype(BF16)
                va[h, :HD, mine] = dvt[h, :, mine].astype(BF16)
            lo, hi = some[0], some[-1] + 1
            ctx = ctx_s[lo:hi, :, mine].reshape((hi - lo) * HD, blk)
            grad_proj = projected(some)
            grad_d = dot(ctx, g_s[mine, :], 1, 0)
            grad_w = dot(grad_proj, n1_s[mine, :], 1, 0)
            for h in some:
                at = attn + h * band
                acc[at : at + 3 * HD, :] += grad_w[3 * (h - lo) * HD : 3 * (h - lo + 1) * HD]
                acc[at + 3 * HD : at + band, :] += grad_d[(h - lo) * HD : (h - lo + 1) * HD]

        @pl.when(group == 0)
        def _():
            weights([0])

            @pl.when(step == count - 1)
            def _():
                gain_sum([0])

        @pl.when(group == 1)
        def _():
            weights(list(range(1, heads)))
            ctx = ctx_s[:, :, mine].reshape(local, blk)
            mix = dot(ctx, wd[...], 0, 0) + x_s[mine, :].astype(F32)
            x_s[mine, :] = mix.astype(BF16)
            grad_proj = projected(range(heads))
            part = dot(grad_proj, wt[...], 0, 0) * gain1 + s_s[mine, :].astype(F32)
            s_s[mine, :] = part.astype(BF16)

            @pl.when(step == 0)
            def _():
                pl.semaphore_wait(free_sem.at[0], 1)
                pl.semaphore_wait(free_sem.at[1], 1)

            hand_over(i)
            ones = jnp.ones((8, blk), BF16)
            vec[6:7, : 3 * local] += dot(ones, grad_proj, 1, 1)[:1]

        return 0

    lax.fori_loop(0, 2 * count, attend, 0)
    again = pltpu.make_async_copy(tok, n1_s.at[own], in_sem.at[0])
    again.start()

    swaps = peers + [sib, across]
    inside = len(peers)

    def swap(q):
        return send(vec, vec_in.at[q], v_send.at[q], v_recv.at[q], swaps[q])

    shared = lax.broadcasted_iota(jnp.int32, vec.shape, 0) < 5

    def finish_swap(q):
        swap(q).wait()
        extra = vec_in[q]
        if q >= inside:
            extra = jnp.where(shared, extra, 0.0)
        vec[...] += extra

    def vectors():
        w32 = wt[...].astype(F32)
        column = jnp.transpose(jnp.broadcast_to(vec[6:7, : 3 * local], (8, 3 * local)))[:, :1]
        grad_bias = jnp.sum(w32 * column, 0, keepdims=True)
        gain_sum(range(1, heads))
        vec[1:2, :] = grad_bias
        vec[0:1, :] = (vec[0:1, :] - bias1 * grad_bias) / gain1
        vec[2:3, :] = (vec[2:3, :] - bias2 * vec[3:4, :]) / gain2
        vec[4:5, :] = jnp.sum(g_s[own, :].astype(F32), 0, keepdims=True)

    def tokens_out():
        for copy in to_owner(flip(t, 2)):
            copy.wait()
        again.wait()
        rows = n1_s[own, :]
        mix = rows.astype(F32) + (outb1_r[...] + outb2_r[...]).reshape(1, width)
        mix += x_s[own, :].astype(F32)
        s = s_s[own, :].astype(F32)
        for w in (2 * chip_bit, 4):
            mix += hold[w].astype(F32)
            s += hold[w + 1].astype(F32)
        mixed_o[...] = mix.astype(BF16)
        unit, inverse = unit_rows(rows)
        gtok_o[...] = g_s[own, :].astype(F32) + inverse * (
            s - jnp.mean(s, -1, keepdims=True) - unit * jnp.mean(s * unit, -1, keepdims=True)
        )

    jobs = [(when, functools.partial(advance, k, step)) for when, k, step in after]
    jobs.append((last_time + 2.9, vectors))
    jobs.append((last_time + 3.0, functools.partial(pass_on, 0)))
    for q in range(len(swaps)):

        def trade(q=q):
            if q > 0:
                finish_swap(q - 1)
            swap(q).start()

        jobs.append((last_time + 4.0 + 3.5 * q, trade))
    jobs.append((last_time + 4.0 + 3.5 * len(swaps), lambda: finish_swap(len(swaps) - 1)))
    jobs.append((last_time + 32.0, tokens_out))
    for _, job in sorted(jobs, key=lambda pair: pair[0]):
        job()
    out_copy = pltpu.make_async_copy(res, res_o, out_sem.at[0])
    out_copy.start()
    vec_o[...] = vec[...]
    for i in range(count):

        @pl.when(core_bit != i % 2)
        def _(i=i):
            for copy in to_sib(i):
                copy.wait_send()

    out_copy.wait()


def finish(res, mixed, gtok, vec, *outs):
    (mixed_o, gtok_o, gain1_o, bias1_o, gain2_o, bias2_o, qkv_o, qkvb_o, wd_o, db_o, we_o, be_o, wc_o, cb_o) = outs
    step = pl.program_id(0)
    width = res.shape[1]
    heads = wd_o.shape[0] // HD
    band = 4 * HD

    @pl.when(step == 0)
    def _():
        wc_o[...] = res[...].astype(F32)
        mixed_o[...] = mixed[...]
        gtok_o[...] = gtok[...]
        for ref, row in ((gain1_o, 0), (bias1_o, 1), (gain2_o, 2), (bias2_o, 3), (db_o, 4), (cb_o, 4), (be_o, 5)):
            ref[...] = vec[row, :]
        for h in range(heads):
            for c in range(3):
                lo = (3 * h + c) * HD
                qkvb_o[c : c + 1, h * HD : (h + 1) * HD] = vec[6:7, lo : lo + HD]

    @pl.when(step == 1)
    def _():
        we_o[...] = res[...].astype(F32)

    @pl.when(step == 2)
    def _():
        for h in range(heads):
            lo = h * band
            for c in range(3):
                qkv_o[c, h * HD : (h + 1) * HD, :] = res[lo + c * HD : lo + (c + 1) * HD, :].astype(F32)
            wd_o[h * HD : (h + 1) * HD, :] = res[lo + 3 * HD : lo + band, :].astype(F32)


def shards(
    n,
    tokens,
    input_gain,
    input_bias,
    post_gain,
    post_bias,
    query_key_value,
    query_key_value_bias,
    dense_weight,
    dense_bias,
    expand_weight,
    expand_bias,
    contract_weight,
    contract_bias,
    lengths,
    cotangent,
):
    blk, width = tokens.shape
    local = query_key_value.shape[2]
    hidden = expand_weight.shape[1]
    heads = local // HD
    total = 4 * blk
    rounds = n.bit_length() - 2
    swaps = rounds + 3
    cosine, sine = angle_rows(total)
    vmem = pl.BlockSpec(memory_space=pltpu.VMEM)
    smem = pl.BlockSpec(memory_space=pltpu.SMEM)
    hbm = pl.BlockSpec(memory_space=pl.ANY)
    dma = pltpu.SemaphoreType.DMA
    mixed, grad_tokens, res, vec = pl.pallas_call(
        functools.partial(core, n),
        name="core",
        out_shape=(
            jax.ShapeDtypeStruct((blk, width), BF16),
            jax.ShapeDtypeStruct((blk, width), F32),
            jax.ShapeDtypeStruct((3 * width, width), BF16),
            jax.ShapeDtypeStruct((8, width), F32),
        ),
        in_specs=[hbm, hbm, smem] + [vmem] * 7 + [hbm, vmem, hbm, hbm, hbm, vmem, vmem],
        out_specs=[vmem, vmem, hbm, vmem],
        scratch_shapes=[
            pltpu.VMEM((total, width), BF16),
            pltpu.VMEM((total, width), BF16),
            pltpu.VMEM((total, width), BF16),
            pltpu.VMEM((total, width), BF16),
            pltpu.VMEM((3 * local, width), BF16),
            pltpu.VMEM((local, width), BF16),
            pltpu.VMEM((width, hidden), BF16),
            pltpu.VMEM((hidden, width), BF16),
            pltpu.VMEM((3 * local, 1), F32),
            pltpu.VMEM((3 * width, width), F32),
            pltpu.VMEM((3 * width, width), BF16),
            pltpu.VMEM((6, blk, width), BF16),
            pltpu.VMEM((heads, 2 * HD, total), BF16),
            pltpu.VMEM((heads, HD, total), BF16),
            pltpu.VMEM((heads, total, 2 * HD), BF16),
            pltpu.VMEM((heads, HD + 16, total), BF16),
            pltpu.VMEM((heads, total, HD), BF16),
            pltpu.VMEM((heads, HD, total), BF16),
            pltpu.VMEM((LEN, blk), BF16),
            pltpu.VMEM((8, blk), F32),
            pltpu.VMEM((heads, HD, total), F32),
            pltpu.VMEM((heads, HD, total), F32),
            pltpu.VMEM((heads, HD, total), BF16),
            pltpu.VMEM((heads, HD, blk), F32),
            pltpu.VMEM((8, width), F32),
            pltpu.VMEM((swaps, 8, width), F32),
            pltpu.VMEM((7, SUB, width // 2), BF16),
            pltpu.VMEM((7, SUB, width // 2), BF16),
            pltpu.VMEM((7, SUB, width // 2), BF16),
            dma((5 + 3 * heads,)),
            dma((6,)),
            dma((6,)),
            dma((3, 2)),
            dma((3, 2)),
            dma((2 * rounds + 2, len(pieces(n)))),
            dma((2 * rounds + 2, len(pieces(n)))),
            dma((swaps,)),
            dma((swaps,)),
            dma((1,)),
            pltpu.SemaphoreType.REGULAR((2,)),
        ],
        compiler_params=pltpu.CompilerParams(
            vmem_limit_bytes=63 * 2**20, collective_id=0, has_side_effects=True
        ),
    )(
        tokens,
        cotangent,
        lengths,
        input_gain,
        input_bias,
        post_gain,
        post_bias,
        expand_bias,
        dense_bias,
        contract_bias,
        jnp.transpose(query_key_value, (0, 2, 1)),
        query_key_value_bias,
        dense_weight,
        expand_weight,
        contract_weight,
        cosine,
        sine,
    )

    def whole(*shape):
        return pl.BlockSpec(shape, lambda g: (0,) * len(shape))

    vector = jax.ShapeDtypeStruct((width,), F32)
    outs = pl.pallas_call(
        finish,
        name="finish",
        grid=(3,),
        in_specs=[
            pl.BlockSpec((width, width), lambda g: (g, 0)),
            whole(blk, width),
            whole(blk, width),
            whole(8, width),
        ],
        out_specs=[whole(blk, width), whole(blk, width)]
        + [whole(width)] * 4
        + [
            whole(3, local, width),
            whole(3, local),
            whole(local, width),
            whole(width),
            whole(width, hidden),
            whole(hidden),
            whole(hidden, width),
            whole(width),
        ],
        out_shape=(
            jax.ShapeDtypeStruct((blk, width), BF16),
            jax.ShapeDtypeStruct((blk, width), F32),
            vector,
            vector,
            vector,
            vector,
            jax.ShapeDtypeStruct((3, local, width), F32),
            jax.ShapeDtypeStruct((3, local), F32),
            jax.ShapeDtypeStruct((local, width), F32),
            vector,
            jax.ShapeDtypeStruct((width, hidden), F32),
            jax.ShapeDtypeStruct((hidden,), F32),
            jax.ShapeDtypeStruct((hidden, width), F32),
            vector,
        ),
        compiler_params=pltpu.CompilerParams(vmem_limit_bytes=63 * 2**20),
    )(res, mixed, grad_tokens, vec)
    outs = list(outs)
    outs[6] = jnp.transpose(outs[6], (0, 2, 1))
    return tuple(outs)


def solution(mesh):
    rows = P(("dp", "tensor"), None)
    weights = (
        P(None, None, "tensor"),
        P(None, "tensor"),
        P("tensor", None),
        P(),
        P(None, "tensor"),
        P("tensor"),
        P("tensor", None),
        P(),
    )
    return jax.shard_map(
        functools.partial(shards, mesh.shape["dp"]),
        mesh=mesh,
        in_specs=(rows, P(), P(), P(), P()) + weights + (P("dp"), rows),
        out_specs=(rows, rows, P(), P(), P(), P()) + weights,
        check_vma=False,
    )
```

```python
import functools

import jax
import jax.numpy as jnp
import numpy as np
from jax import lax
from jax.experimental import pallas as pl
from jax.experimental.pallas import tpu as pltpu
from jax.sharding import PartitionSpec as P

HD = 64
ROT = 16
LEN = 2048
EPS = 1e-05
MASKED = -1e30
F32 = jnp.float32
BF16 = jnp.bfloat16


def dot(a, b, ca, cb):
    return lax.dot_general(a, b, (((ca,), (cb,)), ((), ())), preferred_element_type=F32)


def angle_rows(count):
    half = ROT // 2
    freqs = np.float32(10000.0) ** (
        np.float32(-2.0) * np.arange(half, dtype=np.float32) / np.float32(ROT)
    )
    place = (np.arange(count) % LEN).astype(np.float32)
    angle = (freqs[:, None] * place[None, :]).astype(np.float32)
    return np.cos(angle), np.sin(angle)


def unit_rows(rows):
    values = rows.astype(F32)
    centred = values - jnp.mean(values, -1, keepdims=True)
    inverse = lax.rsqrt(jnp.mean(centred * centred, -1, keepdims=True) + EPS)
    return centred * inverse, inverse

MESH = pl.DeviceIdType.MESH
SUB = 256
UNIT = 1.0
FRONT = 0.52
ORDER = (0,)


def flip(value, bits):
    bit = 1
    while bit <= bits:
        if (bits // bit) % 2:
            value = value + bit * (1 - 2 * ((value // bit) % 2))
        bit *= 2
    return value


def pieces(n, heads):
    bits = tuple(range(n.bit_length() - 1))
    orders = (bits, bits[1:] + bits[:1], bits[1:2] + bits[:1] + bits[2:])
    count = 6 + heads
    made = []
    for k in range(count):
        parts = 2 if k == count - 1 and n <= 16 else 1
        size = SUB // parts
        made += [[SUB * k + size * p, size] for p in range(parts)]
    return [(a, b, orders[ORDER[k % len(ORDER)]]) for k, (a, b) in enumerate(made)]


def plan(chunks, ready, points, width, margin=0.5, rate=0.045, delay=3.0, work=0.2):
    free = {}
    clock = points[0]
    reached = 0
    todo = [(when, k, 0) for k, when in enumerate(ready)]
    made = []
    while todo:
        todo.sort()
        when, k, step = todo.pop(0)
        later = [(at, u) for u, at in enumerate(points) if at >= when and u >= reached]
        if later:
            at, reached = later[0]
            clock = max(at, clock)
        else:
            reached = len(points)
            clock = max(when, clock, points[-1] + 1.5)
        clock += work
        made.append((clock, reached, k, step))
        _, rows, order = chunks[k]
        if step < 2 * len(order):
            turn = min(step, 2 * len(order) - 1 - step)
            cost = rows * width * 2e-6 / 2 ** (turn + 1) / rate
            uses = {0: {"x": 1}, 1: {"end": 1}}.get(order[turn], {"end": 1, "mid": 2})
            through = clock
            for link, share in uses.items():
                free[link] = max(free.get(link, points[0]), clock) + share * cost
                through = max(through, free[link])
            todo.append((through + delay + (margin if later else 0.0), k, step + 1))
    return made


def core(
    n,
    tok,
    cot,
    len_ref,
    gain1_r,
    bias1_r,
    gain2_r,
    bias2_r,
    exp_r,
    outb1_r,
    outb2_r,
    qkv,
    qkv_b,
    wd_h,
    we_h,
    wc_h,
    cos_t,
    sin_t,
    mixed_o,
    gtok_o,
    res_o,
    vec_o,
    x_s,
    g_s,
    n1_s,
    s_s,
    wt,
    wd,
    we,
    wc,
    qb_s,
    acc,
    res,
    hold,
    qa,
    kt,
    kr,
    va,
    vr,
    dot_s,
    lse,
    dkt,
    dvt,
    ctx_s,
    vec,
    vec_in,
    sx,
    rx,
    in_sem,
    ag_send,
    ag_recv,
    rs_send,
    rs_recv,
    ar_send,
    ar_recv,
    v_send,
    v_recv,
    out_sem,
    free_sem,
):
    blk, width = tok.shape
    total = x_s.shape[0]
    local = wd.shape[0]
    heads = local // HD
    count = total // blk
    per = LEN // blk
    root = HD**-0.5
    band = 4 * HD
    attn = 2 * width
    bits = n.bit_length() - 1
    dp = lax.axis_index("dp")
    t = lax.axis_index("tensor")
    core_bit = t % 2
    chip_bit = t // 2
    sib = (dp, flip(t, 1))
    across = (dp, flip(t, 2))
    peers = [(flip(dp, 2**q), t) for q in range(bits)]

    def send(src, dst, ssem, rsem, where):
        return pltpu.make_async_remote_copy(
            src_ref=src,
            dst_ref=dst,
            send_sem=ssem,
            recv_sem=rsem,
            device_id=where,
            device_id_type=MESH,
        )

    def block(b):
        return pl.ds(pl.multiple_of(b * blk, blk), blk)

    own = block(t)
    other = block(flip(t, 2))
    fetch = [
        pltpu.make_async_copy(tok, x_s.at[own], in_sem.at[0]),
        pltpu.make_async_copy(cot, g_s.at[own], in_sem.at[1]),
        pltpu.make_async_copy(we_h, we, in_sem.at[2]),
        pltpu.make_async_copy(wc_h, wc, in_sem.at[3]),
        pltpu.make_async_copy(wd_h, wd, in_sem.at[4]),
    ]
    for h in range(heads):
        for c in range(3):
            fetch.append(
                pltpu.make_async_copy(
                    qkv.at[c, h * HD : (h + 1) * HD, :],
                    wt.at[(3 * h + c) * HD : (3 * h + c + 1) * HD, :],
                    in_sem.at[5 + 3 * h + c],
                )
            )
    for copy in fetch:
        copy.start()

    barrier = pltpu.get_barrier_semaphore()
    greeted = [sib, across] + peers
    for who in greeted:
        pl.semaphore_signal(barrier, inc=1, device_id=who, device_id_type=MESH)
    pl.semaphore_wait(barrier, len(greeted))

    gather = [
        send(tok, x_s.at[own], ag_send.at[0], ag_recv.at[0], across),
        send(cot, g_s.at[own], ag_send.at[1], ag_recv.at[1], across),
        send(tok, x_s.at[own], ag_send.at[2], ag_recv.at[2], sib),
        send(cot, g_s.at[own], ag_send.at[3], ag_recv.at[3], sib),
        send(x_s.at[other], x_s.at[other], ag_send.at[4], ag_recv.at[4], sib),
        send(g_s.at[other], g_s.at[other], ag_send.at[5], ag_recv.at[5], sib),
    ]
    gather[0].start()
    gather[2].start()
    gather[3].start()

    gain1, bias1, gain2, bias2, exp_b = (
        r[...].reshape(1, width) for r in (gain1_r, bias1_r, gain2_r, bias2_r, exp_r)
    )
    for c in range(3):
        column = jnp.transpose(jnp.broadcast_to(qkv_b[c : c + 1, :], (8, local)))
        for h in range(heads):
            qb_s[(3 * h + c) * HD : (3 * h + c + 1) * HD, :] = column[h * HD : (h + 1) * HD, :1]
    for ref in (acc, vec):
        ref[...] = jnp.zeros_like(ref)
    one_row = (lax.broadcasted_iota(jnp.int32, (heads, HD, total), 1) == 0).astype(F32)
    qa[:, HD:, :] = one_row.astype(BF16)
    va[:, HD:, :] = one_row[:, : va.shape[1] - HD, :].astype(BF16)
    for copy in fetch:
        copy.wait()

    chunks = pieces(n, heads)

    def rows_of(k, first, size):
        step = min(chunks[k][1] // n, 128)
        return pl.ds(pl.multiple_of(chunks[k][0] + first, step), size)

    def first_of(k, q):
        first = 0
        for p in range(q):
            first = first + ((dp // 2 ** chunks[k][2][p]) % 2) * (chunks[k][1] // 2 ** (p + 1))
        return first

    def kept(k, q):
        return rows_of(k, first_of(k, q), chunks[k][1] // 2**q)

    def given(k, q):
        size = chunks[k][1] // 2**q
        bit = (dp // 2 ** chunks[k][2][q - 1]) % 2
        return rows_of(k, first_of(k, q - 1) + (1 - bit) * size, size)

    def landing(k, q):
        first, rows, _ = chunks[k]
        return pl.ds(first + rows - rows // 2 ** (q - 1), rows // 2**q)

    def ar_copy(k, step):
        sems = (ar_send.at[step, k], ar_recv.at[step, k])
        order = chunks[k][2]
        if step < bits:
            return send(sx.at[landing(k, step + 1)], rx.at[landing(k, step + 1)], *sems, peers[order[step]])
        q = 2 * bits - step
        piece = res.at[kept(k, q)]
        return send(piece, piece, *sems, peers[order[q - 1]])

    def advance(k, step):
        if step > 0:
            ar_copy(k, step - 1).wait()
        if 1 <= step <= bits:
            mine = kept(k, step)
            done = acc[mine, :] + rx[landing(k, step), :].astype(F32)
            if step < bits:
                acc[mine, :] = done
            else:
                res[mine, :] = done.astype(BF16)
        if step < bits:
            sx[landing(k, step + 1), :] = acc[given(k, step + 1), :].astype(BF16)
        if step < 2 * bits:
            ar_copy(k, step).start()

    first_it = 9
    points = [-14.2, -12.3, -10.4, -8.9]
    lead = len(points)
    points += [-7.4 + FRONT * (u + 1) for u in range(heads * count)]
    mid = len(points)
    ends = []
    clock = 0.0
    for h in range(heads):
        for i in range(count - 1, -1, -1):
            for _ in range(i + 1):
                clock += UNIT
                points.append(clock)
            clock += 0.7 if h < heads - 1 else 1.6
        ends.append(clock)
    last_time = clock
    ready = [points[0]] * 3 + [points[2]] * 3 + ends
    ready += [last_time] * (len(chunks) - len(ready))
    ticks = {}
    after = []
    for when, u, k, step in plan(chunks, ready, points, width):
        if u < len(points):
            ticks.setdefault(u, []).append(functools.partial(advance, k, step))
        else:
            after.append((when, functools.partial(advance, k, step)))

    def forward(b, slot, before_mix):
        rows = block(b)
        unit, _ = unit_rows(x_s[rows, :])
        n1 = (unit * gain1 + bias1).astype(BF16)
        n2 = (unit * gain2 + bias2).astype(BF16)
        n1_s[rows, :] = n1
        hold[2 + slot] = n2
        pre = dot(n2, we[...], 1, 0) + exp_b
        big = 0.5 * (1.0 + lax.erf(pre * np.float32(0.5**0.5)))
        act = (pre * big).astype(BF16)
        slope = big + pre * (jnp.exp(-0.5 * pre * pre) * np.float32((2 * np.pi) ** -0.5))
        hold[slot] = act
        hold[4 + slot] = slope.astype(BF16)
        mix = dot(act, wc[...], 1, 0).astype(BF16)
        before_mix()
        x_s[rows, :] = mix
        proj = dot(wt[...], n1, 1, 1) + qb_s[...]
        cosine = cos_t[:, rows]
        sine = sin_t[:, rows]

        def turn(rows_in):
            a = rows_in[: ROT // 2]
            c = rows_in[ROT // 2 : ROT]
            return jnp.concatenate(
                [a * cosine - c * sine, c * cosine + a * sine, rows_in[ROT:]], 0
            )

        place = lax.broadcasted_iota(jnp.int32, (HD, blk), 1) + (b % per) * blk
        first = lax.broadcasted_iota(jnp.int32, (HD, blk), 0) == 0
        extra = jnp.where(first & (place >= len_ref[0]), MASKED, 0.0)
        for h in range(heads):
            lo = 3 * h * HD
            q = turn(proj[lo : lo + HD])
            k = turn(proj[lo + HD : lo + 2 * HD])
            v = proj[lo + 2 * HD : lo + 3 * HD]
            qa[h, :HD, rows] = (q * root).astype(BF16)
            kt[h, :, rows] = k.astype(BF16)
            kr[h, rows, :] = jnp.transpose(jnp.concatenate([k, extra], 0)).astype(BF16)
            va[h, :HD, rows] = v.astype(BF16)
            vr[h, rows, :] = jnp.transpose(v).astype(BF16)

    def mate(k):
        low = (t + k) % 2
        high = (t // 2 + k // 2) % 2
        return low + 2 * high

    key_i = lax.broadcasted_iota(jnp.int32, (blk, blk), 0)
    query_i = lax.broadcasted_iota(jnp.int32, (blk, blk), 1)

    def serve(unit, low, high):
        for u, jobs in ticks.items():
            if low <= u < high:

                @pl.when(unit == u)
                def _(jobs=jobs):
                    for job in jobs:
                        job()

    def front(i):
        passed = jnp.where(i == count - 1, lead, -mid)
        base = (i // per) * per
        mine = block(i)

        def head(h, _):
            q_aug = qa[h, :, mine]

            def weigh(j, scores, high, out):
                top = jnp.max(jnp.max(scores.reshape(blk // 8, 8, blk), 0), 0, keepdims=True)
                top = jnp.maximum(high, top)
                p = jnp.exp(scores - top).astype(BF16)
                return top, out * jnp.exp(high - top) + dot(va[h, :, block(j)], p, 1, 0)

            def onward(j, carry):
                more = weigh(j, dot(kr[h, block(j), :], q_aug, 1, 0), *carry)
                serve(passed + h * count + (j - base), lead, mid)
                return more

            begin = (jnp.full((1, blk), MASKED, F32), jnp.zeros((va.shape[1], blk), F32))
            carry = lax.fori_loop(base, i, onward, begin)
            scores = dot(kr[h, mine, :], q_aug, 1, 0)
            high, out = weigh(i, jnp.where(key_i <= query_i, scores, MASKED), *carry)
            norm = out[HD : HD + 1]
            ctx_s[h, :, mine] = (out[:HD] * (1.0 / norm)).astype(BF16)
            lse[pl.ds(h, 1), mine] = high + jnp.log(norm)
            serve(passed + h * count + (i - base), lead, mid)
            return 0

        lax.fori_loop(0, heads, head, 0)
        ctx = ctx_s[:, :, mine].reshape(local, blk)
        mix = dot(ctx, wd[...], 0, 0) + x_s[mine, :].astype(F32)
        x_s[mine, :] = mix.astype(BF16)

    def phase(it, _):
        late = it // 7 > 0
        b = mate(jnp.where(late, 2 + (it + 1) % 2, it % 4))
        slot = jnp.where(late, (it + 1) % 2, (it % 4) // 3)
        rows = block(b)

        @pl.when(it == 1)
        def _():
            gather[2].wait_recv()
            gather[3].wait_recv()

        @pl.when(it == 2)
        def _():
            gather[0].wait_send()
            gather[1].start()
            gather[0].wait_recv()
            gather[4].start()

        @pl.when(it == 3)
        def _():
            gather[4].wait_recv()

        @pl.when(it < 4)
        def _():
            def settle():
                @pl.when(it == 2)
                def _():
                    gather[4].wait_send()

            forward(b, slot, settle)

        @pl.when(((it > 3) & (it < 7)) | (it == 13))
        def _():
            front(jnp.where(late, count - 1, it - 4))

        @pl.when(it == 7)
        def _():
            gather[1].wait_recv()
            gather[5].start()

        @pl.when(it == 8)
        def _():
            gather[5].wait_recv()

        serve(it - first_it, 0, lead)

        @pl.when((it < 2) | (it == 7) | (it == 8))
        def _():
            acc[:width] += dot(hold[slot], g_s[rows, :], 0, 0)

        @pl.when((it < 2) | (it == 9) | (it == 10))
        def _():
            slope = hold[4 + slot].astype(F32)
            grad_pre = (dot(g_s[rows, :], wc[...], 1, 1) * slope).astype(BF16)
            hold[slot] = grad_pre
            vec[5:6, :] += jnp.sum(grad_pre.astype(F32), 0, keepdims=True)
            acc[width : 2 * width] += dot(hold[2 + slot], grad_pre, 0, 0)

        @pl.when((it < 2) | (it == 11) | (it == 12))
        def _():
            part = dot(hold[slot], we[...], 1, 1)
            s_s[rows, :] = (part * gain2).astype(BF16)
            vec[2:3, :] += jnp.sum(part * hold[2 + slot].astype(F32), 0, keepdims=True)
            vec[3:4, :] += jnp.sum(part, 0, keepdims=True)
            grad_ctx = dot(wd[...], g_s[rows, :], 1, 1).astype(BF16)
            for h in range(heads):
                dot_s[h, :, rows] = grad_ctx[h * HD : (h + 1) * HD]

        return 0

    lax.fori_loop(0, 14, phase, 0)
    for k in (1, 2, 3, 5):
        gather[k].wait_send()
    pl.semaphore_signal(free_sem.at[0], inc=1, device_id=sib, device_id_type=MESH)
    pl.semaphore_signal(free_sem.at[1], inc=1, device_id=across, device_id_type=MESH)

    def dense_grad(i, _):
        grad_d = dot(ctx_s[:, :, block(i)].reshape(local, blk), g_s[block(i), :], 1, 0)
        for h in range(heads):
            at = attn + h * band + 3 * HD
            acc[at : at + HD, :] += grad_d[h * HD : (h + 1) * HD]
        return 0

    lax.fori_loop(0, count, dense_grad, 0)

    sums = (x_s, s_s)

    def to_sib(i, w):
        slot = i // 2
        src = sums[w].at[block(i)]
        return send(src, hold.at[2 * slot + w], rs_send.at[slot, w], rs_recv.at[slot, w], sib)

    def to_owner(i, w):
        src = sums[w].at[block(i)]
        return send(src, hold.at[4 + w], rs_send.at[2, w], rs_recv.at[2, w], across)

    def hand_over(i, w):
        @pl.when(core_bit != i % 2)
        def _():
            to_sib(i, w).start()

    def pass_on(i, w):
        @pl.when(core_bit == i % 2)
        def _():
            to_sib(i, w).wait_recv()

        @pl.when((core_bit == i % 2) & (chip_bit != i // 2))
        def _():
            rows = block(i)
            both = sums[w][rows, :].astype(F32) + hold[2 * (i // 2) + w].astype(F32)
            sums[w][rows, :] = both.astype(BF16)
            to_owner(i, w).start()

    def mixes_over():
        pl.semaphore_wait(free_sem.at[0], 1)
        pl.semaphore_wait(free_sem.at[1], 1)

        def one(i, _):
            hand_over(i, 0)
            return 0

        lax.fori_loop(0, count, one, 0)

    def mixes_on():
        def one(i, _):
            pass_on(i, 0)
            return 0

        lax.fori_loop(0, count, one, 0)

    ticks.setdefault(mid + 3, []).insert(0, mixes_over)
    ticks.setdefault(mid + 7, []).insert(0, mixes_on)

    def attend(visit, _):
        h = visit // count
        i = count - 1 - visit % count
        base = (i // per) * per
        mine = block(i)
        passed = h * (count * (count + 1) // 2) + mid
        passed += count * (count - 1 - i) - ((count - 1 - i) * (count - 2 - i)) // 2

        @pl.when(i == count - 1)
        def _():
            dkt[...] = jnp.zeros_like(dkt)
            dvt[...] = jnp.zeros_like(dvt)

        q_aug = qa[h, :, mine]
        q = q_aug[:HD]
        go = dot_s[h, :, mine]
        total_log = lse[pl.ds(h, 1), mine]
        inner = jnp.sum(ctx_s[h, :, mine].astype(F32) * go.astype(F32), 0, keepdims=True)

        def back(j, scores):
            cols = block(j)
            p = jnp.exp(scores - total_log)
            dvt[:, cols] += dot(go, p.astype(BF16), 1, 1)
            dp_t = dot(vr[h, cols, :], go, 1, 0)
            ds = (p * (dp_t - inner)).astype(BF16)
            dkt[:, cols] += dot(q, ds, 1, 1)
            return dot(kt[h, :, cols], ds, 1, 0)

        def onward(j, dq):
            more = back(j, dot(kr[h, block(j), :], q_aug, 1, 0))
            serve(passed + (j - base), mid, len(points))
            return dq + more

        dq = lax.fori_loop(base, i, onward, jnp.zeros((HD, blk), F32))
        scores = dot(kr[h, mine, :], q_aug, 1, 0)
        dq += back(i, jnp.where(key_i <= query_i, scores, MASKED))
        serve(passed + (i - base), mid, len(points))
        cosine = cos_t[:, mine]
        sine = sin_t[:, mine]

        def unturn(rows_in):
            a = rows_in[: ROT // 2]
            c = rows_in[ROT // 2 : ROT]
            return jnp.concatenate(
                [a * cosine + c * sine, c * cosine - a * sine, rows_in[ROT:]], 0
            )

        qa[h, :HD, mine] = unturn(dq * root).astype(BF16)
        kt[h, :, mine] = unturn(dkt[:, mine]).astype(BF16)
        va[h, :HD, mine] = dvt[:, mine].astype(BF16)
        grad_proj = jnp.concatenate([qa[h, :HD, mine], kt[h, :, mine], va[h, :HD, mine]], 0)
        at = attn + h * band
        acc[pl.ds(pl.multiple_of(at, HD), 3 * HD), :] += dot(grad_proj, n1_s[mine, :], 1, 0)

        @pl.when(i == 0)
        def _():
            w32 = wt[pl.ds(pl.multiple_of(3 * h * HD, HD), 3 * HD), :].astype(F32)
            grads = acc[pl.ds(pl.multiple_of(at, HD), 3 * HD), :]
            vec[0:1, :] += jnp.sum(w32 * grads, 0, keepdims=True)

        @pl.when(h == heads - 1)
        def _():
            @pl.when(i < count - 1)
            def _():
                pass_on(i + 1, 1)

            parts = [(qa[g, :HD, mine], kt[g, :, mine], va[g, :HD, mine]) for g in range(heads)]
            every = jnp.concatenate([x for three in parts for x in three], 0)
            part = dot(every, wt[...], 0, 0) * gain1 + s_s[mine, :].astype(F32)
            s_s[mine, :] = part.astype(BF16)
            hand_over(i, 1)
            ones = jnp.ones((8, blk), BF16)
            vec[6:7, : 3 * local] += dot(ones, every, 1, 1)[:1]

        return 0

    lax.fori_loop(0, heads * count, attend, 0)
    again = pltpu.make_async_copy(tok, n1_s.at[own], in_sem.at[0])
    again.start()

    swaps = peers + [sib, across]
    inside = len(peers)

    def swap(q):
        return send(vec, vec_in.at[q], v_send.at[q], v_recv.at[q], swaps[q])

    shared = lax.broadcasted_iota(jnp.int32, vec.shape, 0) < 5

    def finish_swap(q):
        swap(q).wait()
        extra = vec_in[q]
        if q >= inside:
            extra = jnp.where(shared, extra, 0.0)
        vec[...] += extra

    def vectors():
        w32 = wt[...].astype(F32)
        column = jnp.transpose(jnp.broadcast_to(vec[6:7, : 3 * local], (8, 3 * local)))[:, :1]
        grad_bias = jnp.sum(w32 * column, 0, keepdims=True)
        vec[1:2, :] = grad_bias
        vec[0:1, :] = (vec[0:1, :] - bias1 * grad_bias) / gain1
        vec[2:3, :] = (vec[2:3, :] - bias2 * vec[3:4, :]) / gain2
        vec[4:5, :] = jnp.sum(g_s[own, :].astype(F32), 0, keepdims=True)

    def tokens_out():
        for w in range(2):
            to_owner(flip(t, 2), w).wait()
        again.wait()
        rows = n1_s[own, :]
        mix = rows.astype(F32) + (outb1_r[...] + outb2_r[...]).reshape(1, width)
        mix += x_s[own, :].astype(F32)
        s = s_s[own, :].astype(F32)
        for w in (2 * chip_bit, 4):
            mix += hold[w].astype(F32)
            s += hold[w + 1].astype(F32)
        mixed_o[...] = mix.astype(BF16)
        unit, inverse = unit_rows(rows)
        gtok_o[...] = g_s[own, :].astype(F32) + inverse * (
            s - jnp.mean(s, -1, keepdims=True) - unit * jnp.mean(s * unit, -1, keepdims=True)
        )

    jobs = list(after)
    jobs.append((last_time + 2.9, vectors))
    jobs.append((last_time + 3.0, functools.partial(pass_on, 0, 1)))
    for q in range(len(swaps)):

        def trade(q=q):
            if q > 0:
                finish_swap(q - 1)
            swap(q).start()

        jobs.append((last_time + 4.0 + 3.5 * q, trade))
    jobs.append((last_time + 4.0 + 3.5 * len(swaps), lambda: finish_swap(len(swaps) - 1)))
    jobs.append((last_time + 20.0, tokens_out))
    for _, job in sorted(jobs, key=lambda pair: pair[0]):
        job()
    out_copy = pltpu.make_async_copy(res, res_o, out_sem.at[0])
    out_copy.start()
    vec_o[...] = vec[...]
    for i in range(count):

        @pl.when(core_bit != i % 2)
        def _(i=i):
            for w in range(2):
                to_sib(i, w).wait_send()

    out_copy.wait()


def finish(res, mixed, gtok, vec, *outs):
    (mixed_o, gtok_o, gain1_o, bias1_o, gain2_o, bias2_o, qkv_o, qkvb_o, wd_o, db_o, we_o, be_o, wc_o, cb_o) = outs
    step = pl.program_id(0)
    width = res.shape[1]
    heads = wd_o.shape[0] // HD
    band = 4 * HD

    @pl.when(step == 0)
    def _():
        wc_o[...] = res[...].astype(F32)
        mixed_o[...] = mixed[...]
        gtok_o[...] = gtok[...]
        for ref, row in ((gain1_o, 0), (bias1_o, 1), (gain2_o, 2), (bias2_o, 3), (db_o, 4), (cb_o, 4), (be_o, 5)):
            ref[...] = vec[row, :]
        for h in range(heads):
            for c in range(3):
                lo = (3 * h + c) * HD
                qkvb_o[c : c + 1, h * HD : (h + 1) * HD] = vec[6:7, lo : lo + HD]

    @pl.when(step == 1)
    def _():
        we_o[...] = res[...].astype(F32)

    @pl.when(step == 2)
    def _():
        for h in range(heads):
            lo = h * band
            for c in range(3):
                qkv_o[c, h * HD : (h + 1) * HD, :] = res[lo + c * HD : lo + (c + 1) * HD, :].astype(F32)
            wd_o[h * HD : (h + 1) * HD, :] = res[lo + 3 * HD : lo + band, :].astype(F32)


def shards(
    n,
    tokens,
    input_gain,
    input_bias,
    post_gain,
    post_bias,
    query_key_value,
    query_key_value_bias,
    dense_weight,
    dense_bias,
    expand_weight,
    expand_bias,
    contract_weight,
    contract_bias,
    lengths,
    cotangent,
):
    blk, width = tokens.shape
    local = query_key_value.shape[2]
    hidden = expand_weight.shape[1]
    heads = local // HD
    total = 4 * blk
    bits = n.bit_length() - 1
    swaps = bits + 2
    parts = len(pieces(n, heads))
    cosine, sine = angle_rows(total)
    vmem = pl.BlockSpec(memory_space=pltpu.VMEM)
    smem = pl.BlockSpec(memory_space=pltpu.SMEM)
    hbm = pl.BlockSpec(memory_space=pl.ANY)
    dma = pltpu.SemaphoreType.DMA
    mixed, grad_tokens, res, vec = pl.pallas_call(
        functools.partial(core, n),
        name="core",
        out_shape=(
            jax.ShapeDtypeStruct((blk, width), BF16),
            jax.ShapeDtypeStruct((blk, width), F32),
            jax.ShapeDtypeStruct((3 * width, width), BF16),
            jax.ShapeDtypeStruct((8, width), F32),
        ),
        in_specs=[hbm, hbm, smem] + [vmem] * 7 + [hbm, vmem, hbm, hbm, hbm, vmem, vmem],
        out_specs=[vmem, vmem, hbm, vmem],
        scratch_shapes=[
            pltpu.VMEM((total, width), BF16),
            pltpu.VMEM((total, width), BF16),
            pltpu.VMEM((total, width), BF16),
            pltpu.VMEM((total, width), BF16),
            pltpu.VMEM((3 * local, width), BF16),
            pltpu.VMEM((local, width), BF16),
            pltpu.VMEM((width, hidden), BF16),
            pltpu.VMEM((hidden, width), BF16),
            pltpu.VMEM((3 * local, 1), F32),
            pltpu.VMEM((3 * width, width), F32),
            pltpu.VMEM((3 * width, width), BF16),
            pltpu.VMEM((6, blk, width), BF16),
            pltpu.VMEM((heads, 2 * HD, total), BF16),
            pltpu.VMEM((heads, HD, total), BF16),
            pltpu.VMEM((heads, total, 2 * HD), BF16),
            pltpu.VMEM((heads, HD + 16, total), BF16),
            pltpu.VMEM((heads, total, HD), BF16),
            pltpu.VMEM((heads, HD, total), BF16),
            pltpu.VMEM((8, total), F32),
            pltpu.VMEM((HD, total), F32),
            pltpu.VMEM((HD, total), F32),
            pltpu.VMEM((heads, HD, total), BF16),
            pltpu.VMEM((8, width), F32),
            pltpu.VMEM((swaps, 8, width), F32),
            pltpu.VMEM((3 * width, width), BF16),
            pltpu.VMEM((3 * width, width), BF16),
            dma((5 + 3 * heads,)),
            dma((6,)),
            dma((6,)),
            dma((3, 2)),
            dma((3, 2)),
            dma((2 * bits, parts)),
            dma((2 * bits, parts)),
            dma((swaps,)),
            dma((swaps,)),
            dma((1,)),
            pltpu.SemaphoreType.REGULAR((2,)),
        ],
        compiler_params=pltpu.CompilerParams(
            vmem_limit_bytes=63 * 2**20, collective_id=0, has_side_effects=True
        ),
    )(
        tokens,
        cotangent,
        lengths,
        input_gain,
        input_bias,
        post_gain,
        post_bias,
        expand_bias,
        dense_bias,
        contract_bias,
        jnp.transpose(query_key_value, (0, 2, 1)),
        query_key_value_bias,
        dense_weight,
        expand_weight,
        contract_weight,
        cosine,
        sine,
    )

    def whole(*shape):
        return pl.BlockSpec(shape, lambda g: (0,) * len(shape))

    vector = jax.ShapeDtypeStruct((width,), F32)
    outs = pl.pallas_call(
        finish,
        name="finish",
        grid=(3,),
        in_specs=[
            pl.BlockSpec((width, width), lambda g: (g, 0)),
            whole(blk, width),
            whole(blk, width),
            whole(8, width),
        ],
        out_specs=[whole(blk, width), whole(blk, width)]
        + [whole(width)] * 4
        + [
            whole(3, local, width),
            whole(3, local),
            whole(local, width),
            whole(width),
            whole(width, hidden),
            whole(hidden),
            whole(hidden, width),
            whole(width),
        ],
        out_shape=(
            jax.ShapeDtypeStruct((blk, width), BF16),
            jax.ShapeDtypeStruct((blk, width), F32),
            vector,
            vector,
            vector,
            vector,
            jax.ShapeDtypeStruct((3, local, width), F32),
            jax.ShapeDtypeStruct((3, local), F32),
            jax.ShapeDtypeStruct((local, width), F32),
            vector,
            jax.ShapeDtypeStruct((width, hidden), F32),
            jax.ShapeDtypeStruct((hidden,), F32),
            jax.ShapeDtypeStruct((hidden, width), F32),
            vector,
        ),
        compiler_params=pltpu.CompilerParams(vmem_limit_bytes=63 * 2**20),
    )(res, mixed, grad_tokens, vec)
    outs = list(outs)
    outs[6] = jnp.transpose(outs[6], (0, 2, 1))
    return tuple(outs)


def solution(mesh):
    rows = P(("dp", "tensor"), None)
    weights = (
        P(None, None, "tensor"),
        P(None, "tensor"),
        P("tensor", None),
        P(),
        P(None, "tensor"),
        P("tensor"),
        P("tensor", None),
        P(),
    )
    return jax.shard_map(
        functools.partial(shards, mesh.shape["dp"]),
        mesh=mesh,
        in_specs=(rows, P(), P(), P(), P()) + weights + (P("dp"), rows),
        out_specs=(rows, rows, P(), P(), P(), P()) + weights,
        check_vma=False,
    )
```

```python
import functools

import jax
import jax.numpy as jnp
import numpy as np
from jax import lax
from jax.experimental import pallas as pl
from jax.experimental.pallas import tpu as pltpu
from jax.sharding import PartitionSpec as P

HD = 64
ROT = 16
LEN = 2048
EPS = 1e-05
MASKED = -1e30
F32 = jnp.float32
BF16 = jnp.bfloat16


def dot(a, b, ca, cb):
    return lax.dot_general(a, b, (((ca,), (cb,)), ((), ())), preferred_element_type=F32)


def angle_rows(count):
    half = ROT // 2
    freqs = np.float32(10000.0) ** (
        np.float32(-2.0) * np.arange(half, dtype=np.float32) / np.float32(ROT)
    )
    place = (np.arange(count) % LEN).astype(np.float32)
    angle = (freqs[:, None] * place[None, :]).astype(np.float32)
    return np.cos(angle), np.sin(angle)


def unit_rows(rows):
    values = rows.astype(F32)
    centred = values - jnp.mean(values, -1, keepdims=True)
    inverse = lax.rsqrt(jnp.mean(centred * centred, -1, keepdims=True) + EPS)
    return centred * inverse, inverse

MESH = pl.DeviceIdType.MESH
SUB = 256
UNIT = 1.0
FRONT = 0.52


def flip(value, bits):
    bit = 1
    while bit <= bits:
        if (bits // bit) % 2:
            value = value + bit * (1 - 2 * ((value // bit) % 2))
        bit *= 2
    return value


def pieces(n, heads):
    bits = n.bit_length() - 1
    count = 6 + heads
    made = []
    base = 0
    for k in range(count):
        last = k == count - 1
        parts = 2 if last and n <= 16 else 1
        size = SUB // parts
        depth = max(bits - 2, 1) if last else bits - 1
        room = size - size // 2**depth + (bits - depth) * (size // 2**depth)
        for p in range(parts):
            made.append((SUB * k + size * p, size, depth, base, room))
            base += room
    return made


def trade_size(rows, depth, bits, step):
    if step < depth:
        return rows // 2 ** (step + 1)
    if step < bits:
        return rows // 2**depth
    return rows // 2 ** (depth - (step - bits))


def trade_bit(depth, bits, step):
    return step if step < bits else depth - (step - bits) - 1


def plan(bits, chunks, ready, points, width, margin=0.5, rate=0.045, delay=3.0, work=0.2):
    free = {}
    clock = points[0]
    reached = 0
    todo = [(when, k, 0) for k, when in enumerate(ready)]
    made = []
    while todo:
        todo.sort()
        when, k, step = todo.pop(0)
        later = [(at, u) for u, at in enumerate(points) if at >= when and u >= reached]
        if later:
            at, reached = later[0]
            clock = max(at, clock)
        else:
            reached = len(points)
            clock = max(when, clock, points[-1] + 1.5)
        clock += work
        made.append((clock, reached, k, step))
        _, rows, depth, _, _ = chunks[k]
        if step < bits + depth:
            cost = trade_size(rows, depth, bits, step) * width * 2e-6 / rate
            uses = {0: {"x": 1}, 1: {"end": 1}}.get(trade_bit(depth, bits, step), {"end": 1, "mid": 2})
            through = clock
            for link, share in uses.items():
                free[link] = max(free.get(link, points[0]), clock) + share * cost
                through = max(through, free[link])
            todo.append((through + delay + (margin if later else 0.0), k, step + 1))
    return made


def core(
    n,
    tok,
    cot,
    len_ref,
    gain1_r,
    bias1_r,
    gain2_r,
    bias2_r,
    exp_r,
    outb1_r,
    outb2_r,
    qkv,
    qkv_b,
    wd_h,
    we_h,
    wc_h,
    cos_t,
    sin_t,
    mixed_o,
    gtok_o,
    res_o,
    vec_o,
    x_s,
    g_s,
    n1_s,
    s_s,
    wt,
    wd,
    we,
    wc,
    qb_s,
    acc,
    res,
    hold,
    qa,
    kt,
    kr,
    va,
    vr,
    dot_s,
    lse,
    dkt,
    dvt,
    ctx_s,
    mixed_s,
    gtok_s,
    vec,
    vec_in,
    sx,
    rx,
    in_sem,
    ag_send,
    ag_recv,
    rs_send,
    rs_recv,
    ar_send,
    ar_recv,
    v_send,
    v_recv,
    out_sem,
    free_sem,
):
    blk, width = tok.shape
    total = x_s.shape[0]
    local = wd.shape[0]
    heads = local // HD
    count = total // blk
    per = LEN // blk
    root = HD**-0.5
    band = 4 * HD
    attn = 2 * width
    bits = n.bit_length() - 1
    dp = lax.axis_index("dp")
    t = lax.axis_index("tensor")
    core_bit = t % 2
    chip_bit = t // 2
    sib = (dp, flip(t, 1))
    across = (dp, flip(t, 2))
    peers = [(flip(dp, 2**q), t) for q in range(bits)]

    def send(src, dst, ssem, rsem, where):
        return pltpu.make_async_remote_copy(
            src_ref=src,
            dst_ref=dst,
            send_sem=ssem,
            recv_sem=rsem,
            device_id=where,
            device_id_type=MESH,
        )

    def block(b):
        return pl.ds(pl.multiple_of(b * blk, blk), blk)

    own = block(t)
    other = block(flip(t, 2))
    fetch = [
        pltpu.make_async_copy(tok, x_s.at[own], in_sem.at[0]),
        pltpu.make_async_copy(cot, g_s.at[own], in_sem.at[1]),
        pltpu.make_async_copy(we_h, we, in_sem.at[2]),
        pltpu.make_async_copy(wc_h, wc, in_sem.at[3]),
        pltpu.make_async_copy(wd_h, wd, in_sem.at[4]),
    ]
    for h in range(heads):
        for c in range(3):
            fetch.append(
                pltpu.make_async_copy(
                    qkv.at[c, h * HD : (h + 1) * HD, :],
                    wt.at[(3 * h + c) * HD : (3 * h + c + 1) * HD, :],
                    in_sem.at[5 + 3 * h + c],
                )
            )
    for copy in fetch:
        copy.start()

    barrier = pltpu.get_barrier_semaphore()
    greeted = [sib, across] + peers
    for who in greeted:
        pl.semaphore_signal(barrier, inc=1, device_id=who, device_id_type=MESH)
    pl.semaphore_wait(barrier, len(greeted))

    gather = [
        send(tok, x_s.at[own], ag_send.at[0], ag_recv.at[0], across),
        send(cot, g_s.at[own], ag_send.at[1], ag_recv.at[1], across),
        send(tok, x_s.at[own], ag_send.at[2], ag_recv.at[2], sib),
        send(cot, g_s.at[own], ag_send.at[3], ag_recv.at[3], sib),
        send(x_s.at[other], x_s.at[other], ag_send.at[4], ag_recv.at[4], sib),
        send(g_s.at[other], g_s.at[other], ag_send.at[5], ag_recv.at[5], sib),
    ]
    gather[0].start()
    gather[2].start()
    gather[3].start()

    gain1, bias1, gain2, bias2, exp_b = (
        r[...].reshape(1, width) for r in (gain1_r, bias1_r, gain2_r, bias2_r, exp_r)
    )
    for c in range(3):
        column = jnp.transpose(jnp.broadcast_to(qkv_b[c : c + 1, :], (8, local)))
        for h in range(heads):
            qb_s[(3 * h + c) * HD : (3 * h + c + 1) * HD, :] = column[h * HD : (h + 1) * HD, :1]
    for ref in (acc, vec):
        ref[...] = jnp.zeros_like(ref)
    one_row = (lax.broadcasted_iota(jnp.int32, (heads, HD, total), 1) == 0).astype(F32)
    qa[:, HD:, :] = one_row.astype(BF16)
    va[:, HD:, :] = one_row[:, : va.shape[1] - HD, :].astype(BF16)
    for copy in fetch:
        copy.wait()

    chunks = pieces(n, heads)

    def rows_of(k, first, size):
        step = min(chunks[k][1] // 2 ** chunks[k][2], 128)
        return pl.ds(pl.multiple_of(chunks[k][0] + first, step), size)

    def first_of(k, q):
        first = 0
        for p in range(q):
            first = first + ((dp // 2**p) % 2) * (chunks[k][1] // 2 ** (p + 1))
        return first

    def kept(k, q):
        return rows_of(k, first_of(k, q), chunks[k][1] // 2**q)

    def given(k, q):
        size = chunks[k][1] // 2**q
        bit = (dp // 2 ** (q - 1)) % 2
        return rows_of(k, first_of(k, q - 1) + (1 - bit) * size, size)

    def landing(k, step):
        _, rows, depth, base, _ = chunks[k]
        low = sum(trade_size(rows, depth, bits, p) for p in range(step))
        return pl.ds(base + low, trade_size(rows, depth, bits, step))

    def ar_copy(k, step):
        sems = (ar_send.at[step, k], ar_recv.at[step, k])
        depth = chunks[k][2]
        who = peers[trade_bit(depth, bits, step)]
        if step < bits:
            return send(sx.at[landing(k, step)], rx.at[landing(k, step)], *sems, who)
        piece = res.at[kept(k, depth - (step - bits))]
        return send(piece, piece, *sems, who)

    def chunk_out(k):
        rows = kept(k, 0)
        return pltpu.make_async_copy(res.at[rows], res_o.at[rows], out_sem.at[2 + k])

    def advance(k, step):
        depth = chunks[k][2]
        if step > 0:
            ar_copy(k, step - 1).wait()
        if 1 <= step <= bits:
            mine = kept(k, min(step, depth))
            had = acc[mine, :] if step <= depth else sx[landing(k, step - 1), :].astype(F32)
            done = had + rx[landing(k, step - 1), :].astype(F32)
            if step < bits:
                acc[mine, :] = done
            else:
                res[mine, :] = done.astype(BF16)
        if step < bits:
            gone = given(k, step + 1) if step < depth else kept(k, depth)
            sx[landing(k, step), :] = acc[gone, :].astype(BF16)
        if step < bits + depth:
            ar_copy(k, step).start()
        else:
            chunk_out(k).start()

    first_it = 9
    points = [-11.8, -9.9, -8.0]
    lead = len(points)
    points += [-7.8 + FRONT * (u + 1) for u in range(heads * count)]
    mid = len(points)
    ends = []
    clock = 0.0
    for h in range(heads):
        for i in range(count - 1, -1, -1):
            for _ in range(i + 1):
                clock += UNIT
                points.append(clock)
            clock += 0.7
        ends.append(clock)
    last_time = clock
    ready = [points[0]] * 3 + [points[2]] * 3 + ends
    ready += [last_time] * (len(chunks) - len(ready))
    ticks = {}
    after = []
    for when, u, k, step in plan(bits, chunks, ready, points, width):
        if u < len(points):
            ticks.setdefault(u, []).append(functools.partial(advance, k, step))
        else:
            after.append((when, functools.partial(advance, k, step)))

    def forward(b, slot, before_mix):
        rows = block(b)
        unit, _ = unit_rows(x_s[rows, :])
        n1 = (unit * gain1 + bias1).astype(BF16)
        n2 = (unit * gain2 + bias2).astype(BF16)
        n1_s[rows, :] = n1
        hold[2 + slot] = n2
        pre = dot(n2, we[...], 1, 0) + exp_b
        big = 0.5 * (1.0 + lax.erf(pre * np.float32(0.5**0.5)))
        act = (pre * big).astype(BF16)
        slope = big + pre * (jnp.exp(-0.5 * pre * pre) * np.float32((2 * np.pi) ** -0.5))
        hold[slot] = act
        hold[4 + slot] = slope.astype(BF16)
        mix = dot(act, wc[...], 1, 0).astype(BF16)
        before_mix()
        x_s[rows, :] = mix
        proj = dot(wt[...], n1, 1, 1) + qb_s[...]
        cosine = cos_t[:, rows]
        sine = sin_t[:, rows]

        def turn(rows_in):
            a = rows_in[: ROT // 2]
            c = rows_in[ROT // 2 : ROT]
            return jnp.concatenate(
                [a * cosine - c * sine, c * cosine + a * sine, rows_in[ROT:]], 0
            )

        place = lax.broadcasted_iota(jnp.int32, (HD, blk), 1) + (b % per) * blk
        first = lax.broadcasted_iota(jnp.int32, (HD, blk), 0) == 0
        extra = jnp.where(first & (place >= len_ref[0]), MASKED, 0.0)
        for h in range(heads):
            lo = 3 * h * HD
            q = turn(proj[lo : lo + HD])
            k = turn(proj[lo + HD : lo + 2 * HD])
            v = proj[lo + 2 * HD : lo + 3 * HD]
            qa[h, :HD, rows] = (q * root).astype(BF16)
            kt[h, :, rows] = k.astype(BF16)
            kr[h, rows, :] = jnp.transpose(jnp.concatenate([k, extra], 0)).astype(BF16)
            va[h, :HD, rows] = v.astype(BF16)
            vr[h, rows, :] = jnp.transpose(v).astype(BF16)

    def mate(k):
        low = (t + k) % 2
        high = (t // 2 + k // 2) % 2
        return low + 2 * high

    key_i = lax.broadcasted_iota(jnp.int32, (blk, blk), 0)
    query_i = lax.broadcasted_iota(jnp.int32, (blk, blk), 1)

    def serve(unit, low, high):
        for u, jobs in ticks.items():
            if low <= u < high:

                @pl.when(unit == u)
                def _(jobs=jobs):
                    for job in jobs:
                        job()

    def front(i):
        passed = jnp.where(i == count - 1, lead, -mid)
        base = (i // per) * per
        mine = block(i)

        def head(h, _):
            q_aug = qa[h, :, mine]

            def weigh(j, scores, high, out):
                top = jnp.max(jnp.max(scores.reshape(blk // 8, 8, blk), 0), 0, keepdims=True)
                top = jnp.maximum(high, top)
                p = jnp.exp(scores - top).astype(BF16)
                return top, out * jnp.exp(high - top) + dot(va[h, :, block(j)], p, 1, 0)

            def onward(j, carry):
                more = weigh(j, dot(kr[h, block(j), :], q_aug, 1, 0), *carry)
                serve(passed + h * count + (j - base), lead, mid)
                return more

            begin = (jnp.full((1, blk), MASKED, F32), jnp.zeros((va.shape[1], blk), F32))
            carry = lax.fori_loop(base, i, onward, begin)
            scores = dot(kr[h, mine, :], q_aug, 1, 0)
            high, out = weigh(i, jnp.where(key_i <= query_i, scores, MASKED), *carry)
            norm = out[HD : HD + 1]
            ctx_s[h, :, mine] = (out[:HD] * (1.0 / norm)).astype(BF16)
            lse[pl.ds(h, 1), mine] = high + jnp.log(norm)
            serve(passed + h * count + (i - base), lead, mid)
            return 0

        lax.fori_loop(0, heads, head, 0)
        ctx = ctx_s[:, :, mine].reshape(local, blk)
        mix = dot(ctx, wd[...], 0, 0) + x_s[mine, :].astype(F32)
        x_s[mine, :] = mix.astype(BF16)

    def feed_part(rows):
        part = dot(s_s[rows, :], we[...], 1, 1)
        vec[2:3, :] += jnp.sum(part * n1_s[rows, :].astype(F32), 0, keepdims=True)
        vec[3:4, :] += jnp.sum(part, 0, keepdims=True)
        return part * gain2

    def phase(it, _):
        late = it // 7 > 0
        b = mate(jnp.where(late, 2 + (it + 1) % 2, it % 4))
        slot = jnp.where(late, (it + 1) % 2, (it % 4) // 3)
        rows = block(b)

        @pl.when(it == 1)
        def _():
            gather[2].wait_recv()
            gather[3].wait_recv()

        @pl.when(it == 2)
        def _():
            gather[0].wait_send()
            gather[1].start()
            gather[0].wait_recv()
            gather[4].start()

        @pl.when(it == 3)
        def _():
            gather[4].wait_recv()

        @pl.when(it < 4)
        def _():
            def settle():
                @pl.when(it == 2)
                def _():
                    gather[4].wait_send()

            forward(b, slot, settle)

        @pl.when(((it > 3) & (it < 7)) | (it == 11))
        def _():
            front(jnp.where(late, count - 1, it - 4))

        @pl.when(it == 7)
        def _():
            gather[1].wait_recv()
            gather[5].start()

        @pl.when(it == 8)
        def _():
            gather[5].wait_recv()

        serve(it - first_it, 0, lead)

        @pl.when((it < 2) | (it == 7) | (it == 8))
        def _():
            acc[:width] += dot(hold[slot], g_s[rows, :], 0, 0)

        @pl.when((it < 2) | (it == 9) | (it == 10))
        def _():
            slope = hold[4 + slot].astype(F32)
            grad_pre = (dot(g_s[rows, :], wc[...], 1, 1) * slope).astype(BF16)
            s_s[rows, :] = grad_pre
            vec[5:6, :] += jnp.sum(grad_pre.astype(F32), 0, keepdims=True)
            acc[width : 2 * width] += dot(hold[2 + slot], grad_pre, 0, 0)
            grad_ctx = dot(wd[...], g_s[rows, :], 1, 1).astype(BF16)
            for h in range(heads):
                dot_s[h, :, rows] = grad_ctx[h * HD : (h + 1) * HD]

        @pl.when(it < 2)
        def _():
            s_s[rows, :] = feed_part(rows).astype(BF16)

        return 0

    lax.fori_loop(0, 12, phase, 0)
    for k in (1, 2, 3, 5):
        gather[k].wait_send()
    pl.semaphore_signal(free_sem.at[0], inc=1, device_id=sib, device_id_type=MESH)
    pl.semaphore_signal(free_sem.at[1], inc=1, device_id=across, device_id_type=MESH)

    def dense_grad(i, _):
        grad_d = dot(ctx_s[:, :, block(i)].reshape(local, blk), g_s[block(i), :], 1, 0)
        for h in range(heads):
            at = attn + h * band + 3 * HD
            acc[at : at + HD, :] += grad_d[h * HD : (h + 1) * HD]
        return 0

    lax.fori_loop(0, count, dense_grad, 0)

    sums = (x_s, s_s)

    def to_sib(i, w):
        slot = i // 2
        src = sums[w].at[block(i)]
        return send(src, hold.at[2 * slot + w], rs_send.at[slot, w], rs_recv.at[slot, w], sib)

    def to_owner(i, w):
        src = sums[w].at[block(i)]
        return send(src, hold.at[4 + w], rs_send.at[2, w], rs_recv.at[2, w], across)

    def hand_over(i, w):
        @pl.when(core_bit != i % 2)
        def _():
            to_sib(i, w).start()

    def pass_on(i, w):
        @pl.when(core_bit == i % 2)
        def _():
            to_sib(i, w).wait_recv()

        @pl.when((core_bit == i % 2) & (chip_bit != i // 2))
        def _():
            rows = block(i)
            both = sums[w][rows, :].astype(F32) + hold[2 * (i // 2) + w].astype(F32)
            sums[w][rows, :] = both.astype(BF16)
            to_owner(i, w).start()

    def mixes_over():
        pl.semaphore_wait(free_sem.at[0], 1)
        pl.semaphore_wait(free_sem.at[1], 1)

        def one(i, _):
            hand_over(i, 0)
            return 0

        lax.fori_loop(0, count, one, 0)

    def mixes_on():
        def one(i, _):
            pass_on(i, 0)
            return 0

        lax.fori_loop(0, count, one, 0)

    ticks.setdefault(mid + 3, []).insert(0, mixes_over)
    ticks.setdefault(mid + 7, []).insert(0, mixes_on)

    def attend(visit, _):
        h = visit // count
        i = count - 1 - visit % count
        base = (i // per) * per
        mine = block(i)
        passed = h * (count * (count + 1) // 2) + mid
        passed += count * (count - 1 - i) - ((count - 1 - i) * (count - 2 - i)) // 2

        @pl.when(i == count - 1)
        def _():
            dkt[...] = jnp.zeros_like(dkt)
            dvt[...] = jnp.zeros_like(dvt)

        q_aug = qa[h, :, mine]
        q = q_aug[:HD]
        go = dot_s[h, :, mine]
        total_log = lse[pl.ds(h, 1), mine]
        inner = jnp.sum(ctx_s[h, :, mine].astype(F32) * go.astype(F32), 0, keepdims=True)

        def back(j, scores):
            cols = block(j)
            p = jnp.exp(scores - total_log)
            dvt[:, cols] += dot(go, p.astype(BF16), 1, 1)
            dp_t = dot(vr[h, cols, :], go, 1, 0)
            ds = (p * (dp_t - inner)).astype(BF16)
            dkt[:, cols] += dot(q, ds, 1, 1)
            return dot(kt[h, :, cols], ds, 1, 0)

        def onward(j, dq):
            more = back(j, dot(kr[h, block(j), :], q_aug, 1, 0))
            serve(passed + (j - base), mid, len(points))
            return dq + more

        dq = lax.fori_loop(base, i, onward, jnp.zeros((HD, blk), F32))
        scores = dot(kr[h, mine, :], q_aug, 1, 0)
        dq += back(i, jnp.where(key_i <= query_i, scores, MASKED))
        serve(passed + (i - base), mid, len(points))
        cosine = cos_t[:, mine]
        sine = sin_t[:, mine]

        def unturn(rows_in):
            a = rows_in[: ROT // 2]
            c = rows_in[ROT // 2 : ROT]
            return jnp.concatenate(
                [a * cosine + c * sine, c * cosine - a * sine, rows_in[ROT:]], 0
            )

        qa[h, :HD, mine] = unturn(dq * root).astype(BF16)
        kt[h, :, mine] = unturn(dkt[:, mine]).astype(BF16)
        va[h, :HD, mine] = dvt[:, mine].astype(BF16)
        grad_proj = jnp.concatenate([qa[h, :HD, mine], kt[h, :, mine], va[h, :HD, mine]], 0)
        at = attn + h * band
        acc[pl.ds(pl.multiple_of(at, HD), 3 * HD), :] += dot(grad_proj, n1_s[mine, :], 1, 0)

        @pl.when(i == 0)
        def _():
            w32 = wt[pl.ds(pl.multiple_of(3 * h * HD, HD), 3 * HD), :].astype(F32)
            grads = acc[pl.ds(pl.multiple_of(at, HD), 3 * HD), :]
            vec[0:1, :] += jnp.sum(w32 * grads, 0, keepdims=True)

        return 0

    lax.fori_loop(0, heads * count, attend, 0)

    def token_grads(r):
        i = mate(r)
        mine = block(i)
        parts = [(qa[h, :HD, mine], kt[h, :, mine], va[h, :HD, mine]) for h in range(heads)]
        every = jnp.concatenate([x for three in parts for x in three], 0)
        fed = s_s[mine, :].astype(F32) if r < 2 else feed_part(mine)
        s_s[mine, :] = (dot(every, wt[...], 0, 0) * gain1 + fed).astype(BF16)
        hand_over(i, 1)
        ones = jnp.ones((8, blk), BF16)
        vec[6:7, : 3 * local] += dot(ones, every, 1, 1)[:1]

    again = pltpu.make_async_copy(tok, n1_s.at[own], in_sem.at[0])

    swaps = peers + [sib, across]
    inside = len(peers)

    def swap(q):
        return send(vec, vec_in.at[q], v_send.at[q], v_recv.at[q], swaps[q])

    shared = lax.broadcasted_iota(jnp.int32, vec.shape, 0) < 5

    def finish_swap(q):
        swap(q).wait()
        extra = vec_in[q]
        if q >= inside:
            extra = jnp.where(shared, extra, 0.0)
        vec[...] += extra

    def vectors():
        w32 = wt[...].astype(F32)
        column = jnp.transpose(jnp.broadcast_to(vec[6:7, : 3 * local], (8, 3 * local)))[:, :1]
        grad_bias = jnp.sum(w32 * column, 0, keepdims=True)
        vec[1:2, :] = grad_bias
        vec[0:1, :] = (vec[0:1, :] - bias1 * grad_bias) / gain1
        vec[2:3, :] = (vec[2:3, :] - bias1 * vec[3:4, :]) / gain1
        vec[4:5, :] = jnp.sum(g_s[own, :].astype(F32), 0, keepdims=True)
        again.start()

    out_copies = [
        pltpu.make_async_copy(mixed_s, mixed_o, out_sem.at[0]),
        pltpu.make_async_copy(gtok_s, gtok_o, out_sem.at[1]),
    ]

    def tokens_out():
        to_sib(t, 1).wait_recv()
        for w in range(2):
            to_owner(flip(t, 2), w).wait()
        again.wait()
        rows = n1_s[own, :]
        mix = rows.astype(F32) + (outb1_r[...] + outb2_r[...]).reshape(1, width)
        mix += x_s[own, :].astype(F32)
        s = s_s[own, :].astype(F32)
        for w in (2 * chip_bit, 4):
            mix += hold[w].astype(F32)
            s += hold[w + 1].astype(F32)
        mixed_s[...] = mix.astype(BF16)
        unit, inverse = unit_rows(rows)
        gtok_s[...] = g_s[own, :].astype(F32) + inverse * (
            s - jnp.mean(s, -1, keepdims=True) - unit * jnp.mean(s * unit, -1, keepdims=True)
        )
        for copy in out_copies:
            copy.start()

    jobs = list(after)
    jobs.append((last_time + 1.7, functools.partial(token_grads, 3)))
    jobs.append((last_time + 3.7, functools.partial(token_grads, 2)))
    jobs.append((last_time + 5.7, functools.partial(token_grads, 1)))
    jobs.append((last_time + 6.8, lambda: pass_on(mate(2), 1)))
    jobs.append((last_time + 7.3, functools.partial(token_grads, 0)))
    jobs.append((last_time + 8.5, vectors))
    for q in range(len(swaps)):

        def trade(q=q):
            if q > 0:
                finish_swap(q - 1)
            swap(q).start()

        jobs.append((last_time + 9.5 + 3.2 * q, trade))
    jobs.append((last_time + 9.5 + 3.2 * len(swaps), lambda: finish_swap(len(swaps) - 1)))
    jobs.append((last_time + 27.0, tokens_out))
    for _, job in sorted(jobs, key=lambda pair: pair[0]):
        job()
    vec_o[...] = vec[...]
    for i in range(count):

        @pl.when(core_bit != i % 2)
        def _(i=i):
            for w in range(2):
                to_sib(i, w).wait_send()

    for copy in out_copies:
        copy.wait()
    for k in range(len(chunks)):
        chunk_out(k).wait()


def finish(res, mixed, gtok, vec, *refs):
    outs, (low, high, mid_m, mid_g, moved, in_sem, out_sem) = refs[:14], refs[14:]
    mixed_o, gtok_o, gain1_o, bias1_o, gain2_o, bias2_o, qkv_o, qkvb_o, wd_o, db_o, we_o, be_o, wc_o, cb_o = outs
    width = res.shape[1]
    heads = wd_o.shape[0] // HD
    count = low.shape[0] // SUB
    passing = [
        pltpu.make_async_copy(mixed, mid_m, moved.at[0]),
        pltpu.make_async_copy(gtok, mid_g, moved.at[1]),
    ]
    leaving = [
        pltpu.make_async_copy(mid_m, mixed_o, moved.at[2]),
        pltpu.make_async_copy(mid_g, gtok_o, moved.at[3]),
    ]

    def rows(k):
        return pl.ds(k * SUB, SUB)

    comes = [pltpu.make_async_copy(res.at[rows(k)], low.at[rows(k)], in_sem.at[k]) for k in range(count)]
    goes = []
    for k in range(6):
        where = (wc_o, we_o)[k // 3].at[rows(k % 3)]
        goes.append([pltpu.make_async_copy(high.at[rows(k)], where, out_sem.at[k])])
    for h in range(heads):
        first = (6 + h) * SUB
        places = [qkv_o.at[c, h * HD : (h + 1) * HD, :] for c in range(3)] + [wd_o.at[h * HD : (h + 1) * HD]]
        goes.append(
            [
                pltpu.make_async_copy(
                    high.at[pl.ds(first + c * HD, HD)], place, out_sem.at[6 + 4 * h + c]
                )
                for c, place in enumerate(places)
            ]
        )
    for copy in passing + comes:
        copy.start()
    for ref, row in (
        (gain1_o, 0),
        (bias1_o, 1),
        (gain2_o, 2),
        (bias2_o, 3),
        (db_o, 4),
        (cb_o, 4),
        (be_o, 5),
    ):
        ref[...] = vec[row, :]
    for h in range(heads):
        for c in range(3):
            lo = (3 * h + c) * HD
            qkvb_o[c : c + 1, h * HD : (h + 1) * HD] = vec[6:7, lo : lo + HD]
    for k in range(count):
        comes[k].wait()
        high[rows(k), :] = low[rows(k), :].astype(F32)
        for copy in goes[k]:
            copy.start()
        if k == 0:
            for come, go in zip(passing, leaving):
                come.wait()
                go.start()
    for copy in [x for some in goes for x in some] + leaving:
        copy.wait()


def shards(
    n,
    tokens,
    input_gain,
    input_bias,
    post_gain,
    post_bias,
    query_key_value,
    query_key_value_bias,
    dense_weight,
    dense_bias,
    expand_weight,
    expand_bias,
    contract_weight,
    contract_bias,
    lengths,
    cotangent,
):
    blk, width = tokens.shape
    local = query_key_value.shape[2]
    hidden = expand_weight.shape[1]
    heads = local // HD
    total = 4 * blk
    bits = n.bit_length() - 1
    swaps = bits + 2
    parts = len(pieces(n, heads))
    room = sum(chunk[4] for chunk in pieces(n, heads))
    cosine, sine = angle_rows(total)
    vmem = pl.BlockSpec(memory_space=pltpu.VMEM)
    smem = pl.BlockSpec(memory_space=pltpu.SMEM)
    hbm = pl.BlockSpec(memory_space=pl.ANY)
    dma = pltpu.SemaphoreType.DMA
    mixed, grad_tokens, res, vec = pl.pallas_call(
        functools.partial(core, n),
        name="core",
        out_shape=(
            jax.ShapeDtypeStruct((blk, width), BF16),
            jax.ShapeDtypeStruct((blk, width), F32),
            jax.ShapeDtypeStruct((3 * width, width), BF16),
            jax.ShapeDtypeStruct((8, width), F32),
        ),
        in_specs=[hbm, hbm, smem] + [vmem] * 7 + [hbm, vmem, hbm, hbm, hbm, vmem, vmem],
        out_specs=[hbm, hbm, hbm, vmem],
        scratch_shapes=[
            pltpu.VMEM((total, width), BF16),
            pltpu.VMEM((total, width), BF16),
            pltpu.VMEM((total, width), BF16),
            pltpu.VMEM((total, width), BF16),
            pltpu.VMEM((3 * local, width), BF16),
            pltpu.VMEM((local, width), BF16),
            pltpu.VMEM((width, hidden), BF16),
            pltpu.VMEM((hidden, width), BF16),
            pltpu.VMEM((3 * local, 1), F32),
            pltpu.VMEM((3 * width, width), F32),
            pltpu.VMEM((3 * width, width), BF16),
            pltpu.VMEM((6, blk, width), BF16),
            pltpu.VMEM((heads, 2 * HD, total), BF16),
            pltpu.VMEM((heads, HD, total), BF16),
            pltpu.VMEM((heads, total, 2 * HD), BF16),
            pltpu.VMEM((heads, HD + 16, total), BF16),
            pltpu.VMEM((heads, total, HD), BF16),
            pltpu.VMEM((heads, HD, total), BF16),
            pltpu.VMEM((8, total), F32),
            pltpu.VMEM((HD, total), F32),
            pltpu.VMEM((HD, total), F32),
            pltpu.VMEM((heads, HD, total), BF16),
            pltpu.VMEM((blk, width), BF16),
            pltpu.VMEM((blk, width), F32),
            pltpu.VMEM((8, width), F32),
            pltpu.VMEM((swaps, 8, width), F32),
            pltpu.VMEM((room, width), BF16),
            pltpu.VMEM((room, width), BF16),
            dma((5 + 3 * heads,)),
            dma((6,)),
            dma((6,)),
            dma((3, 2)),
            dma((3, 2)),
            dma((2 * bits, parts)),
            dma((2 * bits, parts)),
            dma((swaps,)),
            dma((swaps,)),
            dma((2 + parts,)),
            pltpu.SemaphoreType.REGULAR((2,)),
        ],
        compiler_params=pltpu.CompilerParams(
            vmem_limit_bytes=63 * 2**20, collective_id=0, has_side_effects=True
        ),
    )(
        tokens,
        cotangent,
        lengths,
        input_gain,
        input_bias,
        post_gain,
        post_bias,
        expand_bias,
        dense_bias,
        contract_bias,
        jnp.transpose(query_key_value, (0, 2, 1)),
        query_key_value_bias,
        dense_weight,
        expand_weight,
        contract_weight,
        cosine,
        sine,
    )

    vector = jax.ShapeDtypeStruct((width,), F32)
    outs = pl.pallas_call(
        finish,
        name="finish",
        in_specs=[hbm, hbm, hbm, vmem],
        out_specs=[hbm, hbm] + [vmem] * 4 + [hbm, vmem, hbm, vmem, hbm, vmem, hbm, vmem],
        scratch_shapes=[
            pltpu.VMEM((3 * width, width), BF16),
            pltpu.VMEM((3 * width, width), F32),
            pltpu.VMEM((blk, width), BF16),
            pltpu.VMEM((blk, width), F32),
            dma((4,)),
            dma((9,)),
            dma((6 + 4 * heads,)),
        ],
        out_shape=(
            jax.ShapeDtypeStruct((blk, width), BF16),
            jax.ShapeDtypeStruct((blk, width), F32),
            vector,
            vector,
            vector,
            vector,
            jax.ShapeDtypeStruct((3, local, width), F32),
            jax.ShapeDtypeStruct((3, local), F32),
            jax.ShapeDtypeStruct((local, width), F32),
            vector,
            jax.ShapeDtypeStruct((width, hidden), F32),
            jax.ShapeDtypeStruct((hidden,), F32),
            jax.ShapeDtypeStruct((hidden, width), F32),
            vector,
        ),
        compiler_params=pltpu.CompilerParams(vmem_limit_bytes=63 * 2**20),
    )(res, mixed, grad_tokens, vec)
    outs = list(outs)
    outs[6] = jnp.transpose(outs[6], (0, 2, 1))
    return tuple(outs)


def solution(mesh):
    rows = P(("dp", "tensor"), None)
    weights = (
        P(None, None, "tensor"),
        P(None, "tensor"),
        P("tensor", None),
        P(),
        P(None, "tensor"),
        P("tensor"),
        P("tensor", None),
        P(),
    )
    return jax.shard_map(
        functools.partial(shards, mesh.shape["dp"]),
        mesh=mesh,
        in_specs=(rows, P(), P(), P(), P()) + weights + (P("dp"), rows),
        out_specs=(rows, rows, P(), P(), P(), P()) + weights,
        check_vma=False,
    )
```

```python
import functools

import jax
import jax.numpy as jnp
import numpy as np
from jax import lax
from jax.experimental import pallas as pl
from jax.experimental.pallas import tpu as pltpu
from jax.sharding import PartitionSpec as P

HD = 64
ROT = 16
LEN = 2048
EPS = 1e-05
MASKED = -1e30
F32 = jnp.float32
BF16 = jnp.bfloat16


def dot(a, b, ca, cb):
    return lax.dot_general(a, b, (((ca,), (cb,)), ((), ())), preferred_element_type=F32)


def angle_rows(count):
    half = ROT // 2
    freqs = np.float32(10000.0) ** (
        np.float32(-2.0) * np.arange(half, dtype=np.float32) / np.float32(ROT)
    )
    place = (np.arange(count) % LEN).astype(np.float32)
    angle = (freqs[:, None] * place[None, :]).astype(np.float32)
    return np.cos(angle), np.sin(angle)


def unit_rows(rows):
    values = rows.astype(F32)
    centred = values - jnp.mean(values, -1, keepdims=True)
    inverse = lax.rsqrt(jnp.mean(centred * centred, -1, keepdims=True) + EPS)
    return centred * inverse, inverse

MESH = pl.DeviceIdType.MESH
SUB = 256
UNIT = 1.0
FRONT = 0.52


def flip(value, bits):
    bit = 1
    while bit <= bits:
        if (bits // bit) % 2:
            value = value + bit * (1 - 2 * ((value // bit) % 2))
        bit *= 2
    return value


def pieces(n, heads):
    bits = n.bit_length() - 1
    count = 6 + heads
    made = []
    base = 0
    for k in range(count):
        last = k == count - 1
        parts = 2 if last and n <= 16 else 1
        size = SUB // parts
        depth = max(bits - 2, 1) if last else bits - 1
        room = size - size // 2**depth + (bits - depth) * (size // 2**depth)
        for p in range(parts):
            made.append((SUB * k + size * p, size, depth, base, room))
            base += room
    return made


def trade_size(rows, depth, bits, step):
    if step < depth:
        return rows // 2 ** (step + 1)
    if step < bits:
        return rows // 2**depth
    return rows // 2 ** (depth - (step - bits))


def trade_bit(depth, bits, step):
    return step if step < bits else depth - (step - bits) - 1


def plan(bits, chunks, ready, points, width, margin=0.3, rate=0.043, delay=2.2, work=0.2):
    free = {}
    clock = points[0]
    reached = 0
    todo = [(when, k, 0) for k, when in enumerate(ready)]
    made = []
    while todo:
        todo.sort()
        when, k, step = todo.pop(0)
        later = [(at, u) for u, at in enumerate(points) if at >= when and u >= reached]
        if later:
            at, reached = later[0]
            clock = max(at, clock)
        else:
            reached = len(points)
            clock = max(when, clock, points[-1] + 1.5)
        clock += work
        made.append((clock, reached, k, step))
        _, rows, depth, _, _ = chunks[k]
        if step < bits + depth:
            cost = trade_size(rows, depth, bits, step) * width * 2e-6 / rate
            uses = {0: {"x": 1}, 1: {"end": 1}}.get(trade_bit(depth, bits, step), {"end": 1, "mid": 2})
            through = clock
            for link, share in uses.items():
                free[link] = max(free.get(link, points[0]), clock) + share * cost
                through = max(through, free[link])
            todo.append((through + delay + (margin if later else 0.0), k, step + 1))
    return made


def core(
    n,
    tok,
    cot,
    len_ref,
    gain1_r,
    bias1_r,
    gain2_r,
    bias2_r,
    exp_r,
    outb1_r,
    outb2_r,
    qkv,
    qkv_b,
    wd_h,
    we_h,
    wc_h,
    cos_t,
    sin_t,
    mixed_o,
    gtok_o,
    res_o,
    vec_o,
    x_s,
    g_s,
    n1_s,
    s_s,
    wt,
    wd,
    we,
    wc,
    qb_s,
    acc,
    res,
    hold,
    qa,
    kt,
    kr,
    va,
    vr,
    dot_s,
    lse,
    dkt,
    dvt,
    ctx_s,
    mixed_s,
    gtok_s,
    vec,
    vec_in,
    sx,
    rx,
    in_sem,
    ag_send,
    ag_recv,
    rs_send,
    rs_recv,
    ar_send,
    ar_recv,
    v_send,
    v_recv,
    out_sem,
    free_sem,
):
    blk, width = tok.shape
    total = x_s.shape[0]
    local = wd.shape[0]
    heads = local // HD
    count = total // blk
    per = LEN // blk
    root = HD**-0.5
    band = 4 * HD
    attn = 2 * width
    bits = n.bit_length() - 1
    dp = lax.axis_index("dp")
    t = lax.axis_index("tensor")
    core_bit = t % 2
    chip_bit = t // 2
    sib = (dp, flip(t, 1))
    across = (dp, flip(t, 2))
    peers = [(flip(dp, 2**q), t) for q in range(bits)]

    def send(src, dst, ssem, rsem, where):
        return pltpu.make_async_remote_copy(
            src_ref=src,
            dst_ref=dst,
            send_sem=ssem,
            recv_sem=rsem,
            device_id=where,
            device_id_type=MESH,
        )

    def block(b):
        return pl.ds(pl.multiple_of(b * blk, blk), blk)

    own = block(t)
    other = block(flip(t, 2))
    fetch = [
        pltpu.make_async_copy(tok, x_s.at[own], in_sem.at[0]),
        pltpu.make_async_copy(cot, g_s.at[own], in_sem.at[1]),
        pltpu.make_async_copy(we_h, we, in_sem.at[2]),
        pltpu.make_async_copy(wc_h, wc, in_sem.at[3]),
        pltpu.make_async_copy(wd_h, wd, in_sem.at[4]),
    ]
    for h in range(heads):
        for c in range(3):
            fetch.append(
                pltpu.make_async_copy(
                    qkv.at[c, h * HD : (h + 1) * HD, :],
                    wt.at[(3 * h + c) * HD : (3 * h + c + 1) * HD, :],
                    in_sem.at[5 + 3 * h + c],
                )
            )
    for copy in fetch:
        copy.start()

    barrier = pltpu.get_barrier_semaphore()
    greeted = [sib, across] + peers
    for who in greeted:
        pl.semaphore_signal(barrier, inc=1, device_id=who, device_id_type=MESH)
    pl.semaphore_wait(barrier, len(greeted))

    gather = [
        send(tok, x_s.at[own], ag_send.at[0], ag_recv.at[0], across),
        send(cot, g_s.at[own], ag_send.at[1], ag_recv.at[1], across),
        send(tok, x_s.at[own], ag_send.at[2], ag_recv.at[2], sib),
        send(cot, g_s.at[own], ag_send.at[3], ag_recv.at[3], sib),
        send(x_s.at[other], x_s.at[other], ag_send.at[4], ag_recv.at[4], sib),
        send(g_s.at[other], g_s.at[other], ag_send.at[5], ag_recv.at[5], sib),
    ]
    gather[0].start()
    gather[2].start()
    gather[3].start()

    gain1, bias1, gain2, bias2, exp_b = (
        r[...].reshape(1, width) for r in (gain1_r, bias1_r, gain2_r, bias2_r, exp_r)
    )
    for c in range(3):
        column = jnp.transpose(jnp.broadcast_to(qkv_b[c : c + 1, :], (8, local)))
        for h in range(heads):
            qb_s[(3 * h + c) * HD : (3 * h + c + 1) * HD, :] = column[h * HD : (h + 1) * HD, :1]
    for ref in (acc, vec):
        ref[...] = jnp.zeros_like(ref)
    one_row = (lax.broadcasted_iota(jnp.int32, (heads, HD, total), 1) == 0).astype(F32)
    qa[:, HD:, :] = one_row.astype(BF16)
    va[:, HD:, :] = one_row[:, : va.shape[1] - HD, :].astype(BF16)
    for copy in fetch:
        copy.wait()

    chunks = pieces(n, heads)

    def rows_of(k, first, size):
        step = min(chunks[k][1] // 2 ** chunks[k][2], 128)
        return pl.ds(pl.multiple_of(chunks[k][0] + first, step), size)

    def first_of(k, q):
        first = 0
        for p in range(q):
            first = first + ((dp // 2**p) % 2) * (chunks[k][1] // 2 ** (p + 1))
        return first

    def kept(k, q):
        return rows_of(k, first_of(k, q), chunks[k][1] // 2**q)

    def given(k, q):
        size = chunks[k][1] // 2**q
        bit = (dp // 2 ** (q - 1)) % 2
        return rows_of(k, first_of(k, q - 1) + (1 - bit) * size, size)

    def landing(k, step):
        _, rows, depth, base, _ = chunks[k]
        low = sum(trade_size(rows, depth, bits, p) for p in range(step))
        return pl.ds(base + low, trade_size(rows, depth, bits, step))

    def ar_copy(k, step):
        sems = (ar_send.at[step, k], ar_recv.at[step, k])
        depth = chunks[k][2]
        who = peers[trade_bit(depth, bits, step)]
        if step < bits:
            return send(sx.at[landing(k, step)], rx.at[landing(k, step)], *sems, who)
        piece = res.at[kept(k, depth - (step - bits))]
        return send(piece, piece, *sems, who)

    def chunk_out(k):
        rows = kept(k, 0)
        return pltpu.make_async_copy(res.at[rows], res_o.at[rows], out_sem.at[2 + k])

    def advance(k, step):
        depth = chunks[k][2]
        if step > 0:
            ar_copy(k, step - 1).wait()
        if 1 <= step <= bits:
            mine = kept(k, min(step, depth))
            had = acc[mine, :] if step <= depth else sx[landing(k, step - 1), :].astype(F32)
            done = had + rx[landing(k, step - 1), :].astype(F32)
            if step < bits:
                acc[mine, :] = done
            else:
                res[mine, :] = done.astype(BF16)
        if step < bits:
            gone = given(k, step + 1) if step < depth else kept(k, depth)
            sx[landing(k, step), :] = acc[gone, :].astype(BF16)
        if step < bits + depth:
            ar_copy(k, step).start()
        else:
            chunk_out(k).start()

    first_it = 9
    points = [-11.8, -9.9, -8.0]
    lead = len(points)
    points += [-7.8 + FRONT * (u + 1) for u in range(heads * count)]
    mid = len(points)
    ends = []
    clock = 0.0
    for h in range(heads):
        for i in range(count - 1, -1, -1):
            for _ in range(i + 1):
                clock += UNIT
                points.append(clock)
            clock += 0.7
        ends.append(clock)
    last_time = clock
    ready = [points[0]] * 3 + [points[2]] * 3 + ends
    ready += [last_time] * (len(chunks) - len(ready))
    ticks = {}
    after = []
    for when, u, k, step in plan(bits, chunks, ready, points, width):
        if u < len(points):
            ticks.setdefault(u, []).append(functools.partial(advance, k, step))
        else:
            after.append((when, functools.partial(advance, k, step)))

    def forward(b, slot, before_mix):
        rows = block(b)
        unit, _ = unit_rows(x_s[rows, :])
        n1 = (unit * gain1 + bias1).astype(BF16)
        n2 = (unit * gain2 + bias2).astype(BF16)
        n1_s[rows, :] = n1
        hold[2 + slot] = n2
        pre = dot(n2, we[...], 1, 0) + exp_b
        big = 0.5 * (1.0 + lax.erf(pre * np.float32(0.5**0.5)))
        act = (pre * big).astype(BF16)
        slope = big + pre * (jnp.exp(-0.5 * pre * pre) * np.float32((2 * np.pi) ** -0.5))
        hold[slot] = act
        hold[4 + slot] = slope.astype(BF16)
        mix = dot(act, wc[...], 1, 0).astype(BF16)
        before_mix()
        x_s[rows, :] = mix
        proj = dot(wt[...], n1, 1, 1) + qb_s[...]
        cosine = cos_t[:, rows]
        sine = sin_t[:, rows]

        def turn(rows_in):
            a = rows_in[: ROT // 2]
            c = rows_in[ROT // 2 : ROT]
            return jnp.concatenate(
                [a * cosine - c * sine, c * cosine + a * sine, rows_in[ROT:]], 0
            )

        place = lax.broadcasted_iota(jnp.int32, (HD, blk), 1) + (b % per) * blk
        first = lax.broadcasted_iota(jnp.int32, (HD, blk), 0) == 0
        extra = jnp.where(first & (place >= len_ref[0]), MASKED, 0.0)
        for h in range(heads):
            lo = 3 * h * HD
            q = turn(proj[lo : lo + HD])
            k = turn(proj[lo + HD : lo + 2 * HD])
            v = proj[lo + 2 * HD : lo + 3 * HD]
            qa[h, :HD, rows] = (q * root).astype(BF16)
            kt[h, :, rows] = k.astype(BF16)
            kr[h, rows, :] = jnp.transpose(jnp.concatenate([k, extra], 0)).astype(BF16)
            va[h, :HD, rows] = v.astype(BF16)
            vr[h, rows, :] = jnp.transpose(v).astype(BF16)

    def mate(k):
        low = (t + k) % 2
        high = (t // 2 + k // 2) % 2
        return low + 2 * high

    key_i = lax.broadcasted_iota(jnp.int32, (blk, blk), 0)
    query_i = lax.broadcasted_iota(jnp.int32, (blk, blk), 1)

    def serve(unit, low, high):
        for u, jobs in ticks.items():
            if low <= u < high:

                @pl.when(unit == u)
                def _(jobs=jobs):
                    for job in jobs:
                        job()

    def front(i):
        passed = jnp.where(i == count - 1, lead, -mid)
        base = (i // per) * per
        mine = block(i)

        def head(h, _):
            q_aug = qa[h, :, mine]

            def weigh(j, scores, high, out):
                top = jnp.max(jnp.max(scores.reshape(blk // 8, 8, blk), 0), 0, keepdims=True)
                top = jnp.maximum(high, top)
                p = jnp.exp(scores - top).astype(BF16)
                return top, out * jnp.exp(high - top) + dot(va[h, :, block(j)], p, 1, 0)

            def onward(j, carry):
                more = weigh(j, dot(kr[h, block(j), :], q_aug, 1, 0), *carry)
                serve(passed + h * count + (j - base), lead, mid)
                return more

            begin = (jnp.full((1, blk), MASKED, F32), jnp.zeros((va.shape[1], blk), F32))
            carry = lax.fori_loop(base, i, onward, begin)
            scores = dot(kr[h, mine, :], q_aug, 1, 0)
            high, out = weigh(i, jnp.where(key_i <= query_i, scores, MASKED), *carry)
            norm = out[HD : HD + 1]
            ctx_s[h, :, mine] = (out[:HD] * (1.0 / norm)).astype(BF16)
            lse[pl.ds(h, 1), mine] = high + jnp.log(norm)
            serve(passed + h * count + (i - base), lead, mid)
            return 0

        lax.fori_loop(0, heads, head, 0)
        ctx = ctx_s[:, :, mine].reshape(local, blk)
        mix = dot(ctx, wd[...], 0, 0) + x_s[mine, :].astype(F32)
        x_s[mine, :] = mix.astype(BF16)

    def feed_part(rows):
        part = dot(s_s[rows, :], we[...], 1, 1)
        vec[2:3, :] += jnp.sum(part * n1_s[rows, :].astype(F32), 0, keepdims=True)
        vec[3:4, :] += jnp.sum(part, 0, keepdims=True)
        return part * gain2

    def phase(it, _):
        late = it // 7 > 0
        b = mate(jnp.where(late, 2 + (it + 1) % 2, it % 4))
        slot = jnp.where(late, (it + 1) % 2, (it % 4) // 3)
        rows = block(b)

        @pl.when(it == 1)
        def _():
            gather[2].wait_recv()
            gather[3].wait_recv()

        @pl.when(it == 2)
        def _():
            gather[0].wait_send()
            gather[1].start()
            gather[0].wait_recv()
            gather[4].start()

        @pl.when(it == 3)
        def _():
            gather[4].wait_recv()

        @pl.when(it < 4)
        def _():
            def settle():
                @pl.when(it == 2)
                def _():
                    gather[4].wait_send()

            forward(b, slot, settle)

        @pl.when(((it > 3) & (it < 7)) | (it == 11))
        def _():
            front(jnp.where(late, count - 1, it - 4))

        @pl.when(it == 7)
        def _():
            gather[1].wait_recv()
            gather[5].start()

        @pl.when(it == 8)
        def _():
            gather[5].wait_recv()

        serve(it - first_it, 0, lead)

        @pl.when((it < 2) | (it == 7) | (it == 8))
        def _():
            acc[:width] += dot(hold[slot], g_s[rows, :], 0, 0)

        @pl.when((it < 2) | (it == 9) | (it == 10))
        def _():
            slope = hold[4 + slot].astype(F32)
            grad_pre = (dot(g_s[rows, :], wc[...], 1, 1) * slope).astype(BF16)
            s_s[rows, :] = grad_pre
            vec[5:6, :] += jnp.sum(grad_pre.astype(F32), 0, keepdims=True)
            acc[width : 2 * width] += dot(hold[2 + slot], grad_pre, 0, 0)
            grad_ctx = dot(wd[...], g_s[rows, :], 1, 1).astype(BF16)
            for h in range(heads):
                dot_s[h, :, rows] = grad_ctx[h * HD : (h + 1) * HD]

        @pl.when(it < 2)
        def _():
            s_s[rows, :] = feed_part(rows).astype(BF16)

        return 0

    lax.fori_loop(0, 12, phase, 0)
    for k in (1, 2, 3, 5):
        gather[k].wait_send()
    pl.semaphore_signal(free_sem.at[0], inc=1, device_id=sib, device_id_type=MESH)
    pl.semaphore_signal(free_sem.at[1], inc=1, device_id=across, device_id_type=MESH)

    def dense_grad(i, _):
        grad_d = dot(ctx_s[:, :, block(i)].reshape(local, blk), g_s[block(i), :], 1, 0)
        for h in range(heads):
            at = attn + h * band + 3 * HD
            acc[at : at + HD, :] += grad_d[h * HD : (h + 1) * HD]
        return 0

    lax.fori_loop(0, count, dense_grad, 0)

    sums = (x_s, s_s)

    def to_sib(i, w):
        slot = i // 2
        src = sums[w].at[block(i)]
        return send(src, hold.at[2 * slot + w], rs_send.at[slot, w], rs_recv.at[slot, w], sib)

    def to_owner(i, w):
        src = sums[w].at[block(i)]
        return send(src, hold.at[4 + w], rs_send.at[2, w], rs_recv.at[2, w], across)

    def hand_over(i, w):
        @pl.when(core_bit != i % 2)
        def _():
            to_sib(i, w).start()

    def pass_on(i, w):
        @pl.when(core_bit == i % 2)
        def _():
            to_sib(i, w).wait_recv()

        @pl.when((core_bit == i % 2) & (chip_bit != i // 2))
        def _():
            rows = block(i)
            both = sums[w][rows, :].astype(F32) + hold[2 * (i // 2) + w].astype(F32)
            sums[w][rows, :] = both.astype(BF16)
            to_owner(i, w).start()

    def mixes_over():
        pl.semaphore_wait(free_sem.at[0], 1)
        pl.semaphore_wait(free_sem.at[1], 1)

        def one(i, _):
            hand_over(i, 0)
            return 0

        lax.fori_loop(0, count, one, 0)

    def mixes_on():
        def one(i, _):
            pass_on(i, 0)
            return 0

        lax.fori_loop(0, count, one, 0)

    ticks.setdefault(mid + 3, []).insert(0, mixes_over)
    ticks.setdefault(mid + 7, []).insert(0, mixes_on)

    def attend(visit, _):
        h = visit // count
        i = count - 1 - visit % count
        base = (i // per) * per
        mine = block(i)
        passed = h * (count * (count + 1) // 2) + mid
        passed += count * (count - 1 - i) - ((count - 1 - i) * (count - 2 - i)) // 2

        @pl.when(i == count - 1)
        def _():
            dkt[...] = jnp.zeros_like(dkt)
            dvt[...] = jnp.zeros_like(dvt)

        q_aug = qa[h, :, mine]
        q = q_aug[:HD]
        go = dot_s[h, :, mine]
        total_log = lse[pl.ds(h, 1), mine]
        inner = jnp.sum(ctx_s[h, :, mine].astype(F32) * go.astype(F32), 0, keepdims=True)

        def back(j, scores):
            cols = block(j)
            p = jnp.exp(scores - total_log)
            dvt[:, cols] += dot(go, p.astype(BF16), 1, 1)
            dp_t = dot(vr[h, cols, :], go, 1, 0)
            ds = (p * (dp_t - inner)).astype(BF16)
            dkt[:, cols] += dot(q, ds, 1, 1)
            return dot(kt[h, :, cols], ds, 1, 0)

        def onward(j, dq):
            more = back(j, dot(kr[h, block(j), :], q_aug, 1, 0))
            serve(passed + (j - base), mid, len(points))
            return dq + more

        dq = lax.fori_loop(base, i, onward, jnp.zeros((HD, blk), F32))
        scores = dot(kr[h, mine, :], q_aug, 1, 0)
        dq += back(i, jnp.where(key_i <= query_i, scores, MASKED))
        serve(passed + (i - base), mid, len(points))
        cosine = cos_t[:, mine]
        sine = sin_t[:, mine]

        def unturn(rows_in):
            a = rows_in[: ROT // 2]
            c = rows_in[ROT // 2 : ROT]
            return jnp.concatenate(
                [a * cosine + c * sine, c * cosine - a * sine, rows_in[ROT:]], 0
            )

        qa[h, :HD, mine] = unturn(dq * root).astype(BF16)
        kt[h, :, mine] = unturn(dkt[:, mine]).astype(BF16)
        va[h, :HD, mine] = dvt[:, mine].astype(BF16)
        grad_proj = jnp.concatenate([qa[h, :HD, mine], kt[h, :, mine], va[h, :HD, mine]], 0)
        at = attn + h * band
        acc[pl.ds(pl.multiple_of(at, HD), 3 * HD), :] += dot(grad_proj, n1_s[mine, :], 1, 0)

        @pl.when(i == 0)
        def _():
            w32 = wt[pl.ds(pl.multiple_of(3 * h * HD, HD), 3 * HD), :].astype(F32)
            grads = acc[pl.ds(pl.multiple_of(at, HD), 3 * HD), :]
            vec[0:1, :] += jnp.sum(w32 * grads, 0, keepdims=True)

        return 0

    lax.fori_loop(0, heads * count, attend, 0)

    def token_grads(r):
        i = mate(r)
        mine = block(i)
        parts = [(qa[h, :HD, mine], kt[h, :, mine], va[h, :HD, mine]) for h in range(heads)]
        every = jnp.concatenate([x for three in parts for x in three], 0)
        fed = s_s[mine, :].astype(F32) if r < 2 else feed_part(mine)
        s_s[mine, :] = (dot(every, wt[...], 0, 0) * gain1 + fed).astype(BF16)
        hand_over(i, 1)
        ones = jnp.ones((8, blk), BF16)
        vec[6:7, : 3 * local] += dot(ones, every, 1, 1)[:1]

    again = pltpu.make_async_copy(tok, n1_s.at[own], in_sem.at[0])

    swaps = peers + [sib, across]
    inside = len(peers)

    def swap(q):
        return send(vec, vec_in.at[q], v_send.at[q], v_recv.at[q], swaps[q])

    shared = lax.broadcasted_iota(jnp.int32, vec.shape, 0) < 5

    def finish_swap(q):
        swap(q).wait()
        extra = vec_in[q]
        if q >= inside:
            extra = jnp.where(shared, extra, 0.0)
        vec[...] += extra

    def vectors():
        w32 = wt[...].astype(F32)
        column = jnp.transpose(jnp.broadcast_to(vec[6:7, : 3 * local], (8, 3 * local)))[:, :1]
        grad_bias = jnp.sum(w32 * column, 0, keepdims=True)
        vec[1:2, :] = grad_bias
        vec[0:1, :] = (vec[0:1, :] - bias1 * grad_bias) / gain1
        vec[2:3, :] = (vec[2:3, :] - bias1 * vec[3:4, :]) / gain1
        vec[4:5, :] = jnp.sum(g_s[own, :].astype(F32), 0, keepdims=True)
        again.start()

    out_copies = [
        pltpu.make_async_copy(mixed_s, mixed_o, out_sem.at[0]),
        pltpu.make_async_copy(gtok_s, gtok_o, out_sem.at[1]),
    ]

    def tokens_out():
        to_sib(t, 1).wait_recv()
        for w in range(2):
            to_owner(flip(t, 2), w).wait()
        again.wait()
        rows = n1_s[own, :]
        mix = rows.astype(F32) + (outb1_r[...] + outb2_r[...]).reshape(1, width)
        mix += x_s[own, :].astype(F32)
        s = s_s[own, :].astype(F32)
        for w in (2 * chip_bit, 4):
            mix += hold[w].astype(F32)
            s += hold[w + 1].astype(F32)
        mixed_s[...] = mix.astype(BF16)
        unit, inverse = unit_rows(rows)
        gtok_s[...] = g_s[own, :].astype(F32) + inverse * (
            s - jnp.mean(s, -1, keepdims=True) - unit * jnp.mean(s * unit, -1, keepdims=True)
        )
        for copy in out_copies:
            copy.start()

    jobs = list(after)
    jobs.append((last_time + 1.7, functools.partial(token_grads, 3)))
    jobs.append((last_time + 3.7, functools.partial(token_grads, 2)))
    jobs.append((last_time + 5.7, functools.partial(token_grads, 1)))
    jobs.append((last_time + 6.8, lambda: pass_on(mate(2), 1)))
    jobs.append((last_time + 7.3, functools.partial(token_grads, 0)))
    jobs.append((last_time + 8.5, vectors))
    for q in range(len(swaps)):

        def trade(q=q):
            if q > 0:
                finish_swap(q - 1)
            swap(q).start()

        jobs.append((last_time + 9.5 + 3.2 * q, trade))
    jobs.append((last_time + 9.5 + 3.2 * len(swaps), lambda: finish_swap(len(swaps) - 1)))
    jobs.append((last_time + 27.0, tokens_out))
    for _, job in sorted(jobs, key=lambda pair: pair[0]):
        job()
    vec_o[...] = vec[...]
    for i in range(count):

        @pl.when(core_bit != i % 2)
        def _(i=i):
            for w in range(2):
                to_sib(i, w).wait_send()

    for copy in out_copies:
        copy.wait()
    for k in range(len(chunks)):
        chunk_out(k).wait()


def finish(res, mixed, gtok, vec, *refs):
    outs, (low, high, mid_m, mid_g, moved, in_sem, out_sem) = refs[:14], refs[14:]
    mixed_o, gtok_o, gain1_o, bias1_o, gain2_o, bias2_o, qkv_o, qkvb_o, wd_o, db_o, we_o, be_o, wc_o, cb_o = outs
    width = res.shape[1]
    heads = wd_o.shape[0] // HD
    count = low.shape[0] // SUB
    passing = [
        pltpu.make_async_copy(mixed, mid_m, moved.at[0]),
        pltpu.make_async_copy(gtok, mid_g, moved.at[1]),
    ]
    leaving = [
        pltpu.make_async_copy(mid_m, mixed_o, moved.at[2]),
        pltpu.make_async_copy(mid_g, gtok_o, moved.at[3]),
    ]

    def rows(k):
        return pl.ds(k * SUB, SUB)

    comes = [pltpu.make_async_copy(res.at[rows(k)], low.at[rows(k)], in_sem.at[k]) for k in range(count)]
    goes = []
    for k in range(6):
        where = (wc_o, we_o)[k // 3].at[rows(k % 3)]
        goes.append([pltpu.make_async_copy(high.at[rows(k)], where, out_sem.at[k])])
    for h in range(heads):
        first = (6 + h) * SUB
        places = [qkv_o.at[c, h * HD : (h + 1) * HD, :] for c in range(3)] + [wd_o.at[h * HD : (h + 1) * HD]]
        goes.append(
            [
                pltpu.make_async_copy(
                    high.at[pl.ds(first + c * HD, HD)], place, out_sem.at[6 + 4 * h + c]
                )
                for c, place in enumerate(places)
            ]
        )
    for copy in passing + comes:
        copy.start()
    for ref, row in (
        (gain1_o, 0),
        (bias1_o, 1),
        (gain2_o, 2),
        (bias2_o, 3),
        (db_o, 4),
        (cb_o, 4),
        (be_o, 5),
    ):
        ref[...] = vec[row, :]
    for h in range(heads):
        for c in range(3):
            lo = (3 * h + c) * HD
            qkvb_o[c : c + 1, h * HD : (h + 1) * HD] = vec[6:7, lo : lo + HD]
    for k in range(count):
        comes[k].wait()
        high[rows(k), :] = low[rows(k), :].astype(F32)
        for copy in goes[k]:
            copy.start()
        if k == 0:
            for come, go in zip(passing, leaving):
                come.wait()
                go.start()
    for copy in [x for some in goes for x in some] + leaving:
        copy.wait()


def shards(
    n,
    tokens,
    input_gain,
    input_bias,
    post_gain,
    post_bias,
    query_key_value,
    query_key_value_bias,
    dense_weight,
    dense_bias,
    expand_weight,
    expand_bias,
    contract_weight,
    contract_bias,
    lengths,
    cotangent,
):
    blk, width = tokens.shape
    local = query_key_value.shape[2]
    hidden = expand_weight.shape[1]
    heads = local // HD
    total = 4 * blk
    bits = n.bit_length() - 1
    swaps = bits + 2
    parts = len(pieces(n, heads))
    room = sum(chunk[4] for chunk in pieces(n, heads))
    cosine, sine = angle_rows(total)
    vmem = pl.BlockSpec(memory_space=pltpu.VMEM)
    smem = pl.BlockSpec(memory_space=pltpu.SMEM)
    hbm = pl.BlockSpec(memory_space=pl.ANY)
    dma = pltpu.SemaphoreType.DMA
    mixed, grad_tokens, res, vec = pl.pallas_call(
        functools.partial(core, n),
        name="core",
        out_shape=(
            jax.ShapeDtypeStruct((blk, width), BF16),
            jax.ShapeDtypeStruct((blk, width), F32),
            jax.ShapeDtypeStruct((3 * width, width), BF16),
            jax.ShapeDtypeStruct((8, width), F32),
        ),
        in_specs=[hbm, hbm, smem] + [vmem] * 7 + [hbm, vmem, hbm, hbm, hbm, vmem, vmem],
        out_specs=[hbm, hbm, hbm, vmem],
        scratch_shapes=[
            pltpu.VMEM((total, width), BF16),
            pltpu.VMEM((total, width), BF16),
            pltpu.VMEM((total, width), BF16),
            pltpu.VMEM((total, width), BF16),
            pltpu.VMEM((3 * local, width), BF16),
            pltpu.VMEM((local, width), BF16),
            pltpu.VMEM((width, hidden), BF16),
            pltpu.VMEM((hidden, width), BF16),
            pltpu.VMEM((3 * local, 1), F32),
            pltpu.VMEM((3 * width, width), F32),
            pltpu.VMEM((3 * width, width), BF16),
            pltpu.VMEM((6, blk, width), BF16),
            pltpu.VMEM((heads, 2 * HD, total), BF16),
            pltpu.VMEM((heads, HD, total), BF16),
            pltpu.VMEM((heads, total, 2 * HD), BF16),
            pltpu.VMEM((heads, HD + 16, total), BF16),
            pltpu.VMEM((heads, total, HD), BF16),
            pltpu.VMEM((heads, HD, total), BF16),
            pltpu.VMEM((8, total), F32),
            pltpu.VMEM((HD, total), F32),
            pltpu.VMEM((HD, total), F32),
            pltpu.VMEM((heads, HD, total), BF16),
            pltpu.VMEM((blk, width), BF16),
            pltpu.VMEM((blk, width), F32),
            pltpu.VMEM((8, width), F32),
            pltpu.VMEM((swaps, 8, width), F32),
            pltpu.VMEM((room, width), BF16),
            pltpu.VMEM((room, width), BF16),
            dma((5 + 3 * heads,)),
            dma((6,)),
            dma((6,)),
            dma((3, 2)),
            dma((3, 2)),
            dma((2 * bits, parts)),
            dma((2 * bits, parts)),
            dma((swaps,)),
            dma((swaps,)),
            dma((2 + parts,)),
            pltpu.SemaphoreType.REGULAR((2,)),
        ],
        compiler_params=pltpu.CompilerParams(
            vmem_limit_bytes=63 * 2**20, collective_id=0, has_side_effects=True
        ),
    )(
        tokens,
        cotangent,
        lengths,
        input_gain,
        input_bias,
        post_gain,
        post_bias,
        expand_bias,
        dense_bias,
        contract_bias,
        jnp.transpose(query_key_value, (0, 2, 1)),
        query_key_value_bias,
        dense_weight,
        expand_weight,
        contract_weight,
        cosine,
        sine,
    )

    vector = jax.ShapeDtypeStruct((width,), F32)
    outs = pl.pallas_call(
        finish,
        name="finish",
        in_specs=[hbm, hbm, hbm, vmem],
        out_specs=[hbm, hbm] + [vmem] * 4 + [hbm, vmem, hbm, vmem, hbm, vmem, hbm, vmem],
        scratch_shapes=[
            pltpu.VMEM((3 * width, width), BF16),
            pltpu.VMEM((3 * width, width), F32),
            pltpu.VMEM((blk, width), BF16),
            pltpu.VMEM((blk, width), F32),
            dma((4,)),
            dma((9,)),
            dma((6 + 4 * heads,)),
        ],
        out_shape=(
            jax.ShapeDtypeStruct((blk, width), BF16),
            jax.ShapeDtypeStruct((blk, width), F32),
            vector,
            vector,
            vector,
            vector,
            jax.ShapeDtypeStruct((3, local, width), F32),
            jax.ShapeDtypeStruct((3, local), F32),
            jax.ShapeDtypeStruct((local, width), F32),
            vector,
            jax.ShapeDtypeStruct((width, hidden), F32),
            jax.ShapeDtypeStruct((hidden,), F32),
            jax.ShapeDtypeStruct((hidden, width), F32),
            vector,
        ),
        compiler_params=pltpu.CompilerParams(vmem_limit_bytes=63 * 2**20),
    )(res, mixed, grad_tokens, vec)
    outs = list(outs)
    outs[6] = jnp.transpose(outs[6], (0, 2, 1))
    return tuple(outs)


def solution(mesh):
    rows = P(("dp", "tensor"), None)
    weights = (
        P(None, None, "tensor"),
        P(None, "tensor"),
        P("tensor", None),
        P(),
        P(None, "tensor"),
        P("tensor"),
        P("tensor", None),
        P(),
    )
    return jax.shard_map(
        functools.partial(shards, mesh.shape["dp"]),
        mesh=mesh,
        in_specs=(rows, P(), P(), P(), P()) + weights + (P("dp"), rows),
        out_specs=(rows, rows, P(), P(), P(), P()) + weights,
        check_vma=False,
    )
```

```python
import functools

import jax
import jax.numpy as jnp
import numpy as np
from jax import lax
from jax.experimental import pallas as pl
from jax.experimental.pallas import tpu as pltpu
from jax.sharding import PartitionSpec as P

HD = 64
ROT = 16
LEN = 2048
EPS = 1e-05
MASKED = -1e30
F32 = jnp.float32
BF16 = jnp.bfloat16


def dot(a, b, ca, cb):
    return lax.dot_general(a, b, (((ca,), (cb,)), ((), ())), preferred_element_type=F32)


def angle_rows(count):
    half = ROT // 2
    freqs = np.float32(10000.0) ** (
        np.float32(-2.0) * np.arange(half, dtype=np.float32) / np.float32(ROT)
    )
    place = (np.arange(count) % LEN).astype(np.float32)
    angle = (freqs[:, None] * place[None, :]).astype(np.float32)
    return np.cos(angle), np.sin(angle)


def unit_rows(rows):
    values = rows.astype(F32)
    centred = values - jnp.mean(values, -1, keepdims=True)
    inverse = lax.rsqrt(jnp.mean(centred * centred, -1, keepdims=True) + EPS)
    return centred * inverse, inverse

MESH = pl.DeviceIdType.MESH
SUB = 256
UNIT = 1.0
FRONT = 0.52


def flip(value, bits):
    bit = 1
    while bit <= bits:
        if (bits // bit) % 2:
            value = value + bit * (1 - 2 * ((value // bit) % 2))
        bit *= 2
    return value


def pieces(n, heads):
    bits = n.bit_length() - 1
    count = 6 + heads
    made = []
    base = 0
    for k in range(count):
        last = k == count - 1
        parts = 4 if last and n <= 16 else 1
        size = SUB // parts
        depth = max(bits - 2, 1) if last else bits - 1
        room = size - size // 2**depth + (bits - depth) * (size // 2**depth)
        for p in range(parts):
            made.append((SUB * k + size * p, size, depth, base, room))
            base += room
    return made


def trade_size(rows, depth, bits, step):
    if step < depth:
        return rows // 2 ** (step + 1)
    if step < bits:
        return rows // 2**depth
    return rows // 2 ** (depth - (step - bits))


def trade_bit(depth, bits, step):
    return step if step < bits else depth - (step - bits) - 1


def plan(bits, chunks, ready, points, width, margin=0.3, rate=0.043, delay=2.2, work=0.2):
    free = {}
    clock = points[0]
    reached = 0
    todo = [(when, k, 0) for k, when in enumerate(ready)]
    made = []
    while todo:
        todo.sort()
        when, k, step = todo.pop(0)
        later = [(at, u) for u, at in enumerate(points) if at >= when and u >= reached]
        if later:
            at, reached = later[0]
            clock = max(at, clock)
        else:
            reached = len(points)
            clock = max(when, clock, points[-1] + 1.5)
        clock += work
        made.append((clock, reached, k, step))
        _, rows, depth, _, _ = chunks[k]
        if step < bits + depth:
            cost = trade_size(rows, depth, bits, step) * width * 2e-6 / rate
            uses = {0: {"x": 1}, 1: {"end": 1}}.get(trade_bit(depth, bits, step), {"end": 1, "mid": 2})
            through = clock
            for link, share in uses.items():
                free[link] = max(free.get(link, points[0]), clock) + share * cost
                through = max(through, free[link])
            todo.append((through + delay + (margin if later else 0.0), k, step + 1))
    return made


def core(
    n,
    tok,
    cot,
    len_ref,
    gain1_r,
    bias1_r,
    gain2_r,
    bias2_r,
    exp_r,
    outb1_r,
    outb2_r,
    qkv,
    qkv_b,
    wd_h,
    we_h,
    wc_h,
    cos_t,
    sin_t,
    mixed_o,
    gtok_o,
    res_o,
    vec_o,
    x_s,
    g_s,
    n1_s,
    s_s,
    wt,
    wd,
    we,
    wc,
    qb_s,
    acc,
    res,
    hold,
    qa,
    kt,
    kr,
    va,
    vr,
    dot_s,
    lse,
    dkt,
    dvt,
    ctx_s,
    mixed_s,
    gtok_s,
    vec,
    vec_in,
    sx,
    rx,
    in_sem,
    ag_send,
    ag_recv,
    rs_send,
    rs_recv,
    ar_send,
    ar_recv,
    v_send,
    v_recv,
    out_sem,
    free_sem,
):
    blk, width = tok.shape
    total = x_s.shape[0]
    local = wd.shape[0]
    heads = local // HD
    count = total // blk
    per = LEN // blk
    root = HD**-0.5
    band = 4 * HD
    attn = 2 * width
    bits = n.bit_length() - 1
    dp = lax.axis_index("dp")
    t = lax.axis_index("tensor")
    core_bit = t % 2
    chip_bit = t // 2
    sib = (dp, flip(t, 1))
    across = (dp, flip(t, 2))
    peers = [(flip(dp, 2**q), t) for q in range(bits)]

    def send(src, dst, ssem, rsem, where):
        return pltpu.make_async_remote_copy(
            src_ref=src,
            dst_ref=dst,
            send_sem=ssem,
            recv_sem=rsem,
            device_id=where,
            device_id_type=MESH,
        )

    def block(b):
        return pl.ds(pl.multiple_of(b * blk, blk), blk)

    own = block(t)
    other = block(flip(t, 2))
    fetch = [
        pltpu.make_async_copy(tok, x_s.at[own], in_sem.at[0]),
        pltpu.make_async_copy(cot, g_s.at[own], in_sem.at[1]),
        pltpu.make_async_copy(we_h, we, in_sem.at[2]),
        pltpu.make_async_copy(wc_h, wc, in_sem.at[3]),
        pltpu.make_async_copy(wd_h, wd, in_sem.at[4]),
    ]
    for h in range(heads):
        for c in range(3):
            fetch.append(
                pltpu.make_async_copy(
                    qkv.at[c, h * HD : (h + 1) * HD, :],
                    wt.at[(3 * h + c) * HD : (3 * h + c + 1) * HD, :],
                    in_sem.at[5 + 3 * h + c],
                )
            )
    for copy in fetch:
        copy.start()

    barrier = pltpu.get_barrier_semaphore()
    greeted = [sib, across] + peers
    for who in greeted:
        pl.semaphore_signal(barrier, inc=1, device_id=who, device_id_type=MESH)
    pl.semaphore_wait(barrier, len(greeted))

    gather = [
        send(tok, x_s.at[own], ag_send.at[0], ag_recv.at[0], across),
        send(cot, g_s.at[own], ag_send.at[1], ag_recv.at[1], across),
        send(tok, x_s.at[own], ag_send.at[2], ag_recv.at[2], sib),
        send(cot, g_s.at[own], ag_send.at[3], ag_recv.at[3], sib),
        send(x_s.at[other], x_s.at[other], ag_send.at[4], ag_recv.at[4], sib),
        send(g_s.at[other], g_s.at[other], ag_send.at[5], ag_recv.at[5], sib),
    ]
    gather[0].start()
    gather[2].start()
    gather[3].start()

    gain1, bias1, gain2, bias2, exp_b = (
        r[...].reshape(1, width) for r in (gain1_r, bias1_r, gain2_r, bias2_r, exp_r)
    )
    for c in range(3):
        column = jnp.transpose(jnp.broadcast_to(qkv_b[c : c + 1, :], (8, local)))
        for h in range(heads):
            qb_s[(3 * h + c) * HD : (3 * h + c + 1) * HD, :] = column[h * HD : (h + 1) * HD, :1]
    for ref in (acc, vec):
        ref[...] = jnp.zeros_like(ref)
    one_row = (lax.broadcasted_iota(jnp.int32, (heads, HD, total), 1) == 0).astype(F32)
    qa[:, HD:, :] = one_row.astype(BF16)
    va[:, HD:, :] = one_row[:, : va.shape[1] - HD, :].astype(BF16)
    for copy in fetch:
        copy.wait()

    chunks = pieces(n, heads)

    def rows_of(k, first, size):
        step = min(chunks[k][1] // 2 ** chunks[k][2], 128)
        return pl.ds(pl.multiple_of(chunks[k][0] + first, step), size)

    def first_of(k, q):
        first = 0
        for p in range(q):
            first = first + ((dp // 2**p) % 2) * (chunks[k][1] // 2 ** (p + 1))
        return first

    def kept(k, q):
        return rows_of(k, first_of(k, q), chunks[k][1] // 2**q)

    def given(k, q):
        size = chunks[k][1] // 2**q
        bit = (dp // 2 ** (q - 1)) % 2
        return rows_of(k, first_of(k, q - 1) + (1 - bit) * size, size)

    def landing(k, step):
        _, rows, depth, base, _ = chunks[k]
        low = sum(trade_size(rows, depth, bits, p) for p in range(step))
        return pl.ds(base + low, trade_size(rows, depth, bits, step))

    def ar_copy(k, step):
        sems = (ar_send.at[step, k], ar_recv.at[step, k])
        depth = chunks[k][2]
        who = peers[trade_bit(depth, bits, step)]
        if step < bits:
            return send(sx.at[landing(k, step)], rx.at[landing(k, step)], *sems, who)
        piece = res.at[kept(k, depth - (step - bits))]
        return send(piece, piece, *sems, who)

    def chunk_out(k):
        rows = kept(k, 0)
        return pltpu.make_async_copy(res.at[rows], res_o.at[rows], out_sem.at[2 + k])

    def advance(k, step):
        depth = chunks[k][2]
        if step > 0:
            ar_copy(k, step - 1).wait()
        if 1 <= step <= bits:
            mine = kept(k, min(step, depth))
            had = acc[mine, :] if step <= depth else sx[landing(k, step - 1), :].astype(F32)
            done = had + rx[landing(k, step - 1), :].astype(F32)
            if step < bits:
                acc[mine, :] = done
            else:
                res[mine, :] = done.astype(BF16)
        if step < bits:
            gone = given(k, step + 1) if step < depth else kept(k, depth)
            sx[landing(k, step), :] = acc[gone, :].astype(BF16)
        if step < bits + depth:
            ar_copy(k, step).start()
        else:
            chunk_out(k).start()

    first_it = 9
    points = [-11.8, -9.9, -8.0]
    lead = len(points)
    points += [-7.8 + FRONT * (u + 1) for u in range(heads * count)]
    mid = len(points)
    ends = []
    clock = 0.0
    for h in range(heads):
        for i in range(count - 1, -1, -1):
            for _ in range(i + 1):
                clock += UNIT
                points.append(clock)
            clock += 0.7
        ends.append(clock)
    last_time = clock
    ready = [points[0]] * 3 + [points[2]] * 3 + ends
    ready += [last_time] * (len(chunks) - len(ready))
    ticks = {}
    after = []
    for when, u, k, step in plan(bits, chunks, ready, points, width):
        if u < len(points):
            ticks.setdefault(u, []).append(functools.partial(advance, k, step))
        else:
            after.append((when, functools.partial(advance, k, step)))

    def forward(b, slot, before_mix):
        rows = block(b)
        unit, _ = unit_rows(x_s[rows, :])
        n1 = (unit * gain1 + bias1).astype(BF16)
        n2 = (unit * gain2 + bias2).astype(BF16)
        n1_s[rows, :] = n1
        hold[2 + slot] = n2
        pre = dot(n2, we[...], 1, 0) + exp_b
        big = 0.5 * (1.0 + lax.erf(pre * np.float32(0.5**0.5)))
        act = (pre * big).astype(BF16)
        slope = big + pre * (jnp.exp(-0.5 * pre * pre) * np.float32((2 * np.pi) ** -0.5))
        hold[slot] = act
        hold[4 + slot] = slope.astype(BF16)
        mix = dot(act, wc[...], 1, 0).astype(BF16)
        before_mix()
        x_s[rows, :] = mix
        proj = dot(wt[...], n1, 1, 1) + qb_s[...]
        cosine = cos_t[:, rows]
        sine = sin_t[:, rows]

        def turn(rows_in):
            a = rows_in[: ROT // 2]
            c = rows_in[ROT // 2 : ROT]
            return jnp.concatenate(
                [a * cosine - c * sine, c * cosine + a * sine, rows_in[ROT:]], 0
            )

        place = lax.broadcasted_iota(jnp.int32, (HD, blk), 1) + (b % per) * blk
        first = lax.broadcasted_iota(jnp.int32, (HD, blk), 0) == 0
        extra = jnp.where(first & (place >= len_ref[0]), MASKED, 0.0)
        for h in range(heads):
            lo = 3 * h * HD
            q = turn(proj[lo : lo + HD])
            k = turn(proj[lo + HD : lo + 2 * HD])
            v = proj[lo + 2 * HD : lo + 3 * HD]
            qa[h, :HD, rows] = (q * root).astype(BF16)
            kt[h, :, rows] = k.astype(BF16)
            kr[h, rows, :] = jnp.transpose(jnp.concatenate([k, extra], 0)).astype(BF16)
            va[h, :HD, rows] = v.astype(BF16)
            vr[h, rows, :] = jnp.transpose(v).astype(BF16)

    def mate(k):
        low = (t + k) % 2
        high = (t // 2 + k // 2) % 2
        return low + 2 * high

    key_i = lax.broadcasted_iota(jnp.int32, (blk, blk), 0)
    query_i = lax.broadcasted_iota(jnp.int32, (blk, blk), 1)

    def serve(unit, low, high):
        for u, jobs in ticks.items():
            if low <= u < high:

                @pl.when(unit == u)
                def _(jobs=jobs):
                    for job in jobs:
                        job()

    def front(i):
        passed = jnp.where(i == count - 1, lead, -mid)
        base = (i // per) * per
        mine = block(i)

        def head(h, _):
            q_aug = qa[h, :, mine]

            def weigh(j, scores, high, out):
                top = jnp.max(jnp.max(scores.reshape(blk // 8, 8, blk), 0), 0, keepdims=True)
                top = jnp.maximum(high, top)
                p = jnp.exp(scores - top).astype(BF16)
                return top, out * jnp.exp(high - top) + dot(va[h, :, block(j)], p, 1, 0)

            def onward(j, carry):
                more = weigh(j, dot(kr[h, block(j), :], q_aug, 1, 0), *carry)
                serve(passed + h * count + (j - base), lead, mid)
                return more

            begin = (jnp.full((1, blk), MASKED, F32), jnp.zeros((va.shape[1], blk), F32))
            carry = lax.fori_loop(base, i, onward, begin)
            scores = dot(kr[h, mine, :], q_aug, 1, 0)
            high, out = weigh(i, jnp.where(key_i <= query_i, scores, MASKED), *carry)
            norm = out[HD : HD + 1]
            ctx_s[h, :, mine] = (out[:HD] * (1.0 / norm)).astype(BF16)
            lse[pl.ds(h, 1), mine] = high + jnp.log(norm)
            serve(passed + h * count + (i - base), lead, mid)
            return 0

        lax.fori_loop(0, heads, head, 0)
        ctx = ctx_s[:, :, mine].reshape(local, blk)
        mix = dot(ctx, wd[...], 0, 0) + x_s[mine, :].astype(F32)
        x_s[mine, :] = mix.astype(BF16)

    def feed_part(rows):
        part = dot(s_s[rows, :], we[...], 1, 1)
        vec[2:3, :] += jnp.sum(part * n1_s[rows, :].astype(F32), 0, keepdims=True)
        vec[3:4, :] += jnp.sum(part, 0, keepdims=True)
        return part * gain2

    def phase(it, _):
        late = it // 7 > 0
        b = mate(jnp.where(late, 2 + (it + 1) % 2, it % 4))
        slot = jnp.where(late, (it + 1) % 2, (it % 4) // 3)
        rows = block(b)

        @pl.when(it == 1)
        def _():
            gather[2].wait_recv()
            gather[3].wait_recv()

        @pl.when(it == 2)
        def _():
            gather[0].wait_send()
            gather[1].start()
            gather[0].wait_recv()
            gather[4].start()

        @pl.when(it == 3)
        def _():
            gather[4].wait_recv()

        @pl.when(it < 4)
        def _():
            def settle():
                @pl.when(it == 2)
                def _():
                    gather[4].wait_send()

            forward(b, slot, settle)

        @pl.when(((it > 3) & (it < 7)) | (it == 11))
        def _():
            front(jnp.where(late, count - 1, it - 4))

        @pl.when(it == 7)
        def _():
            gather[1].wait_recv()
            gather[5].start()

        @pl.when(it == 8)
        def _():
            gather[5].wait_recv()

        serve(it - first_it, 0, lead)

        @pl.when((it < 2) | (it == 7) | (it == 8))
        def _():
            acc[:width] += dot(hold[slot], g_s[rows, :], 0, 0)

        @pl.when((it < 2) | (it == 9) | (it == 10))
        def _():
            slope = hold[4 + slot].astype(F32)
            grad_pre = (dot(g_s[rows, :], wc[...], 1, 1) * slope).astype(BF16)
            s_s[rows, :] = grad_pre
            vec[5:6, :] += jnp.sum(grad_pre.astype(F32), 0, keepdims=True)
            acc[width : 2 * width] += dot(hold[2 + slot], grad_pre, 0, 0)
            grad_ctx = dot(wd[...], g_s[rows, :], 1, 1).astype(BF16)
            for h in range(heads):
                dot_s[h, :, rows] = grad_ctx[h * HD : (h + 1) * HD]

        @pl.when(it < 2)
        def _():
            s_s[rows, :] = feed_part(rows).astype(BF16)

        return 0

    lax.fori_loop(0, 12, phase, 0)
    for k in (1, 2, 3, 5):
        gather[k].wait_send()
    pl.semaphore_signal(free_sem.at[0], inc=1, device_id=sib, device_id_type=MESH)
    pl.semaphore_signal(free_sem.at[1], inc=1, device_id=across, device_id_type=MESH)

    def dense_grad(i, _):
        grad_d = dot(ctx_s[:, :, block(i)].reshape(local, blk), g_s[block(i), :], 1, 0)
        for h in range(heads):
            at = attn + h * band + 3 * HD
            acc[at : at + HD, :] += grad_d[h * HD : (h + 1) * HD]
        return 0

    lax.fori_loop(0, count, dense_grad, 0)

    sums = (x_s, s_s)

    def to_sib(i, w):
        slot = i // 2
        src = sums[w].at[block(i)]
        return send(src, hold.at[2 * slot + w], rs_send.at[slot, w], rs_recv.at[slot, w], sib)

    def to_owner(i, w):
        src = sums[w].at[block(i)]
        return send(src, hold.at[4 + w], rs_send.at[2, w], rs_recv.at[2, w], across)

    def hand_over(i, w):
        @pl.when(core_bit != i % 2)
        def _():
            to_sib(i, w).start()

    def pass_on(i, w):
        @pl.when(core_bit == i % 2)
        def _():
            to_sib(i, w).wait_recv()

        @pl.when((core_bit == i % 2) & (chip_bit != i // 2))
        def _():
            rows = block(i)
            both = sums[w][rows, :].astype(F32) + hold[2 * (i // 2) + w].astype(F32)
            sums[w][rows, :] = both.astype(BF16)
            to_owner(i, w).start()

    def mixes_over():
        pl.semaphore_wait(free_sem.at[0], 1)
        pl.semaphore_wait(free_sem.at[1], 1)

        def one(i, _):
            hand_over(i, 0)
            return 0

        lax.fori_loop(0, count, one, 0)

    def mixes_on():
        def one(i, _):
            pass_on(i, 0)
            return 0

        lax.fori_loop(0, count, one, 0)

    ticks.setdefault(mid + 6, []).insert(0, mixes_over)
    ticks.setdefault(mid + 13, []).insert(0, mixes_on)

    def attend(visit, _):
        h = visit // count
        i = count - 1 - visit % count
        base = (i // per) * per
        mine = block(i)
        passed = h * (count * (count + 1) // 2) + mid
        passed += count * (count - 1 - i) - ((count - 1 - i) * (count - 2 - i)) // 2

        @pl.when(i == count - 1)
        def _():
            dkt[...] = jnp.zeros_like(dkt)
            dvt[...] = jnp.zeros_like(dvt)

        q_aug = qa[h, :, mine]
        q = q_aug[:HD]
        go = dot_s[h, :, mine]
        total_log = lse[pl.ds(h, 1), mine]
        inner = jnp.sum(ctx_s[h, :, mine].astype(F32) * go.astype(F32), 0, keepdims=True)

        def back(j, scores):
            cols = block(j)
            p = jnp.exp(scores - total_log)
            dvt[:, cols] += dot(go, p.astype(BF16), 1, 1)
            dp_t = dot(vr[h, cols, :], go, 1, 0)
            ds = (p * (dp_t - inner)).astype(BF16)
            dkt[:, cols] += dot(q, ds, 1, 1)
            return dot(kt[h, :, cols], ds, 1, 0)

        def onward(j, dq):
            more = back(j, dot(kr[h, block(j), :], q_aug, 1, 0))
            serve(passed + (j - base), mid, len(points))
            return dq + more

        dq = lax.fori_loop(base, i, onward, jnp.zeros((HD, blk), F32))
        scores = dot(kr[h, mine, :], q_aug, 1, 0)
        dq += back(i, jnp.where(key_i <= query_i, scores, MASKED))
        serve(passed + (i - base), mid, len(points))
        cosine = cos_t[:, mine]
        sine = sin_t[:, mine]

        def unturn(rows_in):
            a = rows_in[: ROT // 2]
            c = rows_in[ROT // 2 : ROT]
            return jnp.concatenate(
                [a * cosine + c * sine, c * cosine - a * sine, rows_in[ROT:]], 0
            )

        qa[h, :HD, mine] = unturn(dq * root).astype(BF16)
        kt[h, :, mine] = unturn(dkt[:, mine]).astype(BF16)
        va[h, :HD, mine] = dvt[:, mine].astype(BF16)
        grad_proj = jnp.concatenate([qa[h, :HD, mine], kt[h, :, mine], va[h, :HD, mine]], 0)
        at = attn + h * band
        acc[pl.ds(pl.multiple_of(at, HD), 3 * HD), :] += dot(grad_proj, n1_s[mine, :], 1, 0)

        @pl.when(i == 0)
        def _():
            w32 = wt[pl.ds(pl.multiple_of(3 * h * HD, HD), 3 * HD), :].astype(F32)
            grads = acc[pl.ds(pl.multiple_of(at, HD), 3 * HD), :]
            vec[0:1, :] += jnp.sum(w32 * grads, 0, keepdims=True)

        return 0

    lax.fori_loop(0, heads * count, attend, 0)

    def token_grads(r):
        i = mate(r)
        mine = block(i)
        parts = [(qa[h, :HD, mine], kt[h, :, mine], va[h, :HD, mine]) for h in range(heads)]
        every = jnp.concatenate([x for three in parts for x in three], 0)
        fed = s_s[mine, :].astype(F32) if r < 2 else feed_part(mine)
        s_s[mine, :] = (dot(every, wt[...], 0, 0) * gain1 + fed).astype(BF16)
        hand_over(i, 1)
        ones = jnp.ones((8, blk), BF16)
        vec[6:7, : 3 * local] += dot(ones, every, 1, 1)[:1]

    again = pltpu.make_async_copy(tok, n1_s.at[own], in_sem.at[0])

    swaps = peers + [sib, across]
    inside = len(peers)

    def swap(q):
        return send(vec, vec_in.at[q], v_send.at[q], v_recv.at[q], swaps[q])

    shared = lax.broadcasted_iota(jnp.int32, vec.shape, 0) < 5

    def finish_swap(q):
        swap(q).wait()
        extra = vec_in[q]
        if q >= inside:
            extra = jnp.where(shared, extra, 0.0)
        vec[...] += extra

    def vectors():
        w32 = wt[...].astype(F32)
        column = jnp.transpose(jnp.broadcast_to(vec[6:7, : 3 * local], (8, 3 * local)))[:, :1]
        grad_bias = jnp.sum(w32 * column, 0, keepdims=True)
        vec[1:2, :] = grad_bias
        vec[0:1, :] = (vec[0:1, :] - bias1 * grad_bias) / gain1
        vec[2:3, :] = (vec[2:3, :] - bias1 * vec[3:4, :]) / gain1
        vec[4:5, :] = jnp.sum(g_s[own, :].astype(F32), 0, keepdims=True)
        again.start()

    out_copies = [
        pltpu.make_async_copy(mixed_s, mixed_o, out_sem.at[0]),
        pltpu.make_async_copy(gtok_s, gtok_o, out_sem.at[1]),
    ]

    def tokens_out():
        to_sib(t, 1).wait_recv()
        for w in range(2):
            to_owner(flip(t, 2), w).wait()
        again.wait()
        rows = n1_s[own, :]
        mix = rows.astype(F32) + (outb1_r[...] + outb2_r[...]).reshape(1, width)
        mix += x_s[own, :].astype(F32)
        s = s_s[own, :].astype(F32)
        for w in (2 * chip_bit, 4):
            mix += hold[w].astype(F32)
            s += hold[w + 1].astype(F32)
        mixed_s[...] = mix.astype(BF16)
        unit, inverse = unit_rows(rows)
        gtok_s[...] = g_s[own, :].astype(F32) + inverse * (
            s - jnp.mean(s, -1, keepdims=True) - unit * jnp.mean(s * unit, -1, keepdims=True)
        )
        for copy in out_copies:
            copy.start()

    jobs = list(after)
    jobs.append((last_time + 1.7, functools.partial(token_grads, 3)))
    jobs.append((last_time + 3.7, functools.partial(token_grads, 2)))
    jobs.append((last_time + 5.7, functools.partial(token_grads, 1)))
    jobs.append((last_time + 6.8, lambda: pass_on(mate(2), 1)))
    jobs.append((last_time + 7.3, functools.partial(token_grads, 0)))
    jobs.append((last_time + 8.5, vectors))
    for q in range(len(swaps)):

        def trade(q=q):
            if q > 0:
                finish_swap(q - 1)
            swap(q).start()

        jobs.append((last_time + 9.5 + 3.2 * q, trade))
    jobs.append((last_time + 9.5 + 3.2 * len(swaps), lambda: finish_swap(len(swaps) - 1)))
    jobs.append((last_time + 31.0, tokens_out))
    for _, job in sorted(jobs, key=lambda pair: pair[0]):
        job()
    vec_o[...] = vec[...]
    for i in range(count):

        @pl.when(core_bit != i % 2)
        def _(i=i):
            for w in range(2):
                to_sib(i, w).wait_send()

    for copy in out_copies:
        copy.wait()
    for k in range(len(chunks)):
        chunk_out(k).wait()


def finish(res, mixed, gtok, vec, *refs):
    outs, (low, high, mid_m, mid_g, moved, in_sem, out_sem) = refs[:14], refs[14:]
    mixed_o, gtok_o, gain1_o, bias1_o, gain2_o, bias2_o, qkv_o, qkvb_o, wd_o, db_o, we_o, be_o, wc_o, cb_o = outs
    width = res.shape[1]
    heads = wd_o.shape[0] // HD
    count = low.shape[0] // SUB
    passing = [
        pltpu.make_async_copy(mixed, mid_m, moved.at[0]),
        pltpu.make_async_copy(gtok, mid_g, moved.at[1]),
    ]
    leaving = [
        pltpu.make_async_copy(mid_m, mixed_o, moved.at[2]),
        pltpu.make_async_copy(mid_g, gtok_o, moved.at[3]),
    ]

    def rows(k):
        return pl.ds(k * SUB, SUB)

    comes = [pltpu.make_async_copy(res.at[rows(k)], low.at[rows(k)], in_sem.at[k]) for k in range(count)]
    goes = []
    for k in range(6):
        where = (wc_o, we_o)[k // 3].at[rows(k % 3)]
        goes.append([pltpu.make_async_copy(high.at[rows(k)], where, out_sem.at[k])])
    for h in range(heads):
        first = (6 + h) * SUB
        places = [qkv_o.at[c, h * HD : (h + 1) * HD, :] for c in range(3)] + [wd_o.at[h * HD : (h + 1) * HD]]
        goes.append(
            [
                pltpu.make_async_copy(
                    high.at[pl.ds(first + c * HD, HD)], place, out_sem.at[6 + 4 * h + c]
                )
                for c, place in enumerate(places)
            ]
        )
    for copy in passing + comes:
        copy.start()
    for ref, row in (
        (gain1_o, 0),
        (bias1_o, 1),
        (gain2_o, 2),
        (bias2_o, 3),
        (db_o, 4),
        (cb_o, 4),
        (be_o, 5),
    ):
        ref[...] = vec[row, :]
    for h in range(heads):
        for c in range(3):
            lo = (3 * h + c) * HD
            qkvb_o[c : c + 1, h * HD : (h + 1) * HD] = vec[6:7, lo : lo + HD]
    for k in range(count):
        comes[k].wait()
        high[rows(k), :] = low[rows(k), :].astype(F32)
        for copy in goes[k]:
            copy.start()
        if k == 0:
            for come, go in zip(passing, leaving):
                come.wait()
                go.start()
    for copy in [x for some in goes for x in some] + leaving:
        copy.wait()


def shards(
    n,
    tokens,
    input_gain,
    input_bias,
    post_gain,
    post_bias,
    query_key_value,
    query_key_value_bias,
    dense_weight,
    dense_bias,
    expand_weight,
    expand_bias,
    contract_weight,
    contract_bias,
    lengths,
    cotangent,
):
    blk, width = tokens.shape
    local = query_key_value.shape[2]
    hidden = expand_weight.shape[1]
    heads = local // HD
    total = 4 * blk
    bits = n.bit_length() - 1
    swaps = bits + 2
    parts = len(pieces(n, heads))
    room = sum(chunk[4] for chunk in pieces(n, heads))
    cosine, sine = angle_rows(total)
    vmem = pl.BlockSpec(memory_space=pltpu.VMEM)
    smem = pl.BlockSpec(memory_space=pltpu.SMEM)
    hbm = pl.BlockSpec(memory_space=pl.ANY)
    dma = pltpu.SemaphoreType.DMA
    mixed, grad_tokens, res, vec = pl.pallas_call(
        functools.partial(core, n),
        name="core",
        out_shape=(
            jax.ShapeDtypeStruct((blk, width), BF16),
            jax.ShapeDtypeStruct((blk, width), F32),
            jax.ShapeDtypeStruct((3 * width, width), BF16),
            jax.ShapeDtypeStruct((8, width), F32),
        ),
        in_specs=[hbm, hbm, smem] + [vmem] * 7 + [hbm, vmem, hbm, hbm, hbm, vmem, vmem],
        out_specs=[hbm, hbm, hbm, vmem],
        scratch_shapes=[
            pltpu.VMEM((total, width), BF16),
            pltpu.VMEM((total, width), BF16),
            pltpu.VMEM((total, width), BF16),
            pltpu.VMEM((total, width), BF16),
            pltpu.VMEM((3 * local, width), BF16),
            pltpu.VMEM((local, width), BF16),
            pltpu.VMEM((width, hidden), BF16),
            pltpu.VMEM((hidden, width), BF16),
            pltpu.VMEM((3 * local, 1), F32),
            pltpu.VMEM((3 * width, width), F32),
            pltpu.VMEM((3 * width, width), BF16),
            pltpu.VMEM((6, blk, width), BF16),
            pltpu.VMEM((heads, 2 * HD, total), BF16),
            pltpu.VMEM((heads, HD, total), BF16),
            pltpu.VMEM((heads, total, 2 * HD), BF16),
            pltpu.VMEM((heads, HD + 16, total), BF16),
            pltpu.VMEM((heads, total, HD), BF16),
            pltpu.VMEM((heads, HD, total), BF16),
            pltpu.VMEM((8, total), F32),
            pltpu.VMEM((HD, total), F32),
            pltpu.VMEM((HD, total), F32),
            pltpu.VMEM((heads, HD, total), BF16),
            pltpu.VMEM((blk, width), BF16),
            pltpu.VMEM((blk, width), F32),
            pltpu.VMEM((8, width), F32),
            pltpu.VMEM((swaps, 8, width), F32),
            pltpu.VMEM((room, width), BF16),
            pltpu.VMEM((room, width), BF16),
            dma((5 + 3 * heads,)),
            dma((6,)),
            dma((6,)),
            dma((3, 2)),
            dma((3, 2)),
            dma((2 * bits, parts)),
            dma((2 * bits, parts)),
            dma((swaps,)),
            dma((swaps,)),
            dma((2 + parts,)),
            pltpu.SemaphoreType.REGULAR((2,)),
        ],
        compiler_params=pltpu.CompilerParams(
            vmem_limit_bytes=63 * 2**20, collective_id=0, has_side_effects=True
        ),
    )(
        tokens,
        cotangent,
        lengths,
        input_gain,
        input_bias,
        post_gain,
        post_bias,
        expand_bias,
        dense_bias,
        contract_bias,
        jnp.transpose(query_key_value, (0, 2, 1)),
        query_key_value_bias,
        dense_weight,
        expand_weight,
        contract_weight,
        cosine,
        sine,
    )

    vector = jax.ShapeDtypeStruct((width,), F32)
    outs = pl.pallas_call(
        finish,
        name="finish",
        in_specs=[hbm, hbm, hbm, vmem],
        out_specs=[hbm, hbm] + [vmem] * 4 + [hbm, vmem, hbm, vmem, hbm, vmem, hbm, vmem],
        scratch_shapes=[
            pltpu.VMEM((3 * width, width), BF16),
            pltpu.VMEM((3 * width, width), F32),
            pltpu.VMEM((blk, width), BF16),
            pltpu.VMEM((blk, width), F32),
            dma((4,)),
            dma((9,)),
            dma((6 + 4 * heads,)),
        ],
        out_shape=(
            jax.ShapeDtypeStruct((blk, width), BF16),
            jax.ShapeDtypeStruct((blk, width), F32),
            vector,
            vector,
            vector,
            vector,
            jax.ShapeDtypeStruct((3, local, width), F32),
            jax.ShapeDtypeStruct((3, local), F32),
            jax.ShapeDtypeStruct((local, width), F32),
            vector,
            jax.ShapeDtypeStruct((width, hidden), F32),
            jax.ShapeDtypeStruct((hidden,), F32),
            jax.ShapeDtypeStruct((hidden, width), F32),
            vector,
        ),
        compiler_params=pltpu.CompilerParams(vmem_limit_bytes=63 * 2**20),
    )(res, mixed, grad_tokens, vec)
    outs = list(outs)
    outs[6] = jnp.transpose(outs[6], (0, 2, 1))
    return tuple(outs)


def solution(mesh):
    rows = P(("dp", "tensor"), None)
    weights = (
        P(None, None, "tensor"),
        P(None, "tensor"),
        P("tensor", None),
        P(),
        P(None, "tensor"),
        P("tensor"),
        P("tensor", None),
        P(),
    )
    return jax.shard_map(
        functools.partial(shards, mesh.shape["dp"]),
        mesh=mesh,
        in_specs=(rows, P(), P(), P(), P()) + weights + (P("dp"), rows),
        out_specs=(rows, rows, P(), P(), P(), P()) + weights,
        check_vma=False,
    )
```
